32 devices in a mesh: grp: 4 (over y, x), rep: 8 (over z, core).
Axes of the slice: x: 2, y: 2, z: 4, core: 2. Of those that a mesh axis runs over, the one named last changes fastest.
Arguments:
- block_input: bfloat16 [32, 1024, 512], P(('grp', 'rep')), may hold values from -11 to 11
- cotangent: bfloat16 [32, 1024, 512], P(('grp', 'rep')), may hold values from -6 to 6
- encoder_states: bfloat16 [32, 512, 512], P(('grp', 'rep')), may hold values from -6 to 6
- segment_ids: int32 [32, 1024], P(('grp', 'rep')), may hold values from 0 to 5, as said below
- bucket_table: int32 [1024], replicated, may hold values from 0 to 31, as said below
- w_attn: float32 [6, 512, 384], P(None, 'grp'), may hold values from -0.125 to 0.125
- w_attn_out: float32 [2, 384, 512], P(None, None, 'grp'), may hold values from -1.75 to 1.75
- w_ff_in: float32 [2, 512, 1024], P(None, 'grp'), may hold values from -0.25 to 0.25
- w_ff_out: float32 [1024, 512], P(None, 'grp'), may hold values from -0.1875 to 0.1875
- norm_gains: float32 [3, 512], P(None, 'grp'), may hold values from 0.5 to 1.5
- rel_bias: float32 [32, 6], P('grp'), may hold values from -3 to 3
- mom_attn: float32 [6, 512, 384], P(None, 'grp'), may hold values from -128 to 128
- mom_attn_out: float32 [2, 384, 512], P(None, None, 'grp'), may hold values from -6 to 6
- mom_ff_in: float32 [2, 512, 1024], P(None, 'grp'), may hold values from -28 to 28
- mom_ff_out: float32 [1024, 512], P(None, 'grp'), may hold values from -28 to 28
- mom_gains: float32 [3, 512], P(None, 'grp'), may hold values from -256 to 256
- mom_bias: float32 [32, 6], P('grp'), may hold values from -256 to 256
- err_attn: float32 [8, 6, 512, 384], P('rep', None, 'grp'), may hold values from -1024 to 1024
- err_attn_out: float32 [8, 2, 384, 512], P('rep', None, None, 'grp'), may hold values from -48 to 48
- err_ff_in: float32 [8, 2, 512, 1024], P('rep', None, 'grp'), may hold values from -224 to 224
- err_ff_out: float32 [8, 1024, 512], P('rep', None, 'grp'), may hold values from -224 to 224
- q_start: float32 [11, 512, 8], P(None, 'grp'), may hold values from -6 to 6
Outputs:
- block_output: bfloat16 [32, 1024, 512], P(('grp', 'rep'))
- input_grad: float32 [32, 1024, 512], P(('grp', 'rep'))
- encoder_grad: float32 [32, 512, 512], P(('grp', 'rep'))
- branch_rms: float32 [4], replicated
- grad_attn: float32 [8, 6, 512, 384], P('rep', None, 'grp')
- grad_attn_out: float32 [8, 2, 384, 512], P('rep', None, None, 'grp')
- grad_ff_in: float32 [8, 2, 512, 1024], P('rep', None, 'grp')
- grad_ff_out: float32 [8, 1024, 512], P('rep', None, 'grp')
- grad_gains: float32 [8, 3, 512], P('rep', None, 'grp')
- grad_bias: float32 [8, 32, 6], P('rep', 'grp')
- new_err_attn: float32 [8, 6, 512, 384], P('rep', None, 'grp')
- new_err_attn_out: float32 [8, 2, 384, 512], P('rep', None, None, 'grp')
- new_err_ff_in: float32 [8, 2, 512, 1024], P('rep', None, 'grp')
- new_err_ff_out: float32 [8, 1024, 512], P('rep', None, 'grp')
- new_mom_attn: float32 [6, 512, 384], P(None, 'grp')
- new_mom_attn_out: float32 [2, 384, 512], P(None, None, 'grp')
- new_mom_ff_in: float32 [2, 512, 1024], P(None, 'grp')
- new_mom_ff_out: float32 [1024, 512], P(None, 'grp')
- new_mom_gains: float32 [3, 512], P(None, 'grp')
- new_mom_bias: float32 [32, 6], P('grp')
- update_attn: float32 [6, 512, 384], P(None, 'grp')
- update_attn_out: float32 [2, 384, 512], P(None, None, 'grp')
- update_ff_in: float32 [2, 512, 1024], P(None, 'grp')
- update_ff_out: float32 [1024, 512], P(None, 'grp')
- update_gains: float32 [3, 512], P(None, 'grp')
- update_bias: float32 [32, 6], P('grp')
- new_factors: float32 [11, 512, 8], P(None, 'grp')
The draws below stay inside these ranges and needn't reach their ends.
Inputs may be any that keep to these rules, and one draw needn't show every extreme that they name: `segment_ids`: in each sequence the tokens before a tail of 1 to 768 positions carry document numbers that start at 1, never fall and end at the sequence's count of documents, which is 5 in every sequence; the tail carries 0. bucket_table[d] belongs to distance d: it equals d for d up to 16, never falls, and is 31 at the last distance.
All inputs are finite; a program needn't handle non-finite values.
Results may differ from the reference program's by a relative error of at most 0.025.
The reference program's roundings to bfloat16 on the way count: a program that leaves them out, or rounds other values in their place, can miss the bound.
Values may be sent and summed in bfloat16 or wider, within the bound.
No kernel may reach another device: no remote copies, remote signals or barrier semaphores. Data moves between devices by JAX's collectives and lax.ppermute only.
A program may use at most 320 MiB of HBM per device.

```python
import jax
import jax.numpy as jnp
from jax import lax

D = 512
H = 6
DK = 64
FF = 1024
NB = 32
RANK = 8
LEN = 1024
ENC = 512
SEQS_DEV = 1
SEQS = 32
N_GRP = 4
N_REP = 8


def draw_block_input(key, part):
    ramp = 0.6 + 1.2 * jnp.arange(SEQS, dtype=jnp.float32) / max(SEQS - 1, 1)
    values = jnp.clip(jax.random.normal(key, (SEQS, LEN, D), jnp.float32), -6.0, 6.0)
    return (values * ramp[:, None, None]).astype(jnp.bfloat16)


def draw_segment_ids(key, part):
    start_key, tail_key = jax.random.split(jax.random.fold_in(key, 11))
    documents = max(2, LEN // 192)
    sequence = jnp.arange(SEQS, dtype=jnp.int32)
    ramp = 1 + (3 * LEN // 4 - 1) * sequence // max(SEQS - 1, 1)
    jitter = jax.random.randint(tail_key, (SEQS,), 0, max(LEN // 16, 1))
    tail = jnp.maximum(ramp - jitter, 1)
    region = (LEN - tail) // documents
    offsets = jax.random.randint(start_key, (SEQS, documents), 0, region[:, None])
    offsets = offsets.at[:, 0].set(0)
    starts = jnp.arange(documents, dtype=jnp.int32)[None, :] * region[:, None] + offsets
    positions = jnp.arange(LEN, dtype=jnp.int32)
    number = jnp.sum((positions[None, :, None] >= starts[:, None, :]).astype(jnp.int32), axis=-1)
    return jnp.where(positions[None, :] < LEN - tail[:, None], number, 0).astype(jnp.int32)


def draw_bucket_table(key, part):
    exact = NB // 2
    distance = jnp.arange(LEN, dtype=jnp.int32)
    steps = (jax.random.randint(jax.random.fold_in(key, 23), (LEN,), 0, LEN) < 2 * NB).astype(jnp.int32)
    steps = jnp.where(distance <= exact, jnp.minimum(distance, 1), steps)
    level = jnp.minimum(jnp.cumsum(steps), NB - 1)
    return jnp.where(distance == LEN - 1, NB - 1, level).astype(jnp.int32)


def levels(stream_key, shape, cuts, smallest, high):
    level = 1.0
    for axis_at, blocks in cuts:
        heights = jax.random.uniform(jax.random.fold_in(jax.random.fold_in(stream_key, 6), axis_at), (blocks,), jnp.float32, smallest / len(cuts), high / len(cuts))
        level = level * jnp.repeat(jnp.exp(heights), shape[axis_at] // blocks).reshape((-1,) + (1,) * (len(shape) - 1 - axis_at))
    return level


def noise(key, shape, spread, reach, pieces=(), kind=jnp.bfloat16):
    level = levels(key, shape, pieces, -0.22, 0.18) if pieces else 1.0
    result = jax.random.normal(key, shape, jnp.float32) * spread * level
    return jnp.minimum(jnp.maximum(result, -reach), reach).astype(kind)


def setup_inputs(seed: int = 0) -> dict:
    key_list = jax.random.split(jax.random.key(seed), 23)
    block_input = draw_block_input(jax.random.fold_in(key_list[22], 71), 0)
    cotangent = noise(key_list[1], (SEQS, LEN, D), 1.0, 6.0, ((0, 32),))
    encoder_states = noise(key_list[2], (SEQS, ENC, D), 1.0, 6.0, ((0, 32),))
    segment_ids = draw_segment_ids(jax.random.fold_in(key_list[22], 71), 0)
    bucket_table = draw_bucket_table(jax.random.fold_in(key_list[22], 71), 0)
    w_attn = noise(key_list[5], (6, D, H * DK), (4 * D) ** -0.5, 0.125, ((1, 4),), jnp.float32)
    w_attn_out = noise(key_list[6], (2, H * DK, D), (max(1, H * DK // 32)) ** -0.5, 1.75, ((2, 4),), jnp.float32)
    w_ff_in = noise(key_list[7], (2, D, FF), D ** -0.5, 0.25, ((1, 4),), jnp.float32)
    w_ff_out = noise(key_list[8], (FF, D), FF ** -0.5, 0.1875, ((1, 4),), jnp.float32)
    norm_gains = jnp.clip(1.0 + 0.1 * jax.random.normal(key_list[9], (3, D), jnp.float32), 0.5, 1.5)
    rel_bias = noise(key_list[10], (NB, H), 1.0, 3.0, ((0, 4),), jnp.float32)
    mom_attn = noise(key_list[11], (6, D, H * DK), (4.2 * (RANK * N_GRP * N_GRP * SEQS_DEV * LEN) ** 0.5 * (D * N_REP) ** -0.5), 128.0, ((1, 4),), jnp.float32)
    mom_attn_out = noise(key_list[12], (2, H * DK, D), (0.17 * (RANK * N_GRP * N_GRP * SEQS_DEV * LEN) ** 0.5 * (D * N_REP) ** -0.5), 6.0, ((2, 4),), jnp.float32)
    mom_ff_in = noise(key_list[13], (2, D, FF), (0.85 * (RANK * N_GRP * N_GRP * SEQS_DEV * LEN) ** 0.5 * (D * N_REP) ** -0.5), 28.0, ((1, 4),), jnp.float32)
    mom_ff_out = noise(key_list[14], (FF, D), (0.85 * (RANK * N_GRP * N_GRP * SEQS_DEV * LEN) ** 0.5 * (D * N_REP) ** -0.5), 28.0, ((1, 4),), jnp.float32)
    mom_gains = noise(key_list[15], (3, D), (2.0 * (N_GRP * SEQS_DEV * LEN) ** 0.5 * N_REP ** -0.5), 256.0, ((1, 4),), jnp.float32)
    mom_bias = noise(key_list[16], (NB, H), (2.0 * (N_GRP * SEQS_DEV * LEN) ** 0.5 * N_REP ** -0.5), 256.0, ((0, 4),), jnp.float32)
    err_attn = noise(key_list[17], (N_REP, 6, D, H * DK), (3.0 * (N_GRP * SEQS_DEV * LEN) ** 0.5), 1024.0, ((0, 8), (2, 4)), jnp.float32)
    err_attn_out = noise(key_list[18], (N_REP, 2, H * DK, D), (0.12 * (N_GRP * SEQS_DEV * LEN) ** 0.5), 48.0, ((0, 8), (3, 4)), jnp.float32)
    err_ff_in = noise(key_list[19], (N_REP, 2, D, FF), (0.6 * (N_GRP * SEQS_DEV * LEN) ** 0.5), 224.0, ((0, 8), (2, 4)), jnp.float32)
    err_ff_out = noise(key_list[20], (N_REP, FF, D), (0.6 * (N_GRP * SEQS_DEV * LEN) ** 0.5), 224.0, ((0, 8), (2, 4)), jnp.float32)
    q_start = noise(key_list[21], (11, D, RANK), 1.0, 6.0, ((1, 4),), jnp.float32)
    return dict(block_input=block_input, cotangent=cotangent, encoder_states=encoder_states, segment_ids=segment_ids, bucket_table=bucket_table, w_attn=w_attn, w_attn_out=w_attn_out, w_ff_in=w_ff_in, w_ff_out=w_ff_out, norm_gains=norm_gains, rel_bias=rel_bias, mom_attn=mom_attn, mom_attn_out=mom_attn_out, mom_ff_in=mom_ff_in, mom_ff_out=mom_ff_out, mom_gains=mom_gains, mom_bias=mom_bias, err_attn=err_attn, err_attn_out=err_attn_out, err_ff_in=err_ff_in, err_ff_out=err_ff_out, q_start=q_start)


@jax.custom_vjp
def low(v):
    return lax.optimization_barrier(v.astype(jnp.bfloat16)).astype(jnp.float32)

@jax.custom_vjp
def low_back(v):
    return v

def low_keep(v):
    return (low(v), None)

def low_pass(kept, grad):
    return (grad,)

def back_keep(v):
    return (v, None)

def back_low(kept, grad):
    return (low(grad),)
low.defvjp(low_keep, low_pass)
low_back.defvjp(back_keep, back_low)
epsilon = 1e-06
decay = 0.5
rates = (0.002, 0.5, 0.015, 0.015, 0.005, 0.05)
masked_score = -1e+30
highest = lax.Precision.HIGHEST

def both(value):
    return low_back(low(value))

def matmul(left, right):
    return jnp.dot(left, right, precision=highest)

def norm_forward(values, gain):
    scale = lax.rsqrt(lax.optimization_barrier(jnp.mean(values * values, axis=-1, keepdims=True)) + epsilon)
    return values * scale * gain

def attend(query, keys, values, bias, allowed):
    rows = query.shape[0]
    count = keys.shape[0]
    heads_q = query.reshape(rows, H, DK)
    heads_k = keys.reshape(count, H, DK)
    heads_v = values.reshape(count, H, DK)
    scores = low_back(jnp.einsum('ihd,jhd->hij', heads_q, heads_k, precision=highest) + bias)
    if allowed is not None:
        scores = jnp.where(allowed[None], scores, masked_score)
    probs = low(jax.nn.softmax(scores, axis=-1))
    mixed = jnp.einsum('hij,jhd->ihd', probs, heads_v, precision=highest)
    return both(mixed.reshape(rows, H * DK))

def layer(weights, stream, states, segment, bucket_table):
    w_attn, w_proj, w_ffin, w_ffout, gains, rel_bias = weights
    attn_low = low(w_attn)
    proj_low = low(w_proj)
    ffin_low = low(w_ffin)
    ffout_low = low(w_ffout)
    gains_low = low(gains)
    table_low = low(rel_bias)
    positions = jnp.arange(stream.shape[0], dtype=jnp.int32)
    gap = positions[:, None] - positions[None, :]
    allowed = (gap >= 0) & (segment[:, None] == segment[None, :])
    bias = jnp.transpose(table_low[bucket_table[jnp.maximum(gap, 0)]], (2, 0, 1))
    normed0 = low(norm_forward(stream, gains_low[0]))
    query = both(matmul(normed0, attn_low[0]))
    keys = both(matmul(normed0, attn_low[1]))
    values = both(matmul(normed0, attn_low[2]))
    branch_self = low_back(matmul(attend(query, keys, values, bias, allowed), proj_low[0]))
    hidden1 = stream + branch_self
    normed1 = low(norm_forward(hidden1, gains_low[1]))
    cross_query = both(matmul(normed1, attn_low[3]))
    cross_keys = both(matmul(states, attn_low[4]))
    cross_values = both(matmul(states, attn_low[5]))
    branch_cross = low_back(matmul(attend(cross_query, cross_keys, cross_values, 0.0, None), proj_low[1]))
    hidden2 = hidden1 + branch_cross
    normed2 = low(norm_forward(hidden2, gains_low[2]))
    gate = low_back(matmul(normed2, ffin_low[0]))
    upward = low_back(matmul(normed2, ffin_low[1]))
    hidden_ff = low(jax.nn.gelu(gate, approximate=True) * upward)
    branch_ff = low_back(matmul(hidden_ff, ffout_low))
    return (hidden2 + branch_ff, (branch_self, branch_cross, branch_ff))

def orthonormal(left):
    columns = []
    for column in range(left.shape[-1]):
        current = left[..., column]
        for earlier in columns:
            current = current - lax.optimization_barrier(jnp.sum(current * earlier, axis=-1, keepdims=True)) * earlier
        current = current * lax.rsqrt(lax.optimization_barrier(jnp.sum(current * current, axis=-1, keepdims=True)) + epsilon)
        columns.append(current)
    return jnp.stack(columns, axis=-1)

def compress(matrices, factor):
    left = jnp.einsum('nkgsw,kgsr->kgwr', matrices, factor, precision=highest) / N_REP
    left = orthonormal(left)
    right = jnp.einsum('nkgsw,kgwr->kgsr', matrices, left, precision=highest) / N_REP
    approx = jnp.einsum('kgsr,kgwr->kgsw', right, left, precision=highest)
    return (approx, right, matrices - approx[None])

def reference(block_input, cotangent, encoder_states, segment_ids, bucket_table, w_attn, w_attn_out, w_ff_in, w_ff_out, norm_gains, rel_bias, mom_attn, mom_attn_out, mom_ff_in, mom_ff_out, mom_gains, mom_bias, err_attn, err_attn_out, err_ff_in, err_ff_out, q_start):
    params = (w_attn, w_attn_out, w_ff_in, w_ff_out, norm_gains, rel_bias)
    sums_init = tuple((jnp.zeros((N_REP,) + weight.shape, jnp.float32) for weight in params))
    bundle = 2 if SEQS % 2 == 0 else 1

    def one_sequence(resid, grad_in, encoder, segment):
        valid = (segment > 0).astype(jnp.float32)
        stream = resid.astype(jnp.float32)

        def forward(weights, stream_in, states):
            return layer(weights, stream_in, states, segment, bucket_table)
        output, pull, branches = jax.vjp(forward, params, stream, encoder.astype(jnp.float32), has_aux=True)
        grads, grad_stream, grad_states = pull(grad_in.astype(jnp.float32) * valid[:, None])
        terms = jnp.stack([jnp.sum(valid * lax.optimization_barrier(jnp.sum(part * part, axis=-1))) for part in (stream,) + branches])
        return (grads, output.astype(jnp.bfloat16), grad_stream, grad_states, terms, jnp.sum(valid))

    def one_bundle(carry, item):
        sums, squares, count = carry
        resid, grad_in, encoder, segment, index = item
        grads, output, grad_stream, grad_states, terms, counted = jax.vmap(one_sequence)(resid, grad_in, encoder, segment)
        replica = index // SEQS_DEV % N_REP
        sums = tuple((total.at[replica].add(part) for total, part in zip(sums, grads)))
        return ((sums, squares + lax.optimization_barrier(jnp.sum(terms, axis=0)), count + jnp.sum(counted)), (output, grad_stream, grad_states))
    steps_count = SEQS // bundle
    carry_init = (sums_init, jnp.zeros((4,), jnp.float32), jnp.zeros((), jnp.float32))
    items = (block_input.reshape(steps_count, bundle, LEN, D), cotangent.reshape(steps_count, bundle, LEN, D), encoder_states.reshape(steps_count, bundle, ENC, D), segment_ids.reshape(steps_count, bundle, LEN), jnp.arange(SEQS, dtype=jnp.int32).reshape(steps_count, bundle))
    (sums, squares, count), (outputs, grads_in, grads_enc) = lax.scan(one_bundle, carry_init, items)
    block_output = outputs.reshape(SEQS, LEN, D)
    input_grad = grads_in.reshape(SEQS, LEN, D)
    encoder_grad = grads_enc.reshape(SEQS, ENC, D)
    branch_rms = jnp.sqrt(squares / (count * D))
    grad_attn, grad_proj, grad_ffin, grad_ffout, grad_gains, grad_bias = sums
    shard = D // N_GRP
    width = H * DK
    factors = q_start.reshape(11, N_GRP, shard, RANK)
    merged_attn = (grad_attn + err_attn).reshape(N_REP, 6, N_GRP, shard, width)
    merged_proj = jnp.transpose((grad_proj + err_attn_out).reshape(N_REP, 2, width, N_GRP, shard), (0, 1, 3, 4, 2))
    merged_ffin = (grad_ffin + err_ff_in).reshape(N_REP, 2, N_GRP, shard, FF)
    merged_ffout = jnp.transpose((grad_ffout + err_ff_out).reshape(N_REP, FF, N_GRP, shard), (0, 2, 3, 1))[:, None]
    approx_attn, right_attn, error_attn = compress(merged_attn, factors[0:6])
    approx_proj, right_proj, error_proj = compress(merged_proj, factors[6:8])
    approx_ffin, right_ffin, error_ffin = compress(merged_ffin, factors[8:10])
    approx_ffout, right_ffout, error_ffout = compress(merged_ffout, factors[10:11])
    new_err_attn = error_attn.reshape(N_REP, 6, D, width)
    new_err_proj = jnp.transpose(error_proj, (0, 1, 4, 2, 3)).reshape(N_REP, 2, width, D)
    new_err_ffin = error_ffin.reshape(N_REP, 2, D, FF)
    new_err_ffout = jnp.transpose(error_ffout[:, 0], (0, 3, 1, 2)).reshape(N_REP, FF, D)
    step_attn = approx_attn.reshape(6, D, width)
    step_proj = jnp.transpose(approx_proj, (0, 3, 1, 2)).reshape(2, width, D)
    step_ffin = approx_ffin.reshape(2, D, FF)
    step_ffout = jnp.transpose(approx_ffout[0], (2, 0, 1)).reshape(FF, D)
    step_gains = lax.optimization_barrier(jnp.sum(grad_gains, axis=0)) / N_REP
    step_bias = lax.optimization_barrier(jnp.sum(grad_bias, axis=0)) / N_REP
    olds = (mom_attn, mom_attn_out, mom_ff_in, mom_ff_out, mom_gains, mom_bias)
    steps = (step_attn, step_proj, step_ffin, step_ffout, step_gains, step_bias)
    moments = tuple((decay * old + fresh for old, fresh in zip(olds, steps)))
    updates = tuple((-rate * moment for rate, moment in zip(rates, moments)))
    new_factors = jnp.concatenate([right_attn, right_proj, right_ffin, right_ffout], axis=0).reshape(11, D, RANK)
    return (block_output, input_grad, encoder_grad, branch_rms, grad_attn, grad_proj, grad_ffin, grad_ffout, grad_gains, grad_bias, new_err_attn, new_err_proj, new_err_ffin, new_err_ffout, moments[0], moments[1], moments[2], moments[3], moments[4], moments[5], updates[0], updates[1], updates[2], updates[3], updates[4], updates[5], new_factors)
```

```python
import functools

import jax
import jax.numpy as jnp
from jax import lax
from jax.experimental import pallas as pl
from jax.experimental.pallas import tpu as pltpu
from jax.sharding import PartitionSpec as P

H = 6
DK = 64
PAIR = 2 * DK
ROWS = 256

epsilon = 1e-06
decay = 0.5
rates = (0.002, 0.5, 0.015, 0.015, 0.005, 0.05)
masked_score = -1e30
highest = lax.Precision.HIGHEST
NT = (((1,), (1,)), ((), ()))
NN = (((1,), (0,)), ((), ()))
TN = (((0,), (0,)), ((), ()))
f32 = jnp.float32
bf16 = jnp.bfloat16


def mm(left, right, dims=NN):
    return lax.dot_general(left, right, dims, preferred_element_type=f32)


def bias_kernel(length, bucket_ref, table_ref, out_ref):
    buckets = table_ref.shape[0]
    bucket = bucket_ref[...]
    match = lax.broadcasted_iota(jnp.int32, (buckets, length), 0) == bucket
    by_gap = mm(table_ref[...], match.astype(bf16), TN)
    tiles = length // ROWS
    wide = 2 * ROWS
    padded = jnp.concatenate(
        [jnp.full((H, ROWS), masked_score, f32), by_gap], axis=1
    )
    for head in range(H):
        for tile in range(tiles):
            first = length - ROWS * (tile + 1)
            line = padded[head : head + 1, first : first + wide]
            rows = jnp.concatenate(
                [line] + [pltpu.roll(line, step, 1) for step in range(1, 8)], axis=0
            )
            while rows.shape[0] < ROWS:
                rows = jnp.concatenate([rows, pltpu.roll(rows, rows.shape[0], 1)], axis=0)
            out_ref[head, ROWS * tile : ROWS * (tile + 1), :] = rows[:, ROWS:]


def bias_tiles(bucket_table, table_low):
    length = bucket_table.shape[0]
    return pl.pallas_call(
        functools.partial(bias_kernel, length),
        out_shape=jax.ShapeDtypeStruct((H, length, ROWS), f32),
        name="bias_tiles",
    )(bucket_table.reshape(1, length), table_low)


def lane_masks(rows):
    lane = lax.broadcasted_iota(jnp.int32, (rows, PAIR), 1)
    return (lane < DK, lane >= DK)


def turned(value):
    return value.astype(f32).T.astype(bf16)


def scores_of(q_ref, keys, bias_ref, qseg_ref, first, count, half, mask):
    query = q_ref[first : first + ROWS, :]
    query = jnp.where(mask, query, jnp.zeros_like(query))
    full = query
    if qseg_ref is not None:
        full = jnp.concatenate([query, qseg_ref[first : first + ROWS, :]], axis=1)
    scores = mm(keys[:count], full, NT)
    if bias_ref is not None:
        length = bias_ref.shape[1]
        scores = scores + bias_ref[half, length - count : length, :]
    return query, scores


def forward_kernel(causal, *refs):
    if causal:
        q_ref, k_ref, v_ref, bias_ref, kseg_ref, qseg_ref, out_ref, log_ref = refs
        keys = jnp.concatenate([k_ref[...], kseg_ref[...]], axis=1)
    else:
        q_ref, k_ref, v_ref, out_ref, log_ref = refs
        bias_ref = qseg_ref = None
        keys = k_ref[...]
    length = q_ref.shape[0]
    values = turned(v_ref[...])
    masks = lane_masks(ROWS)
    log_ref[...] = jnp.zeros_like(log_ref)
    for first in range(0, length, ROWS):
        count = first + ROWS if causal else keys.shape[0]
        mixed = []
        for half in range(2):
            unused, scores = scores_of(
                q_ref, keys, bias_ref, qseg_ref, first, count, half, masks[half]
            )
            top = jnp.max(scores, axis=0, keepdims=True)
            powers = jnp.exp(scores - top)
            total = jnp.sum(powers, axis=0, keepdims=True)
            probs = (powers * (1.0 / total)).astype(bf16)
            mixed.append(mm(values[DK * half : DK * (half + 1), :count], probs))
            log_ref[half : half + 1, first : first + ROWS] = top + jnp.log(total)
        out_ref[first : first + ROWS, :] = jnp.concatenate(mixed, axis=0).T.astype(bf16)


def squeezed(rows, index):
    return pl.BlockSpec((None, rows, PAIR), index)


def column(rows):
    return pl.BlockSpec((rows, PAIR), lambda p: (0, p))


def whole(shape):
    return pl.BlockSpec(shape, lambda p: (0,) * len(shape))


def log_spec(length):
    return pl.BlockSpec((None, 8, length), lambda p: (p, 0, 0))


def bias_spec(length):
    return pl.BlockSpec((2, length, ROWS), lambda p: (p, 0, 0))


def self_forward(heads, bias, kseg, qseg):
    length = heads.shape[1]
    pairs = H // 2
    return pl.pallas_call(
        functools.partial(forward_kernel, True),
        grid=(pairs,),
        in_specs=[
            squeezed(length, lambda p: (0, 0, p)),
            squeezed(length, lambda p: (1, 0, p)),
            squeezed(length, lambda p: (2, 0, p)),
            bias_spec(length),
            whole((length, PAIR)),
            whole((length, PAIR)),
        ],
        out_specs=[column(length), log_spec(length)],
        out_shape=[
            jax.ShapeDtypeStruct((length, H * DK), bf16),
            jax.ShapeDtypeStruct((pairs, 8, length), f32),
        ],
        name="self_forward",
    )(heads, heads, heads, bias, kseg, qseg)


def cross_forward(query, pairs_kv):
    length = query.shape[0]
    states = pairs_kv.shape[1]
    pairs = H // 2
    return pl.pallas_call(
        functools.partial(forward_kernel, False),
        grid=(pairs,),
        in_specs=[
            column(length),
            squeezed(states, lambda p: (0, 0, p)),
            squeezed(states, lambda p: (1, 0, p)),
        ],
        out_specs=[column(length), log_spec(length)],
        out_shape=[
            jax.ShapeDtypeStruct((length, H * DK), bf16),
            jax.ShapeDtypeStruct((pairs, 8, length), f32),
        ],
        name="cross_forward",
    )(query, pairs_kv, pairs_kv)


def backward_kernel(causal, *refs):
    if causal:
        (q_ref, k_ref, v_ref, grad_ref, log_ref, bias_ref, kseg_ref, qseg_ref, bucket_ref,
         out_ref, table_ref, key_sum, value_sum, tile_sum) = refs
        keys = jnp.concatenate([k_ref[...], kseg_ref[...]], axis=1)
        tile_sum[...] = jnp.zeros_like(tile_sum)
    else:
        q_ref, k_ref, v_ref, grad_ref, log_ref, dq_ref, pair_ref, key_sum, value_sum = refs
        bias_ref = qseg_ref = None
        keys = k_ref[...]
    length = q_ref.shape[0]
    states = keys.shape[0]
    turned_keys = turned(k_ref[...])
    masks = lane_masks(ROWS)
    key_sum[...] = jnp.zeros_like(key_sum)
    value_sum[...] = jnp.zeros_like(value_sum)
    for first in range(0, length, ROWS):
        count = first + ROWS if causal else states
        query_grads = []
        for half in range(2):
            query, scores = scores_of(
                q_ref, keys, bias_ref, qseg_ref, first, count, half, masks[half]
            )
            probs = jnp.exp(scores - log_ref[half : half + 1, first : first + ROWS])
            grad = grad_ref[first : first + ROWS, :]
            grad = jnp.where(masks[half], grad, jnp.zeros_like(grad))
            grad_probs = mm(v_ref[:count, :], grad, NT)
            dots = jnp.sum(grad_probs * probs, axis=0, keepdims=True)
            grad_scores = (probs * (grad_probs - dots)).astype(bf16)
            value_sum[:count, :] += mm(probs.astype(bf16), grad)
            key_sum[:count, :] += mm(grad_scores, query)
            query_grads.append(mm(turned_keys[DK * half : DK * (half + 1), :count], grad_scores))
            if causal:
                tile_sum[half, length - count : length, :] += grad_scores.astype(f32)
        joined = jnp.concatenate(query_grads, axis=0).T.astype(bf16)
        if causal:
            out_ref[0, first : first + ROWS, :] = joined
        else:
            dq_ref[first : first + ROWS, :] = joined
    if causal:
        out_ref[1] = key_sum[...].astype(bf16)
        out_ref[2] = value_sum[...].astype(bf16)
        by_gap = jnp.concatenate(
            [diagonal_sums(tile_sum, half) for half in range(2)]
            + [jnp.zeros((6, length), f32)],
            axis=0,
        )
        buckets = table_ref.shape[1]
        match = lax.broadcasted_iota(jnp.int32, (buckets, length), 0) == bucket_ref[...]
        table_ref[...] = lax.dot_general(
            by_gap, match.astype(f32), NT,
            precision=lax.Precision.HIGHEST, preferred_element_type=f32,
        )
    else:
        pair_ref[0] = key_sum[...].astype(bf16)
        pair_ref[1] = value_sum[...].astype(bf16)


def diagonal_sums(tile_sum, half):
    length = tile_sum.shape[1]
    wide = 2 * ROWS
    pieces = []
    carried = None
    for tile in range(length // ROWS):
        rows = tile_sum[half, ROWS * tile : ROWS * (tile + 1), :]
        rows = jnp.concatenate([rows, jnp.zeros_like(rows)], axis=1)
        while rows.shape[0] > 1:
            middle = rows.shape[0] // 2
            rows = rows[:middle] + pltpu.roll(rows[middle:], wide - middle, 1)
        low = rows[:, :ROWS]
        if carried is not None:
            low = low + carried
        carried = rows[:, ROWS:]
        pieces.append(low)
    return jnp.concatenate(pieces[::-1], axis=1)


def self_backward(heads, grad, logs, bias, kseg, qseg, bucket_table, buckets):
    length = heads.shape[1]
    pairs = H // 2
    return pl.pallas_call(
        functools.partial(backward_kernel, True),
        grid=(pairs,),
        in_specs=[
            squeezed(length, lambda p: (0, 0, p)),
            squeezed(length, lambda p: (1, 0, p)),
            squeezed(length, lambda p: (2, 0, p)),
            column(length),
            log_spec(length),
            bias_spec(length),
            whole((length, PAIR)),
            whole((length, PAIR)),
            whole((1, length)),
        ],
        out_specs=[
            pl.BlockSpec((3, length, PAIR), lambda p: (0, 0, p)),
            pl.BlockSpec((None, 8, buckets), lambda p: (p, 0, 0)),
        ],
        out_shape=[
            jax.ShapeDtypeStruct((3, length, H * DK), bf16),
            jax.ShapeDtypeStruct((pairs, 8, buckets), f32),
        ],
        scratch_shapes=[
            pltpu.VMEM((length, PAIR), f32),
            pltpu.VMEM((length, PAIR), f32),
            pltpu.VMEM((2, length, ROWS), f32),
        ],
        name="self_backward",
    )(heads, heads, heads, grad, logs, bias, kseg, qseg, bucket_table.reshape(1, length))


def cross_backward(query, pairs_kv, grad, logs):
    length = query.shape[0]
    states = pairs_kv.shape[1]
    pairs = H // 2
    return pl.pallas_call(
        functools.partial(backward_kernel, False),
        grid=(pairs,),
        in_specs=[
            column(length),
            squeezed(states, lambda p: (0, 0, p)),
            squeezed(states, lambda p: (1, 0, p)),
            column(length),
            log_spec(length),
        ],
        out_specs=[column(length), pl.BlockSpec((2, states, PAIR), lambda p: (0, 0, p))],
        out_shape=[
            jax.ShapeDtypeStruct((length, H * DK), bf16),
            jax.ShapeDtypeStruct((2, states, H * DK), bf16),
        ],
        scratch_shapes=[pltpu.VMEM((states, PAIR), f32), pltpu.VMEM((states, PAIR), f32)],
        name="cross_backward",
    )(query, pairs_kv, pairs_kv, grad, logs)


def norm_forward(values, gain):
    scale = lax.rsqrt(jnp.mean(values * values, axis=-1, keepdims=True) + epsilon)
    return (values * scale * gain, scale)


def norm_backward(values, scale, gain, grad_normed):
    weighted = grad_normed * gain
    grad_values = scale * weighted - values * scale**3 * jnp.mean(
        weighted * values, axis=-1, keepdims=True
    )
    return (grad_values, jnp.sum(grad_normed * values * scale, axis=0))


def gated_unit(gate, upward):
    return jax.nn.gelu(gate, approximate=True) * upward


def orth_kernel(replicas, count, *refs):
    for at in range(count):
        for matrix in range(refs[at].shape[0]):
            current = refs[at][matrix] * (1.0 / replicas)
            row = lax.broadcasted_iota(jnp.int32, (current.shape[0], 1), 0)
            for column in range(current.shape[0]):
                line = current[column : column + 1]
                line = line * lax.rsqrt(jnp.sum(line * line, axis=1, keepdims=True) + epsilon)
                dots = jnp.sum(current * line, axis=1, keepdims=True)
                later = current - dots * line
                current = jnp.where(row > column, later, jnp.where(row == column, line, current))
            refs[count + at][matrix] = current


def orthonormal(totals, replicas):
    return pl.pallas_call(
        functools.partial(orth_kernel, replicas, len(totals)),
        out_shape=[jax.ShapeDtypeStruct(total.shape, total.dtype) for total in totals],
        name="orthonormal",
    )(*totals)


def body(
    block_input,
    cotangent,
    encoder_states,
    segment_ids,
    bucket_table,
    w_attn,
    w_attn_out,
    w_ff_in,
    w_ff_out,
    norm_gains,
    rel_bias,
    mom_attn,
    mom_attn_out,
    mom_ff_in,
    mom_ff_out,
    mom_gains,
    mom_bias,
    err_attn,
    err_attn_out,
    err_ff_in,
    err_ff_out,
    q_start,
):
    sequences, length, width = block_input.shape
    states_len = encoder_states.shape[1]
    tokens = sequences * length
    gathered = (
        lax.all_gather(w_attn.astype(jnp.bfloat16), "grp", axis=1, tiled=True),
        lax.all_gather(w_attn_out.astype(jnp.bfloat16), "grp", axis=2, tiled=True),
        lax.all_gather(w_ff_in.astype(jnp.bfloat16), "grp", axis=1, tiled=True),
        lax.all_gather(w_ff_out.astype(jnp.bfloat16), "grp", axis=1, tiled=True),
        lax.all_gather(norm_gains.astype(jnp.bfloat16), "grp", axis=1, tiled=True),
        lax.all_gather(rel_bias.astype(jnp.bfloat16), "grp", axis=0, tiled=True),
    )
    attn_full, proj_full, ffin_full, ffout_full, gains_low, table_low = gathered
    gains = gains_low.astype(jnp.float32)
    buckets = table_low.shape[0]
    bias = bias_tiles(bucket_table, table_low)
    one_hot = segment_ids[0][:, None] == jnp.arange(PAIR)[None, :]
    kseg = one_hot.astype(jnp.bfloat16)
    known = jnp.arange(PAIR)[None, :] < 8
    qseg = jnp.where(known & ~one_hot, masked_score, 0.0).astype(jnp.bfloat16)
    stream = block_input.reshape(tokens, width).astype(jnp.float32)
    normed0, scale0 = norm_forward(stream, gains[0])
    normed0_low = normed0.astype(jnp.bfloat16)
    self_heads = jnp.einsum(
        "td,kde->kte", normed0_low, attn_full[0:3], preferred_element_type=jnp.float32
    ).astype(jnp.bfloat16)
    attended, self_logs = self_forward(self_heads, bias, kseg, qseg)
    branch_self = jnp.dot(attended, proj_full[0], preferred_element_type=jnp.float32)
    hidden1 = stream + branch_self
    normed1, scale1 = norm_forward(hidden1, gains[1])
    normed1_low = normed1.astype(jnp.bfloat16)
    cross_query = jnp.dot(normed1_low, attn_full[3], preferred_element_type=jnp.float32).astype(
        jnp.bfloat16
    )
    states_flat = encoder_states.reshape(sequences * states_len, width)
    cross_pairs = jnp.einsum(
        "td,kde->kte", states_flat, attn_full[4:6], preferred_element_type=jnp.float32
    ).astype(jnp.bfloat16)
    cross_attended, cross_logs = cross_forward(cross_query, cross_pairs)
    branch_cross = jnp.dot(cross_attended, proj_full[1], preferred_element_type=jnp.float32)
    hidden2 = hidden1 + branch_cross
    normed2, scale2 = norm_forward(hidden2, gains[2])
    normed2_low = normed2.astype(jnp.bfloat16)
    gate_up = jnp.einsum("td,kdf->ktf", normed2_low, ffin_full, preferred_element_type=jnp.float32)
    activated, pull_gate = jax.vjp(gated_unit, gate_up[0], gate_up[1])
    hidden_ff = activated.astype(jnp.bfloat16)
    branch_ff = jnp.dot(hidden_ff, ffout_full, preferred_element_type=jnp.float32)
    output = hidden2 + branch_ff
    block_output = output.astype(jnp.bfloat16).reshape(sequences, length, width)
    valid = (segment_ids.reshape(tokens) > 0).astype(jnp.float32)
    squares = jnp.stack(
        [
            jnp.sum(valid * jnp.sum(part * part, axis=-1))
            for part in (stream, branch_self, branch_cross, branch_ff)
        ]
    )
    square_sums, valid_count = lax.psum((squares, jnp.sum(valid)), ("grp", "rep"))
    branch_rms = jnp.sqrt(square_sums / (valid_count * width))
    grad_out = cotangent.reshape(tokens, width).astype(jnp.float32) * valid[:, None]
    grad_ff_low = grad_out.astype(jnp.bfloat16)
    grad_ffout = jnp.einsum("tf,td->fd", hidden_ff, grad_ff_low, preferred_element_type=jnp.float32)
    grad_hidden = jnp.einsum(
        "td,fd->tf", grad_ff_low, ffout_full, preferred_element_type=jnp.float32
    )
    grad_gate, grad_upward = pull_gate(grad_hidden)
    grad_gate_up = jnp.stack([grad_gate, grad_upward]).astype(jnp.bfloat16)
    grad_ffin = jnp.einsum(
        "td,ktf->kdf", normed2_low, grad_gate_up, preferred_element_type=jnp.float32
    )
    grad_normed2 = jnp.einsum(
        "ktf,kdf->td", grad_gate_up, ffin_full, preferred_element_type=jnp.float32
    )
    grad_part2, grad_gain2 = norm_backward(hidden2, scale2, gains[2], grad_normed2)
    grad_h2 = grad_out + grad_part2
    grad_cross_low = grad_h2.astype(jnp.bfloat16)
    grad_proj_cross = jnp.einsum(
        "te,td->ed", cross_attended, grad_cross_low, preferred_element_type=jnp.float32
    )
    grad_cross_att = jnp.einsum(
        "td,ed->te", grad_cross_low, proj_full[1], preferred_element_type=jnp.float32
    ).astype(jnp.bfloat16)
    grad_cross_query, grad_cross_pairs = cross_backward(
        cross_query, cross_pairs, grad_cross_att, cross_logs
    )
    grad_attn_cq = jnp.einsum(
        "td,te->de", normed1_low, grad_cross_query, preferred_element_type=jnp.float32
    )
    grad_attn_ckv = jnp.einsum(
        "td,kte->kde", states_flat, grad_cross_pairs, preferred_element_type=jnp.float32
    )
    encoder_grad = jnp.einsum(
        "kte,kde->td", grad_cross_pairs, attn_full[4:6], preferred_element_type=jnp.float32
    ).reshape(sequences, states_len, width)
    grad_normed1 = jnp.einsum(
        "te,de->td", grad_cross_query, attn_full[3], preferred_element_type=jnp.float32
    )
    grad_part1, grad_gain1 = norm_backward(hidden1, scale1, gains[1], grad_normed1)
    grad_h1 = grad_h2 + grad_part1
    grad_self_low = grad_h1.astype(jnp.bfloat16)
    grad_proj_self = jnp.einsum(
        "te,td->ed", attended, grad_self_low, preferred_element_type=jnp.float32
    )
    grad_attended = jnp.einsum(
        "td,ed->te", grad_self_low, proj_full[0], preferred_element_type=jnp.float32
    ).astype(jnp.bfloat16)
    grad_self_heads, table_parts = self_backward(
        self_heads, grad_attended, self_logs, bias, kseg, qseg, bucket_table, buckets
    )
    grad_attn_qkv = jnp.einsum(
        "td,kte->kde", normed0_low, grad_self_heads, preferred_element_type=jnp.float32
    )
    grad_normed0 = jnp.einsum(
        "kte,kde->td", grad_self_heads, attn_full[0:3], preferred_element_type=jnp.float32
    )
    grad_part0, grad_gain0 = norm_backward(stream, scale0, gains[0], grad_normed0)
    input_grad = (grad_h1 + grad_part0).reshape(sequences, length, width)
    grad_table = table_parts[:, 0:2].reshape(H, buckets).T
    grad_attn = jnp.concatenate([grad_attn_qkv, grad_attn_cq[None], grad_attn_ckv], axis=0)
    grad_proj = jnp.stack([grad_proj_self, grad_proj_cross])
    grad_gains = jnp.stack([grad_gain0, grad_gain1, grad_gain2])
    shares = (
        lax.psum_scatter(
            grad_attn.astype(jnp.bfloat16), "grp", scatter_dimension=1, tiled=True
        ).astype(jnp.float32),
        lax.psum_scatter(
            grad_proj.astype(jnp.bfloat16), "grp", scatter_dimension=2, tiled=True
        ).astype(jnp.float32),
        lax.psum_scatter(
            grad_ffin.astype(jnp.bfloat16), "grp", scatter_dimension=1, tiled=True
        ).astype(jnp.float32),
        lax.psum_scatter(
            grad_ffout.astype(jnp.bfloat16), "grp", scatter_dimension=1, tiled=True
        ).astype(jnp.float32),
        lax.psum_scatter(
            grad_gains.astype(jnp.bfloat16), "grp", scatter_dimension=1, tiled=True
        ).astype(jnp.float32),
        lax.psum_scatter(
            grad_table.astype(jnp.bfloat16), "grp", scatter_dimension=0, tiled=True
        ).astype(jnp.float32),
    )
    share_attn, share_proj, share_ffin, share_ffout, share_gains, share_bias = shares
    replicas = lax.axis_size("rep")
    merged = (
        share_attn + err_attn[0],
        jnp.swapaxes(share_proj + err_attn_out[0], 1, 2),
        share_ffin + err_ff_in[0],
        (share_ffout + err_ff_out[0]).T[None],
    )
    factors = (q_start[0:6], q_start[6:8], q_start[8:10], q_start[10:11])
    projected = [
        jnp.einsum("ksw,ksr->krw", matrix, factor, precision=highest)
        for matrix, factor in zip(merged, factors)
    ]
    first_sums = lax.psum((projected[0], share_gains, share_bias), "rep")
    left_sums = (
        (first_sums[0],)
        + tuple((lax.psum(part, "rep") for part in projected[1:]))
        + (first_sums[1], first_sums[2])
    )
    lefts = orthonormal(left_sums[0:4], replicas)
    rights = [
        jnp.einsum("ksw,krw->ksr", matrix, left, precision=highest)
        for matrix, left in zip(merged, lefts)
    ]
    right_sums = tuple((lax.psum(part, "rep") for part in rights))
    means = [total / replicas for total in right_sums]
    approx = [
        jnp.einsum("ksr,krw->ksw", mean, left, precision=highest)
        for mean, left in zip(means, lefts)
    ]
    errors = [matrix - change for matrix, change in zip(merged, approx)]
    steps = (
        approx[0],
        jnp.swapaxes(approx[1], 1, 2),
        approx[2],
        approx[3][0].T,
        left_sums[4] / replicas,
        left_sums[5] / replicas,
    )
    olds = (mom_attn, mom_attn_out, mom_ff_in, mom_ff_out, mom_gains, mom_bias)
    moments = tuple((decay * old + fresh for old, fresh in zip(olds, steps)))
    updates = tuple((-rate * moment for rate, moment in zip(rates, moments)))
    new_factors = jnp.concatenate(means, axis=0)
    return (
        block_output,
        input_grad,
        encoder_grad,
        branch_rms,
        share_attn[None],
        share_proj[None],
        share_ffin[None],
        share_ffout[None],
        share_gains[None],
        share_bias[None],
        errors[0][None],
        jnp.swapaxes(errors[1], 1, 2)[None],
        errors[2][None],
        errors[3][0].T[None],
        moments[0],
        moments[1],
        moments[2],
        moments[3],
        moments[4],
        moments[5],
        updates[0],
        updates[1],
        updates[2],
        updates[3],
        updates[4],
        updates[5],
        new_factors,
    )


def solution(mesh):
    in_specs = (
        P(("grp", "rep"), None, None),
        P(("grp", "rep"), None, None),
        P(("grp", "rep"), None, None),
        P(("grp", "rep"), None),
        P(),
        P(None, "grp", None),
        P(None, None, "grp"),
        P(None, "grp", None),
        P(None, "grp"),
        P(None, "grp"),
        P("grp", None),
        P(None, "grp", None),
        P(None, None, "grp"),
        P(None, "grp", None),
        P(None, "grp"),
        P(None, "grp"),
        P("grp", None),
        P("rep", None, "grp", None),
        P("rep", None, None, "grp"),
        P("rep", None, "grp", None),
        P("rep", None, "grp"),
        P(None, "grp", None),
    )
    out_specs = (
        P(("grp", "rep"), None, None),
        P(("grp", "rep"), None, None),
        P(("grp", "rep"), None, None),
        P(),
        P("rep", None, "grp", None),
        P("rep", None, None, "grp"),
        P("rep", None, "grp", None),
        P("rep", None, "grp"),
        P("rep", None, "grp"),
        P("rep", "grp", None),
        P("rep", None, "grp", None),
        P("rep", None, None, "grp"),
        P("rep", None, "grp", None),
        P("rep", None, "grp"),
        P(None, "grp", None),
        P(None, None, "grp"),
        P(None, "grp", None),
        P(None, "grp"),
        P(None, "grp"),
        P("grp", None),
        P(None, "grp", None),
        P(None, None, "grp"),
        P(None, "grp", None),
        P(None, "grp"),
        P(None, "grp"),
        P("grp", None),
        P(None, "grp", None),
    )
    return jax.shard_map(body, mesh=mesh, in_specs=in_specs, out_specs=out_specs, check_vma=False)
```

```python
import functools

import jax
import jax.numpy as jnp
from jax import lax
from jax.experimental import pallas as pl
from jax.experimental.pallas import tpu as pltpu
from jax.sharding import PartitionSpec as P

H = 6
DK = 64
PAIR = 2 * DK
ROWS = 256
SHARE = 128

epsilon = 1e-06
decay = 0.5
rates = (0.002, 0.5, 0.015, 0.015, 0.005, 0.05)
masked_score = -1e30
highest = lax.Precision.HIGHEST
NT = (((1,), (1,)), ((), ()))
NN = (((1,), (0,)), ((), ()))
TN = (((0,), (0,)), ((), ()))
f32 = jnp.float32
bf16 = jnp.bfloat16


def mm(left, right, dims=NN):
    return lax.dot_general(left, right, dims, preferred_element_type=f32)


def bias_kernel(length, bucket_ref, table_ref, out_ref):
    buckets = table_ref.shape[0]
    bucket = bucket_ref[...]
    match = lax.broadcasted_iota(jnp.int32, (buckets, length), 0) == bucket
    by_gap = mm(table_ref[...], match.astype(bf16), TN)
    tiles = length // ROWS
    wide = 2 * ROWS
    padded = jnp.concatenate(
        [jnp.full((H, ROWS), masked_score, f32), by_gap], axis=1
    )
    for head in range(H):
        for tile in range(tiles):
            first = length - ROWS * (tile + 1)
            line = padded[head : head + 1, first : first + wide]
            rows = jnp.concatenate(
                [line] + [pltpu.roll(line, step, 1) for step in range(1, 8)], axis=0
            )
            while rows.shape[0] < ROWS:
                rows = jnp.concatenate([rows, pltpu.roll(rows, rows.shape[0], 1)], axis=0)
            out_ref[head, ROWS * tile : ROWS * (tile + 1), :] = rows[:, ROWS:]


def bias_tiles(bucket_table, table_low):
    length = bucket_table.shape[0]
    return pl.pallas_call(
        functools.partial(bias_kernel, length),
        out_shape=jax.ShapeDtypeStruct((H, length, ROWS), f32),
        name="bias_tiles",
    )(bucket_table.reshape(1, length), table_low)


def lane_masks(rows):
    lane = lax.broadcasted_iota(jnp.int32, (rows, PAIR), 1)
    return (lane < DK, lane >= DK)


def turned(value):
    return value.astype(f32).T.astype(bf16)


def scores_of(q_ref, keys, bias_ref, qseg_ref, first, count, half, mask):
    query = q_ref[first : first + ROWS, :]
    query = jnp.where(mask, query, jnp.zeros_like(query))
    full = query
    if qseg_ref is not None:
        full = jnp.concatenate([query, qseg_ref[first : first + ROWS, :]], axis=1)
    scores = mm(keys[:count], full, NT)
    if bias_ref is not None:
        length = bias_ref.shape[1]
        scores = scores + bias_ref[half, length - count : length, :]
    return query, scores


def forward_kernel(causal, *refs):
    if causal:
        q_ref, k_ref, v_ref, bias_ref, kseg_ref, qseg_ref, out_ref, log_ref = refs
        keys = jnp.concatenate([k_ref[...], kseg_ref[...]], axis=1)
    else:
        q_ref, k_ref, v_ref, out_ref, log_ref = refs
        bias_ref = qseg_ref = None
        keys = k_ref[...]
    length = q_ref.shape[0]
    values = turned(v_ref[...])
    masks = lane_masks(ROWS)
    log_ref[...] = jnp.zeros_like(log_ref)
    for first in range(0, length, ROWS):
        count = first + ROWS if causal else keys.shape[0]
        mixed = []
        for half in range(2):
            unused, scores = scores_of(
                q_ref, keys, bias_ref, qseg_ref, first, count, half, masks[half]
            )
            top = jnp.max(scores, axis=0, keepdims=True)
            powers = jnp.exp(scores - top)
            total = jnp.sum(powers, axis=0, keepdims=True)
            probs = (powers * (1.0 / total)).astype(bf16)
            mixed.append(mm(values[DK * half : DK * (half + 1), :count], probs))
            log_ref[half : half + 1, first : first + ROWS] = top + jnp.log(total)
        out_ref[first : first + ROWS, :] = jnp.concatenate(mixed, axis=0).T.astype(bf16)


def squeezed(rows, index):
    return pl.BlockSpec((None, rows, PAIR), index)


def column(rows):
    return pl.BlockSpec((rows, PAIR), lambda p: (0, p))


def whole(shape):
    return pl.BlockSpec(shape, lambda p: (0,) * len(shape))


def log_spec(length):
    return pl.BlockSpec((None, 8, length), lambda p: (p, 0, 0))


def bias_spec(length):
    return pl.BlockSpec((2, length, ROWS), lambda p: (p, 0, 0))


def self_forward(heads, bias, kseg, qseg):
    length = heads.shape[1]
    pairs = H // 2
    return pl.pallas_call(
        functools.partial(forward_kernel, True),
        grid=(pairs,),
        in_specs=[
            squeezed(length, lambda p: (0, 0, p)),
            squeezed(length, lambda p: (1, 0, p)),
            squeezed(length, lambda p: (2, 0, p)),
            bias_spec(length),
            whole((length, PAIR)),
            whole((length, PAIR)),
        ],
        out_specs=[column(length), log_spec(length)],
        out_shape=[
            jax.ShapeDtypeStruct((length, H * DK), bf16),
            jax.ShapeDtypeStruct((pairs, 8, length), f32),
        ],
        name="self_forward",
    )(heads, heads, heads, bias, kseg, qseg)


def cross_forward(query, pairs_kv):
    length = query.shape[0]
    states = pairs_kv.shape[1]
    pairs = H // 2
    return pl.pallas_call(
        functools.partial(forward_kernel, False),
        grid=(pairs,),
        in_specs=[
            column(length),
            squeezed(states, lambda p: (0, 0, p)),
            squeezed(states, lambda p: (1, 0, p)),
        ],
        out_specs=[column(length), log_spec(length)],
        out_shape=[
            jax.ShapeDtypeStruct((length, H * DK), bf16),
            jax.ShapeDtypeStruct((pairs, 8, length), f32),
        ],
        name="cross_forward",
    )(query, pairs_kv, pairs_kv)


def backward_kernel(causal, *refs):
    if causal:
        (q_ref, k_ref, v_ref, grad_ref, log_ref, bias_ref, kseg_ref, qseg_ref, bucket_ref,
         out_ref, table_ref, key_sum, value_sum, tile_sum) = refs
        keys = jnp.concatenate([k_ref[...], kseg_ref[...]], axis=1)
        tile_sum[...] = jnp.zeros_like(tile_sum)
    else:
        q_ref, k_ref, v_ref, grad_ref, log_ref, dq_ref, pair_ref, key_sum, value_sum = refs
        bias_ref = qseg_ref = None
        keys = k_ref[...]
    length = q_ref.shape[0]
    states = keys.shape[0]
    turned_keys = turned(k_ref[...])
    masks = lane_masks(ROWS)
    key_sum[...] = jnp.zeros_like(key_sum)
    value_sum[...] = jnp.zeros_like(value_sum)
    for first in range(0, length, ROWS):
        count = first + ROWS if causal else states
        query_grads = []
        for half in range(2):
            query, scores = scores_of(
                q_ref, keys, bias_ref, qseg_ref, first, count, half, masks[half]
            )
            probs = jnp.exp(scores - log_ref[half : half + 1, first : first + ROWS])
            grad = grad_ref[first : first + ROWS, :]
            grad = jnp.where(masks[half], grad, jnp.zeros_like(grad))
            grad_probs = mm(v_ref[:count, :], grad, NT)
            dots = jnp.sum(grad_probs * probs, axis=0, keepdims=True)
            grad_scores = (probs * (grad_probs - dots)).astype(bf16)
            value_sum[:count, :] += mm(probs.astype(bf16), grad)
            key_sum[:count, :] += mm(grad_scores, query)
            query_grads.append(mm(turned_keys[DK * half : DK * (half + 1), :count], grad_scores))
            if causal:
                tile_sum[half, length - count : length, :] += grad_scores.astype(f32)
        joined = jnp.concatenate(query_grads, axis=0).T.astype(bf16)
        if causal:
            out_ref[0, first : first + ROWS, :] = joined
        else:
            dq_ref[first : first + ROWS, :] = joined
    if causal:
        out_ref[1] = key_sum[...].astype(bf16)
        out_ref[2] = value_sum[...].astype(bf16)
        by_gap = jnp.concatenate(
            [diagonal_sums(tile_sum, half) for half in range(2)]
            + [jnp.zeros((6, length), f32)],
            axis=0,
        )
        match = lax.broadcasted_iota(jnp.int32, (SHARE, length), 0) == bucket_ref[...]
        table_ref[...] = lax.dot_general(
            by_gap, match.astype(f32), NT,
            precision=lax.Precision.HIGHEST, preferred_element_type=f32,
        )
    else:
        pair_ref[0] = key_sum[...].astype(bf16)
        pair_ref[1] = value_sum[...].astype(bf16)


def diagonal_sums(tile_sum, half):
    length = tile_sum.shape[1]
    wide = 2 * ROWS
    pieces = []
    carried = None
    for tile in range(length // ROWS):
        rows = tile_sum[half, ROWS * tile : ROWS * (tile + 1), :]
        rows = jnp.concatenate([rows, jnp.zeros_like(rows)], axis=1)
        while rows.shape[0] > 1:
            middle = rows.shape[0] // 2
            rows = rows[:middle] + pltpu.roll(rows[middle:], wide - middle, 1)
        low = rows[:, :ROWS]
        if carried is not None:
            low = low + carried
        carried = rows[:, ROWS:]
        pieces.append(low)
    return jnp.concatenate(pieces[::-1], axis=1)


def self_backward(heads, grad, logs, bias, kseg, qseg, bucket_table):
    length = heads.shape[1]
    pairs = H // 2
    return pl.pallas_call(
        functools.partial(backward_kernel, True),
        grid=(pairs,),
        in_specs=[
            squeezed(length, lambda p: (0, 0, p)),
            squeezed(length, lambda p: (1, 0, p)),
            squeezed(length, lambda p: (2, 0, p)),
            column(length),
            log_spec(length),
            bias_spec(length),
            whole((length, PAIR)),
            whole((length, PAIR)),
            whole((1, length)),
        ],
        out_specs=[
            pl.BlockSpec((3, length, PAIR), lambda p: (0, 0, p)),
            pl.BlockSpec((None, 8, SHARE), lambda p: (p, 0, 0)),
        ],
        out_shape=[
            jax.ShapeDtypeStruct((3, length, H * DK), bf16),
            jax.ShapeDtypeStruct((pairs, 8, SHARE), f32),
        ],
        scratch_shapes=[
            pltpu.VMEM((length, PAIR), f32),
            pltpu.VMEM((length, PAIR), f32),
            pltpu.VMEM((2, length, ROWS), f32),
        ],
        name="self_backward",
    )(heads, heads, heads, grad, logs, bias, kseg, qseg, bucket_table.reshape(1, length))


def cross_backward(query, pairs_kv, grad, logs):
    length = query.shape[0]
    states = pairs_kv.shape[1]
    pairs = H // 2
    return pl.pallas_call(
        functools.partial(backward_kernel, False),
        grid=(pairs,),
        in_specs=[
            column(length),
            squeezed(states, lambda p: (0, 0, p)),
            squeezed(states, lambda p: (1, 0, p)),
            column(length),
            log_spec(length),
        ],
        out_specs=[column(length), pl.BlockSpec((2, states, PAIR), lambda p: (0, 0, p))],
        out_shape=[
            jax.ShapeDtypeStruct((length, H * DK), bf16),
            jax.ShapeDtypeStruct((2, states, H * DK), bf16),
        ],
        scratch_shapes=[pltpu.VMEM((states, PAIR), f32), pltpu.VMEM((states, PAIR), f32)],
        name="cross_backward",
    )(query, pairs_kv, pairs_kv, grad, logs)


def call(kernel, grid, in_specs, out_specs, out_shape, scratch, name):
    return pl.pallas_call(
        kernel,
        grid=grid,
        in_specs=in_specs,
        out_specs=out_specs,
        out_shape=out_shape,
        scratch_shapes=scratch,
        name=name,
    )


def shape_of(shape, dtype):
    return jax.ShapeDtypeStruct(shape, dtype)


def rows_spec(rows, width):
    return pl.BlockSpec((rows, width), lambda i: (i, 0))


def fixed(shape):
    return pl.BlockSpec(shape, lambda *i: (0,) * len(shape))


def resident(shape):
    return pl.BlockSpec(
        shape, lambda *i: (0,) * len(shape), pipeline_mode=pl.Buffered(1)
    )


def scalars():
    return pl.BlockSpec(memory_space=pltpu.SMEM)


def part_of(me, step):
    return pl.ds(pl.multiple_of((me ^ step) * SHARE, SHARE), SHARE)


def norm_scale(values):
    return lax.rsqrt(jnp.mean(values * values, axis=-1, keepdims=True) + epsilon)


def norm_pull(values, gain, grad_normed):
    scale = norm_scale(values)
    weighted = grad_normed * gain
    pulled = scale * weighted - values * (
        scale * scale * scale * jnp.mean(weighted * values, axis=-1, keepdims=True)
    )
    return pulled, jnp.sum(grad_normed * values * scale, axis=0, keepdims=True)


def clear_first(*refs):
    @pl.when(pl.program_id(0) == 0)
    def _():
        for ref in refs:
            ref[...] = jnp.zeros_like(ref)


def pack_kernel(here_ref, attn_ref, out_ref, ffin_ref, ffout_ref, one, two, one_half, two_half):
    core = here_ref[1]
    inner = H * DK
    for at in range(2):
        one[inner * at : inner * (at + 1), :] = out_ref[at].astype(bf16)
    base = 2 * inner
    for matrix in range(3):
        for chunk in range(inner // SHARE):
            one[base : base + SHARE, :] = attn_ref[
                3 + matrix, :, SHARE * chunk : SHARE * (chunk + 1)
            ].astype(bf16)
            base += SHARE
    base = 0
    for matrix in range(2):
        for chunk in range(ffin_ref.shape[2] // SHARE):
            two[base : base + SHARE, :] = ffin_ref[
                matrix, :, SHARE * chunk : SHARE * (chunk + 1)
            ].astype(bf16)
            base += SHARE
    two[base:, :] = ffout_ref[...].astype(bf16)
    for full, half in ((one, one_half), (two, two_half)):
        rows = half.shape[0]
        half[...] = full[pl.ds(pl.multiple_of(core * rows, rows), rows), :]


def pack_weights(here, w_attn, w_attn_out, w_ff_in, w_ff_out):
    first = 5 * H * DK
    second = 3 * w_ff_in.shape[2]
    return pl.pallas_call(
        pack_kernel,
        in_specs=[scalars()] + [pl.BlockSpec(memory_space=pltpu.VMEM)] * 4,
        out_shape=[
            shape_of((first, SHARE), bf16),
            shape_of((second, SHARE), bf16),
            shape_of((first // 2, SHARE), bf16),
            shape_of((second // 2, SHARE), bf16),
        ],
        name="pack_weights",
    )(here, w_attn, w_attn_out, w_ff_in, w_ff_out)


def qkv_kernel(here_ref, x_ref, gains_ref, *refs):
    shares, (heads_ref, normed_ref, full_ref) = refs[:4], refs[4:]
    inner = H * DK

    @pl.when(pl.program_id(0) == 0)
    def _():
        for step in range(4):
            for matrix in range(3):
                full_ref[part_of(here_ref[0], step), inner * matrix : inner * (matrix + 1)] = (
                    shares[step][matrix]
                )

    values = x_ref[...].astype(f32)
    normed = (values * norm_scale(values) * gains_ref[0:1, :]).astype(bf16)
    normed_ref[...] = normed
    for matrix in range(3):
        heads_ref[matrix] = mm(
            normed, full_ref[:, inner * matrix : inner * (matrix + 1)]
        ).astype(bf16)


def qkv_forward(here, stream, gains, shares):
    tokens, width = stream.shape
    inner = H * DK
    return call(
        qkv_kernel,
        (tokens // ROWS,),
        [scalars(), rows_spec(ROWS, width), fixed(gains.shape)]
        + [fixed(share.shape) for share in shares],
        [
            pl.BlockSpec((3, ROWS, inner), lambda i: (0, i, 0)),
            rows_spec(ROWS, width),
            fixed((width, 3 * inner)),
        ],
        [
            shape_of((3, tokens, inner), bf16),
            shape_of((tokens, width), bf16),
            shape_of((width, 3 * inner), bf16),
        ],
        [],
        "qkv_forward",
    )(here, stream, gains, *shares)


def join_halves(here_ref, buffer, mine, other):
    rows = mine.shape[0]
    core = here_ref[1]
    buffer[pl.ds(pl.multiple_of(core * rows, rows), rows), :] = mine[...]
    buffer[pl.ds(pl.multiple_of((1 - core) * rows, rows), rows), :] = other[...]


def middle_kernel(here_ref, att_ref, x_ref, valid_ref, states_ref, gains_ref, own, m1, m2, m3,
                  o1, o2, o3, hidden_ref, normed_ref, query_ref, pairs_ref, sums_ref, wo_ref,
                  co_ref, full_ref, buffer):
    inner = H * DK
    clear_first(sums_ref)

    @pl.when(pl.program_id(0) == 0)
    def _():
        for step, pair in enumerate(((own, None), (m1, o1), (m2, o2), (m3, o3))):
            source = own
            if step:
                join_halves(here_ref, buffer, *pair)
                source = buffer
            place = part_of(here_ref[0], step)
            wo_ref[:, place] = source[0:inner, :]
            co_ref[:, place] = source[inner : 2 * inner, :]
            for chunk in range(3 * inner // SHARE):
                base = 2 * inner + SHARE * chunk
                full_ref[place, SHARE * chunk : SHARE * (chunk + 1)] = source[
                    base : base + SHARE, :
                ]

    stream = x_ref[...].astype(f32)
    valid = valid_ref[...]
    branch = mm(att_ref[...], wo_ref[...])
    hidden = stream + branch
    sums_ref[0:1, :] += jnp.sum(valid * (stream * stream), axis=0, keepdims=True)
    sums_ref[1:2, :] += jnp.sum(valid * (branch * branch), axis=0, keepdims=True)
    sums_ref[4:5, :] += jnp.sum(jnp.broadcast_to(valid, stream.shape), axis=0, keepdims=True)
    hidden_ref[...] = hidden
    normed = (hidden * norm_scale(hidden) * gains_ref[1:2, :]).astype(bf16)
    normed_ref[...] = normed
    query_ref[...] = mm(normed, full_ref[:, :inner]).astype(bf16)
    for at in range(2):
        pairs_ref[at] = mm(
            states_ref[...], full_ref[:, inner * (at + 1) : inner * (at + 2)]
        ).astype(bf16)


def middle_forward(here, attended, stream, valid, states, gains, own, mine, other):
    tokens, width = stream.shape
    inner = H * DK
    steps = tokens // ROWS
    state_rows = states.shape[0] // steps
    return call(
        middle_kernel,
        (steps,),
        [
            scalars(),
            rows_spec(ROWS, inner),
            rows_spec(ROWS, width),
            rows_spec(ROWS, 1),
            rows_spec(state_rows, width),
            fixed(gains.shape),
            resident(own.shape),
        ]
        + [resident(mine[0].shape)] * 6,
        [
            rows_spec(ROWS, width),
            rows_spec(ROWS, width),
            rows_spec(ROWS, inner),
            pl.BlockSpec((2, state_rows, inner), lambda i: (0, i, 0)),
            fixed((8, width)),
            fixed((inner, width)),
            fixed((inner, width)),
            fixed((width, 3 * inner)),
        ],
        [
            shape_of((tokens, width), f32),
            shape_of((tokens, width), bf16),
            shape_of((tokens, inner), bf16),
            shape_of((2, states.shape[0], inner), bf16),
            shape_of((8, width), f32),
            shape_of((inner, width), bf16),
            shape_of((inner, width), bf16),
            shape_of((width, 3 * inner), bf16),
        ],
        [pltpu.VMEM(own.shape, bf16)],
        "middle_forward",
    )(here, attended, stream, valid, states, gains, own, *mine, *other)


gelu_scale = 0.7978845608028654
gelu_cubic = 0.044715


def outer_kernel(here_ref, att_ref, hidden_ref, valid_ref, cot_ref, gains_ref, co_ref, own, m1,
                 m2, m3, o1, o2, o3, output_ref, grad_ref, att_grad_ref, sums_ref, gain_ref,
                 mine_ref, s1, s2, s3, buffer, up_ref, down_ref, up_sum, down_sum, out_sum):
    hidden_units = down_ref.shape[0]
    clear_first(sums_ref, gain_ref, up_sum, down_sum, out_sum)

    @pl.when(pl.program_id(0) == 0)
    def _():
        for step, pair in enumerate(((own, None), (m1, o1), (m2, o2), (m3, o3))):
            source = own
            if step:
                join_halves(here_ref, buffer, *pair)
                source = buffer
            place = part_of(here_ref[0], step)
            for chunk in range(2 * hidden_units // SHARE):
                up_ref[place, SHARE * chunk : SHARE * (chunk + 1)] = source[
                    SHARE * chunk : SHARE * (chunk + 1), :
                ]
            down_ref[:, place] = source[2 * hidden_units :, :]

    valid = valid_ref[...]
    attended = att_ref[...]
    branch = mm(attended, co_ref[...])
    hidden = hidden_ref[...] + branch
    sums_ref[2:3, :] += jnp.sum(valid * (branch * branch), axis=0, keepdims=True)
    gain = gains_ref[2:3, :]
    normed = (hidden * norm_scale(hidden) * gain).astype(bf16)
    gate = mm(normed, up_ref[:, :hidden_units])
    upward = mm(normed, up_ref[:, hidden_units:])
    square = gate * gate
    bend = jnp.tanh(gelu_scale * (gate + gelu_cubic * (square * gate)))
    half = 0.5 * (1.0 + bend)
    curved = gate * half
    slope = half + 0.5 * gate * (1.0 - bend * bend) * (
        gelu_scale * (1.0 + 3.0 * gelu_cubic * square)
    )
    active = (curved * upward).astype(bf16)
    branch = mm(active, down_ref[...])
    sums_ref[3:4, :] += jnp.sum(valid * (branch * branch), axis=0, keepdims=True)
    output_ref[...] = (hidden + branch).astype(bf16)
    grad_out = cot_ref[...].astype(f32) * valid
    grad_low = grad_out.astype(bf16)
    down_sum[...] += mm(active, grad_low, TN)
    grad_active = mm(grad_low, down_ref[...], NT)
    grad_gate = (grad_active * upward * slope).astype(bf16)
    grad_upward = (grad_active * curved).astype(bf16)
    up_sum[:, :hidden_units] += mm(normed, grad_gate, TN)
    up_sum[:, hidden_units:] += mm(normed, grad_upward, TN)
    grad_normed = mm(grad_gate, up_ref[:, :hidden_units], NT) + mm(
        grad_upward, up_ref[:, hidden_units:], NT
    )
    pulled, gain_grad = norm_pull(hidden, gain, grad_normed)
    gain_ref[0:1, :] += gain_grad
    grad_hidden = grad_out + pulled
    grad_ref[...] = grad_hidden
    grad_low = grad_hidden.astype(bf16)
    out_sum[...] += mm(attended, grad_low, TN)
    att_grad_ref[...] = mm(grad_low, co_ref[...], NT).astype(bf16)

    @pl.when(pl.program_id(0) == pl.num_programs(0) - 1)
    def _():
        for step, target in enumerate((mine_ref, s1, s2, s3)):
            place = part_of(here_ref[0], step)
            kind = target.dtype
            for chunk in range(2 * hidden_units // SHARE):
                target[SHARE * chunk : SHARE * (chunk + 1), :] = up_sum[
                    place, SHARE * chunk : SHARE * (chunk + 1)
                ].astype(kind)
            target[2 * hidden_units : 3 * hidden_units, :] = down_sum[:, place].astype(kind)
            target[3 * hidden_units :, :] = out_sum[:, place].astype(kind)


def outer_layer(here, attended, hidden, valid, cotangent, gains, co_full, own, mine, other):
    tokens, width = hidden.shape
    inner = H * DK
    units = own.shape[0] // 3
    send = (3 * units + inner, SHARE)
    return call(
        outer_kernel,
        (tokens // ROWS,),
        [
            scalars(),
            rows_spec(ROWS, inner),
            rows_spec(ROWS, width),
            rows_spec(ROWS, 1),
            rows_spec(ROWS, width),
            fixed(gains.shape),
            resident(co_full.shape),
            resident(own.shape),
        ]
        + [resident(mine[0].shape)] * 6,
        [
            rows_spec(ROWS, width),
            rows_spec(ROWS, width),
            rows_spec(ROWS, inner),
            fixed((8, width)),
            fixed((8, width)),
        ]
        + [resident(send)] * 4,
        [
            shape_of((tokens, width), bf16),
            shape_of((tokens, width), f32),
            shape_of((tokens, inner), bf16),
            shape_of((8, width), f32),
            shape_of((8, width), f32),
            shape_of(send, f32),
        ]
        + [shape_of(send, bf16)] * 3,
        [
            pltpu.VMEM(own.shape, bf16),
            pltpu.VMEM((width, 2 * units), bf16),
            pltpu.VMEM((units, width), bf16),
            pltpu.VMEM((width, 2 * units), f32),
            pltpu.VMEM((units, width), f32),
            pltpu.VMEM((inner, width), f32),
        ],
        "outer_layer",
    )(here, attended, hidden, valid, cotangent, gains, co_full, own, *mine, *other)


def inner_kernel(here_ref, query_grad_ref, hidden_ref, normed_ref, att_ref, grad_ref, pair_ref,
                 states_ref, gains_ref, wo_ref, full_ref, grad1_ref, att_grad_ref, states_grad_ref,
                 gain_ref, mine_ref, s1, s2, s3, out_sum, full_sum):
    inner = H * DK
    clear_first(gain_ref, out_sum, full_sum)
    query_grad = query_grad_ref[...]
    grad_normed = mm(query_grad, full_ref[:, :inner], NT)
    pulled, gain_grad = norm_pull(hidden_ref[...], gains_ref[1:2, :], grad_normed)
    gain_ref[0:1, :] += gain_grad
    grad_hidden = grad_ref[...] + pulled
    grad1_ref[...] = grad_hidden
    grad_low = grad_hidden.astype(bf16)
    out_sum[...] += mm(att_ref[...], grad_low, TN)
    att_grad_ref[...] = mm(grad_low, wo_ref[...], NT).astype(bf16)
    full_sum[:, :inner] += mm(normed_ref[...], query_grad, TN)
    total = None
    for at in range(2):
        columns = slice(inner * (at + 1), inner * (at + 2))
        full_sum[:, columns] += mm(states_ref[...], pair_ref[at], TN)
        piece = mm(pair_ref[at], full_ref[:, columns], NT)
        total = piece if total is None else total + piece
    states_grad_ref[...] = total

    @pl.when(pl.program_id(0) == pl.num_programs(0) - 1)
    def _():
        for step, target in enumerate((mine_ref, s1, s2, s3)):
            place = part_of(here_ref[0], step)
            kind = target.dtype
            target[:inner, :] = out_sum[:, place].astype(kind)
            for chunk in range(3 * inner // SHARE):
                base = inner + SHARE * chunk
                target[base : base + SHARE, :] = full_sum[
                    place, SHARE * chunk : SHARE * (chunk + 1)
                ].astype(kind)


def inner_backward(here, query_grad, hidden, normed, attended, grad, pair_grad, states, gains,
                   wo_full, full):
    tokens, width = hidden.shape
    inner = H * DK
    steps = tokens // ROWS
    state_rows = states.shape[0] // steps
    send = (4 * inner, SHARE)
    return call(
        inner_kernel,
        (steps,),
        [
            scalars(),
            rows_spec(ROWS, inner),
            rows_spec(ROWS, width),
            rows_spec(ROWS, width),
            rows_spec(ROWS, inner),
            rows_spec(ROWS, width),
            pl.BlockSpec((2, state_rows, inner), lambda i: (0, i, 0)),
            rows_spec(state_rows, width),
            fixed(gains.shape),
            resident(wo_full.shape),
            resident(full.shape),
        ],
        [
            rows_spec(ROWS, width),
            rows_spec(ROWS, inner),
            rows_spec(state_rows, width),
            fixed((8, width)),
        ]
        + [resident(send)] * 4,
        [
            shape_of((tokens, width), f32),
            shape_of((tokens, inner), bf16),
            shape_of(states.shape, f32),
            shape_of((8, width), f32),
            shape_of(send, f32),
        ]
        + [shape_of(send, bf16)] * 3,
        [pltpu.VMEM((inner, width), f32), pltpu.VMEM((width, 3 * inner), f32)],
        "inner_backward",
    )(here, query_grad, hidden, normed, attended, grad, pair_grad, states, gains, wo_full, full)


def weights_kernel(here_ref, heads_ref, normed_ref, mine_ref, s1, s2, s3, full_sum):
    inner = H * DK
    clear_first(full_sum)
    normed = normed_ref[...]
    for matrix in range(3):
        full_sum[:, inner * matrix : inner * (matrix + 1)] += mm(normed, heads_ref[matrix], TN)

    @pl.when(pl.program_id(0) == pl.num_programs(0) - 1)
    def _():
        for step, target in enumerate((mine_ref, s1, s2, s3)):
            place = part_of(here_ref[0], step)
            for chunk in range(3 * inner // SHARE):
                target[SHARE * chunk : SHARE * (chunk + 1), :] = full_sum[
                    place, SHARE * chunk : SHARE * (chunk + 1)
                ].astype(target.dtype)


def qkv_weights(here, head_grads, normed):
    tokens, width = normed.shape
    inner = H * DK
    send = (3 * inner, SHARE)
    return call(
        weights_kernel,
        (tokens // ROWS,),
        [
            scalars(),
            pl.BlockSpec((3, ROWS, inner), lambda i: (0, i, 0)),
            rows_spec(ROWS, width),
        ],
        [resident(send)] * 4,
        [shape_of(send, f32)] + [shape_of(send, bf16)] * 3,
        [pltpu.VMEM((width, 3 * inner), f32)],
        "qkv_weights",
    )(here, head_grads, normed)


def last_kernel(here_ref, heads_ref, x_ref, grad_ref, gains_ref, full_ref, table_ref, gain1_ref,
                gain2_ref, sums1_ref, sums2_ref, out_ref, mine_ref, s1, s2, s3, gain_sum):
    inner = H * DK
    clear_first(gain_sum)
    grad_normed = None
    for matrix in range(3):
        piece = mm(heads_ref[matrix], full_ref[:, inner * matrix : inner * (matrix + 1)], NT)
        grad_normed = piece if grad_normed is None else grad_normed + piece
    pulled, gain_grad = norm_pull(x_ref[...].astype(f32), gains_ref[0:1, :], grad_normed)
    gain_sum[0:1, :] += gain_grad
    out_ref[...] = grad_ref[...] + pulled

    @pl.when(pl.program_id(0) == pl.num_programs(0) - 1)
    def _():
        table = [table_ref[at, 0:2, :] for at in range(H // 2)]
        sums = sums1_ref[...] + sums2_ref[...]
        folded = sums[:, :SHARE]
        for chunk in range(1, sums.shape[1] // SHARE):
            folded = folded + sums[:, SHARE * chunk : SHARE * (chunk + 1)]
        upper = folded.astype(bf16).astype(f32)
        for step, target in enumerate((mine_ref, s1, s2, s3)):
            place = part_of(here_ref[0], step)
            target[...] = jnp.concatenate(
                [gain_sum[0:1, place], gain1_ref[0:1, place], gain2_ref[0:1, place],
                 jnp.zeros((5, SHARE), f32)]
                + table
                + [jnp.zeros((8 - H, SHARE), f32), upper, folded - upper],
                axis=0,
            ).astype(target.dtype)


def last_backward(here, head_grads, stream, grad, gains, full, table, gain1, gain2, sums1, sums2):
    tokens, width = stream.shape
    inner = H * DK
    send = (32, SHARE)
    return call(
        last_kernel,
        (tokens // ROWS,),
        [
            scalars(),
            pl.BlockSpec((3, ROWS, inner), lambda i: (0, i, 0)),
            rows_spec(ROWS, width),
            rows_spec(ROWS, width),
            fixed(gains.shape),
            resident(full.shape),
            fixed(table.shape),
            fixed(gain1.shape),
            fixed(gain2.shape),
            fixed(sums1.shape),
            fixed(sums2.shape),
        ],
        [rows_spec(ROWS, width)] + [resident(send)] * 4,
        [shape_of((tokens, width), f32), shape_of(send, f32)] + [shape_of(send, bf16)] * 3,
        [pltpu.VMEM((8, width), f32)],
        "last_backward",
    )(here, head_grads, stream, grad, gains, full, table, gain1, gain2, sums1, sums2)


def exact(left, right, dims):
    return lax.dot_general(
        left, right, dims, precision=highest, preferred_element_type=f32
    )


def gathered_sum(refs, first, rows):
    total = refs[0][first : first + rows, :]
    for ref in refs[1:]:
        total = total + ref[first : first + rows, :].astype(f32)
    return total


def tail_kernel(*refs):
    fs, cs = refs[0:4], refs[4:8]
    attn_err, out_err, ffin_err, ffout_err, start_ref = refs[8:13]
    part_ref, out_grad, ffin_grad, ffout_grad, left_ref = refs[13:]
    inner = H * DK
    units = ffout_err.shape[0]
    at = 0
    for matrix in range(3):
        pieces = [
            gathered_sum(cs, inner + inner * matrix + SHARE * chunk, SHARE)
            for chunk in range(inner // SHARE)
        ]
        share = jnp.concatenate(pieces, axis=1)
        part_ref[matrix] = share
        left_ref[:, at : at + inner] = exact(
            start_ref[3 + matrix], share + attn_err[3 + matrix], TN
        )
        at += inner
    for matrix in range(2):
        share = gathered_sum(cs, 0, inner) if matrix == 0 else gathered_sum(fs, 3 * units, inner)
        out_grad[matrix] = share
        left_ref[:, at : at + inner] = exact(
            start_ref[6 + matrix], share + out_err[matrix], (((0,), (1,)), ((), ()))
        )
        at += inner
    for matrix in range(2):
        pieces = [
            gathered_sum(fs, units * matrix + SHARE * chunk, SHARE)
            for chunk in range(units // SHARE)
        ]
        share = jnp.concatenate(pieces, axis=1)
        ffin_grad[matrix] = share
        left_ref[:, at : at + units] = exact(
            start_ref[8 + matrix], share + ffin_err[matrix], TN
        )
        at += units
    share = gathered_sum(fs, 2 * units, units)
    ffout_grad[...] = share
    left_ref[:, at : at + units] = exact(
        start_ref[10], share + ffout_err[...], (((0,), (1,)), ((), ()))
    )


def tail_first(fs, cs, errors, start):
    inner = H * DK
    units = errors[3].shape[0]
    return pl.pallas_call(
        tail_kernel,
        out_shape=[
            shape_of((3, SHARE, inner), f32),
            shape_of((2, inner, SHARE), f32),
            shape_of((2, SHARE, units), f32),
            shape_of((units, SHARE), f32),
            shape_of((8, 5 * inner + 3 * units), f32),
        ],
        name="tail_first",
    )(*fs, *cs, *errors, start)


def tail_qkv_kernel(*refs):
    qs, ts = refs[0:4], refs[4:8]
    attn_err, start_ref, part_ref, grad_ref, left_ref = refs[8:]
    inner = H * DK
    for matrix in range(3):
        pieces = [
            gathered_sum(qs, inner * matrix + SHARE * chunk, SHARE)
            for chunk in range(inner // SHARE)
        ]
        share = jnp.concatenate(pieces, axis=1)
        grad_ref[matrix] = share
        grad_ref[3 + matrix] = part_ref[matrix]
        left_ref[:, inner * matrix : inner * (matrix + 1)] = exact(
            start_ref[matrix], share + attn_err[matrix], TN
        )
    small = gathered_sum(ts, 0, 32)
    base = 3 * inner
    left_ref[:, base : base + SHARE] = small[0:8]
    left_ref[:, base + SHARE : base + 2 * SHARE] = small[8:16]
    left_ref[:, base + 2 * SHARE :] = small[16:24] + small[24:32]


def tail_qkv(qs, ts, attn_err, start, part):
    inner = H * DK
    return pl.pallas_call(
        tail_qkv_kernel,
        out_shape=[
            shape_of(attn_err.shape, f32),
            shape_of((8, 3 * inner + 3 * SHARE), f32),
        ],
        name="tail_qkv",
    )(*qs, *ts, attn_err, start, part)


def orthonormal(current):
    row = lax.broadcasted_iota(jnp.int32, (current.shape[0], 1), 0)
    for column in range(current.shape[0]):
        line = current[column : column + 1]
        line = line * lax.rsqrt(jnp.sum(line * line, axis=1, keepdims=True) + epsilon)
        dots = jnp.sum(current * line, axis=1, keepdims=True)
        later = current - dots * line
        current = jnp.where(row > column, later, jnp.where(row == column, line, current))
    return current


def matrices(inner, units):
    listed = []
    base = 0
    for group, count, width in ((0, 6, inner), (1, 2, inner), (2, 2, units), (3, 1, units)):
        for at in range(count):
            listed.append((group, at, base, width))
            base += width
    return listed


def spot_of(group, at):
    return slice(None) if group == 3 else at


def right_kernel(replicas, listed, groups, total_ref, *refs):
    count = len(groups)
    grads = dict(zip(groups, refs[:count]))
    errors = dict(zip(groups, refs[count : 2 * count]))
    left_ref, right_ref = refs[2 * count :]
    for index, (group, at, base, width) in enumerate(listed):
        columns = slice(base - listed[0][2], base - listed[0][2] + width)
        left = orthonormal(total_ref[:, columns] * (1.0 / replicas))
        left_ref[:, columns] = left
        spot = spot_of(group, at)
        merged = grads[group][spot] + errors[group][spot]
        right_ref[8 * index : 8 * (index + 1), :] = exact(
            left, merged, NN if group in (1, 3) else NT
        )


def tail_right(replicas, listed, total, grads, errors):
    groups = tuple(sorted(set(item[0] for item in listed)))
    lanes = sum(item[3] for item in listed)
    return pl.pallas_call(
        functools.partial(right_kernel, replicas, listed, groups),
        out_shape=[shape_of((8, lanes), f32), shape_of((8 * len(listed), SHARE), f32)],
        name="tail_right",
    )(total, *[grads[group] for group in groups], *[errors[group] for group in groups])


def final_kernel(replicas, listed, groups, more, *refs):
    rights, lefts, refs = refs[0:more], refs[more : 2 * more], refs[2 * more :]
    count = len(groups)
    grads, errors, moments, new_errors, new_moments, updates = (
        dict(zip(groups, refs[count * at : count * (at + 1)])) for at in range(6)
    )
    factor_ref = refs[6 * count]
    for place, (source, row, base, group, at, width) in enumerate(listed):
        mean = rights[source][8 * row : 8 * (row + 1), :] * (1.0 / replicas)
        factor_ref[place] = mean.T
        left = lefts[source][:, base : base + width]
        change = exact(left, mean, TN) if group in (1, 3) else exact(mean, left, TN)
        spot = spot_of(group, at)
        new_errors[group][spot] = grads[group][spot] + errors[group][spot] - change
        moment = decay * moments[group][spot] + change
        new_moments[group][spot] = moment
        updates[group][spot] = -rates[group] * moment


def tail_final(replicas, listed, rights, lefts, grads, errors, moments):
    groups = tuple(sorted(set(item[3] for item in listed)))
    picked = [table[group] for table in (grads, errors, moments) for group in groups]
    shapes = [shape_of(moments[group].shape, f32) for group in groups]
    return pl.pallas_call(
        functools.partial(final_kernel, replicas, listed, groups, len(rights)),
        out_shape=shapes * 3 + [shape_of((len(listed), SHARE, 8), f32)],
        name="tail_final",
    )(*rights, *lefts, *picked)


def swap(value, axis, bit):
    size = lax.axis_size(axis)
    return lax.ppermute(value, axis, [(at, at ^ bit) for at in range(size)])


def sum_over(value, axis):
    bit = 1
    while bit < lax.axis_size(axis):
        value = value + swap(value, axis, bit)
        bit *= 2
    return value


def after(value, *others):
    return lax.optimization_barrier((value,) + others)[0]


def body(
    block_input,
    cotangent,
    encoder_states,
    segment_ids,
    bucket_table,
    w_attn,
    w_attn_out,
    w_ff_in,
    w_ff_out,
    norm_gains,
    rel_bias,
    mom_attn,
    mom_attn_out,
    mom_ff_in,
    mom_ff_out,
    mom_gains,
    mom_bias,
    err_attn,
    err_attn_out,
    err_ff_in,
    err_ff_out,
    q_start,
):
    length, width = block_input.shape[1:]
    replicas = lax.axis_size("rep")
    owners = lax.axis_size("grp")
    buckets = rel_bias.shape[0] * owners
    group = lax.axis_index("grp")
    here = jnp.stack([group, lax.axis_index("rep") % 2]).astype(jnp.int32)
    stream = block_input[0]
    states = encoder_states[0]
    segment = segment_ids[0]
    valid = (segment > 0).astype(f32)[:, None]

    small = jnp.concatenate(
        [norm_gains, jnp.pad(rel_bias, ((0, 0), (0, SHARE - H))), jnp.zeros((5, SHARE), f32)],
        axis=0,
    ).astype(bf16)
    smalls = [small] + [swap(small, "grp", step) for step in range(1, owners)]
    stacked = jnp.stack(smalls)
    ordered = jnp.stack(
        [lax.dynamic_index_in_dim(stacked, group ^ owner, 0, False) for owner in range(owners)]
    )
    gains = ordered[:, 0:3].transpose(1, 0, 2).reshape(3, width).astype(f32)
    table_low = ordered[:, 3:11, :H].reshape(buckets, H)
    first = w_attn[0:3].astype(bf16)
    first_shares = [first] + [
        swap(after(first, smalls[-1]), "grp", step) for step in range(1, owners)
    ]
    one, two, one_half, two_half = pack_weights(here, w_attn, w_attn_out, w_ff_in, w_ff_out)
    bias = bias_tiles(bucket_table, table_low)
    one_hot = segment[:, None] == jnp.arange(PAIR)[None, :]
    kseg = one_hot.astype(bf16)
    known = jnp.arange(PAIR)[None, :] < 8
    qseg = jnp.where(known & ~one_hot, masked_score, 0.0).astype(bf16)
    one_half, bias, *first_shares = lax.optimization_barrier((one_half, bias, *first_shares))
    one_mine = [swap(one_half, "grp", step) for step in range(1, owners)]

    heads, normed0, qkv_full = qkv_forward(here, stream, gains, first_shares)
    attended, self_logs = self_forward(heads, bias, kseg, qseg)
    attended, two_half, *one_mine = lax.optimization_barrier((attended, two_half, *one_mine))
    one_other = [swap(part, "rep", 1) for part in one_mine]
    two_mine = [swap(two_half, "grp", step) for step in range(1, owners)]
    hidden1, normed1, cross_query, cross_pairs, sums1, wo_full, co_full, cross_full = middle_forward(
        here, attended, stream, valid, states, gains, one, one_mine, one_other
    )
    cross_attended, cross_logs = cross_forward(cross_query, cross_pairs)
    cross_attended, *two_mine = lax.optimization_barrier((cross_attended, *two_mine))
    two_other = [swap(part, "rep", 1) for part in two_mine]
    (block_output, grad_h2, grad_cross_att, sums2, gain2, f_own, *f_sends) = outer_layer(
        here, cross_attended, hidden1, valid, cotangent[0], gains, co_full, two, two_mine, two_other
    )
    f_parts = [swap(part, "grp", step) for step, part in zip(range(1, owners), f_sends)]
    grad_cross_query, grad_cross_pairs = cross_backward(
        cross_query, cross_pairs, grad_cross_att, cross_logs
    )
    (grad_h1, grad_attended, encoder_grad, gain1, c_own, *c_sends) = inner_backward(
        here, grad_cross_query, hidden1, normed1, attended, grad_h2, grad_cross_pairs, states, gains,
        wo_full, cross_full,
    )
    c_parts = [swap(part, "grp", step) for step, part in zip(range(1, owners), c_sends)]
    head_grads, table_parts = self_backward(
        heads, grad_attended, self_logs, bias, kseg, qseg, bucket_table
    )
    q_own, *q_sends = qkv_weights(here, head_grads, normed0)
    q_parts = [swap(part, "grp", step) for step, part in zip(range(1, owners), q_sends)]
    (input_grad, t_own, *t_sends) = last_backward(
        here, head_grads, stream, grad_h1, gains, qkv_full, table_parts, gain1, gain2, sums1, sums2
    )
    t_parts = [swap(part, "grp", step) for step, part in zip(range(1, owners), t_sends)]

    errors = (err_attn[0], err_attn_out[0], err_ff_in[0], err_ff_out[0])
    moments = (mom_attn, mom_attn_out, mom_ff_in, mom_ff_out)
    part, out_grad, ffin_grad, ffout_grad, left_two = tail_first(
        [f_own] + f_parts, [c_own] + c_parts, errors, q_start
    )
    left_two = sum_over(left_two, "rep")
    attn_grad, left_one = tail_qkv(
        [q_own] + q_parts, [t_own] + t_parts, errors[0], q_start, part
    )
    base = 3 * H * DK
    share_gains = left_one[0:3, base : base + SHARE]
    table_sum = left_one[0:H, base + SHARE : base + SHARE + buckets]
    share_bias = lax.dynamic_slice_in_dim(
        table_sum, group * (buckets // owners), buckets // owners, 1
    ).T
    left_one = sum_over(left_one, "rep")
    mean_gains = left_one[0:3, base : base + SHARE] / replicas
    mean_bias = lax.dynamic_slice_in_dim(
        left_one[0:H, base + SHARE : base + SHARE + buckets] / replicas,
        group * (buckets // owners), buckets // owners, 1,
    ).T
    totals = jnp.sum(left_one[0:5, base + 2 * SHARE :], axis=1)
    branch_rms = jnp.sqrt(totals[0:4] / totals[4])
    listed = matrices(H * DK, w_ff_out.shape[0])
    later = (part, out_grad, ffin_grad, ffout_grad)
    late_list = [(group, at - 3 if group == 0 else at, at_lane, lanes)
                 for group, at, at_lane, lanes in listed[3:]]
    late_errors = (err_attn[0, 3:], *errors[1:])
    left_late, right_late = tail_right(replicas, late_list, left_two, later, late_errors)
    right_late = sum_over(right_late, "rep")
    grads = (attn_grad, out_grad, ffin_grad, ffout_grad)
    finals_late = tail_final(
        replicas,
        [(0, 3 + place, item[2] - base, item[0], item[1], item[3])
         for place, item in enumerate(listed[6:])],
        [right_late], [left_late], grads, errors, moments,
    )
    left_early, right_early = tail_right(replicas, listed[:3], left_one, grads, errors)
    right_early = sum_over(right_early, "rep")
    finals = tail_final(
        replicas,
        [(0, place, item[2], item[0], item[1], item[3]) for place, item in enumerate(listed[:3])]
        + [(1, place, item[2] - base, item[0], item[1], item[3])
           for place, item in enumerate(listed[3:6])],
        [right_early, right_late], [left_early, left_late], grads, errors, moments,
    )
    gain_moment = decay * mom_gains + mean_gains
    bias_moment = decay * mom_bias + mean_bias
    return (
        block_output[None],
        input_grad[None],
        encoder_grad[None],
        branch_rms,
        attn_grad[None],
        out_grad[None],
        ffin_grad[None],
        ffout_grad[None],
        share_gains[None],
        share_bias[None],
        finals[0][None],
        finals_late[0][None],
        finals_late[1][None],
        finals_late[2][None],
        finals[1],
        finals_late[3],
        finals_late[4],
        finals_late[5],
        gain_moment,
        bias_moment,
        finals[2],
        finals_late[6],
        finals_late[7],
        finals_late[8],
        -rates[4] * gain_moment,
        -rates[5] * bias_moment,
        jnp.concatenate([finals[3], finals_late[9]], axis=0),
    )


def solution(mesh):
    in_specs = (
        P(("grp", "rep"), None, None),
        P(("grp", "rep"), None, None),
        P(("grp", "rep"), None, None),
        P(("grp", "rep"), None),
        P(),
        P(None, "grp", None),
        P(None, None, "grp"),
        P(None, "grp", None),
        P(None, "grp"),
        P(None, "grp"),
        P("grp", None),
        P(None, "grp", None),
        P(None, None, "grp"),
        P(None, "grp", None),
        P(None, "grp"),
        P(None, "grp"),
        P("grp", None),
        P("rep", None, "grp", None),
        P("rep", None, None, "grp"),
        P("rep", None, "grp", None),
        P("rep", None, "grp"),
        P(None, "grp", None),
    )
    out_specs = (
        P(("grp", "rep"), None, None),
        P(("grp", "rep"), None, None),
        P(("grp", "rep"), None, None),
        P(),
        P("rep", None, "grp", None),
        P("rep", None, None, "grp"),
        P("rep", None, "grp", None),
        P("rep", None, "grp"),
        P("rep", None, "grp"),
        P("rep", "grp", None),
        P("rep", None, "grp", None),
        P("rep", None, None, "grp"),
        P("rep", None, "grp", None),
        P("rep", None, "grp"),
        P(None, "grp", None),
        P(None, None, "grp"),
        P(None, "grp", None),
        P(None, "grp"),
        P(None, "grp"),
        P("grp", None),
        P(None, "grp", None),
        P(None, None, "grp"),
        P(None, "grp", None),
        P(None, "grp"),
        P(None, "grp"),
        P("grp", None),
        P(None, "grp", None),
    )
    return jax.shard_map(body, mesh=mesh, in_specs=in_specs, out_specs=out_specs, check_vma=False)
```

```python
import functools

import jax
import jax.numpy as jnp
from jax import lax
from jax.experimental import pallas as pl
from jax.experimental.pallas import tpu as pltpu
from jax.sharding import PartitionSpec as P


H = 6
DK = 64
PAIR = 2 * DK
ROWS = 256
SHARE = 128
TILE = 512

epsilon = 1e-06
decay = 0.5
rates = (0.002, 0.5, 0.015, 0.015, 0.005, 0.05)
masked_score = -1e30
NT = (((1,), (1,)), ((), ()))
NN = (((1,), (0,)), ((), ()))
TN = (((0,), (0,)), ((), ()))
f32 = jnp.float32
bf16 = jnp.bfloat16


def mm(left, right, dims=NN):
    return lax.dot_general(left, right, dims, preferred_element_type=f32)


def bias_kernel(length, bucket_ref, table_ref, out_ref):
    buckets = table_ref.shape[0]
    bucket = bucket_ref[...]
    match = lax.broadcasted_iota(jnp.int32, (buckets, length), 0) == bucket
    by_gap = mm(table_ref[...], match.astype(bf16), TN)
    tiles = length // ROWS
    wide = 2 * ROWS
    padded = jnp.concatenate(
        [jnp.full((H, ROWS), masked_score, f32), by_gap], axis=1
    )
    for head in range(H):
        for tile in range(tiles):
            first = length - ROWS * (tile + 1)
            line = padded[head : head + 1, first : first + wide]
            rows = jnp.concatenate(
                [line] + [pltpu.roll(line, step, 1) for step in range(1, 8)], axis=0
            )
            while rows.shape[0] < ROWS:
                rows = jnp.concatenate([rows, pltpu.roll(rows, rows.shape[0], 1)], axis=0)
            out_ref[head, ROWS * tile : ROWS * (tile + 1), :] = rows[:, ROWS:]


def bias_tiles(bucket_table, table_low):
    length = bucket_table.shape[0]
    return pl.pallas_call(
        functools.partial(bias_kernel, length),
        out_shape=jax.ShapeDtypeStruct((H, length, ROWS), f32),
        name="bias_tiles",
    )(bucket_table.reshape(1, length), table_low)


def lane_masks(rows):
    lane = lax.broadcasted_iota(jnp.int32, (rows, PAIR), 1)
    return (lane < DK, lane >= DK)


def turned(value):
    return value.astype(f32).T.astype(bf16)


def scores_of(q_ref, keys, bias_ref, qseg_ref, first, count, half, mask):
    query = q_ref[first : first + ROWS, :]
    query = jnp.where(mask, query, jnp.zeros_like(query))
    full = query
    if qseg_ref is not None:
        full = jnp.concatenate([query, qseg_ref[first : first + ROWS, :]], axis=1)
    scores = mm(keys[:count], full, NT)
    if bias_ref is not None:
        length = bias_ref.shape[1]
        scores = scores + bias_ref[half, length - count : length, :]
    return query, scores


def forward_kernel(causal, *refs):
    if causal:
        q_ref, k_ref, v_ref, bias_ref, kseg_ref, qseg_ref, out_ref, log_ref = refs
        keys = jnp.concatenate([k_ref[...], kseg_ref[...]], axis=1)
    else:
        q_ref, k_ref, v_ref, out_ref, log_ref = refs
        bias_ref = qseg_ref = None
        keys = k_ref[...]
    length = q_ref.shape[0]
    values = turned(v_ref[...])
    masks = lane_masks(ROWS)
    log_ref[...] = jnp.zeros_like(log_ref)

    def start(first):
        count = first + ROWS if causal else keys.shape[0]
        return [
            scores_of(q_ref, keys, bias_ref, qseg_ref, first, count, half, masks[half])[1]
            for half in range(2)
        ]

    scores = start(0)
    for first in range(0, length, ROWS):
        tops = [jnp.max(score, axis=0, keepdims=True) for score in scores]
        ahead = start(first + ROWS) if first + ROWS < length else None
        powers = [jnp.exp(score - top) for score, top in zip(scores, tops)]
        totals = [jnp.sum(power, axis=0, keepdims=True) for power in powers]
        probs = [(power * (1.0 / total)).astype(bf16) for power, total in zip(powers, totals)]
        mixed = [
            mm(values[DK * half : DK * (half + 1), : probs[half].shape[0]], probs[half])
            for half in range(2)
        ]
        for half in range(2):
            log_ref[half : half + 1, first : first + ROWS] = tops[half] + jnp.log(totals[half])
        out_ref[first : first + ROWS, :] = jnp.concatenate(mixed, axis=0).T.astype(bf16)
        scores = ahead


def squeezed(rows, index):
    return pl.BlockSpec((None, rows, PAIR), index)


def column(rows):
    return pl.BlockSpec((rows, PAIR), lambda p: (0, p))


def whole(shape):
    return pl.BlockSpec(shape, lambda p: (0,) * len(shape))


def log_spec(length):
    return pl.BlockSpec((None, 8, length), lambda p: (p, 0, 0))


def bias_spec(length):
    return pl.BlockSpec((2, length, ROWS), lambda p: (p, 0, 0))


def self_forward(heads, bias, kseg, qseg):
    length = heads.shape[1]
    pairs = H // 2
    return pl.pallas_call(
        functools.partial(forward_kernel, True),
        grid=(pairs,),
        in_specs=[
            squeezed(length, lambda p: (0, 0, p)),
            squeezed(length, lambda p: (1, 0, p)),
            squeezed(length, lambda p: (2, 0, p)),
            bias_spec(length),
            whole((length, PAIR)),
            whole((length, PAIR)),
        ],
        out_specs=[column(length), log_spec(length)],
        out_shape=[
            jax.ShapeDtypeStruct((length, H * DK), bf16),
            jax.ShapeDtypeStruct((pairs, 8, length), f32),
        ],
        name="self_forward",
    )(heads, heads, heads, bias, kseg, qseg)


def cross_forward(query, pairs_kv):
    length = query.shape[0]
    states = pairs_kv.shape[1]
    pairs = H // 2
    return pl.pallas_call(
        functools.partial(forward_kernel, False),
        grid=(pairs,),
        in_specs=[
            column(length),
            squeezed(states, lambda p: (0, 0, p)),
            squeezed(states, lambda p: (1, 0, p)),
        ],
        out_specs=[column(length), log_spec(length)],
        out_shape=[
            jax.ShapeDtypeStruct((length, H * DK), bf16),
            jax.ShapeDtypeStruct((pairs, 8, length), f32),
        ],
        name="cross_forward",
    )(query, pairs_kv, pairs_kv)


def backward_kernel(causal, *refs):
    if causal:
        (q_ref, k_ref, v_ref, grad_ref, log_ref, bias_ref, kseg_ref, qseg_ref, bucket_ref,
         out_ref, table_ref, key_sum, value_sum, tile_sum) = refs
        keys = jnp.concatenate([k_ref[...], kseg_ref[...]], axis=1)
        tile_sum[...] = jnp.zeros_like(tile_sum)
    else:
        q_ref, k_ref, v_ref, grad_ref, log_ref, dq_ref, pair_ref, key_sum, value_sum = refs
        bias_ref = qseg_ref = None
        keys = k_ref[...]
    length = q_ref.shape[0]
    states = keys.shape[0]
    turned_keys = turned(k_ref[...])
    masks = lane_masks(ROWS)
    key_sum[...] = jnp.zeros_like(key_sum)
    value_sum[...] = jnp.zeros_like(value_sum)

    def start(first):
        count = first + ROWS if causal else states
        begun = []
        for half in range(2):
            query, scores = scores_of(
                q_ref, keys, bias_ref, qseg_ref, first, count, half, masks[half]
            )
            grad = grad_ref[first : first + ROWS, :]
            grad = jnp.where(masks[half], grad, jnp.zeros_like(grad))
            begun.append((query, scores, grad, mm(v_ref[:count, :], grad, NT)))
        return begun

    begun = start(0)
    for first in range(0, length, ROWS):
        count = first + ROWS if causal else states
        probs = [
            jnp.exp(begun[half][1] - log_ref[half : half + 1, first : first + ROWS])
            for half in range(2)
        ]
        ahead = start(first + ROWS) if first + ROWS < length else None
        dots = [
            jnp.sum(begun[half][3] * probs[half], axis=0, keepdims=True) for half in range(2)
        ]
        grad_scores = [
            (probs[half] * (begun[half][3] - dots[half])).astype(bf16) for half in range(2)
        ]
        value_sum[:count, :] += mm(
            jnp.concatenate([prob.astype(bf16) for prob in probs], axis=1),
            jnp.concatenate([begun[0][2], begun[1][2]], axis=0),
        )
        key_sum[:count, :] += mm(
            jnp.concatenate(grad_scores, axis=1),
            jnp.concatenate([begun[0][0], begun[1][0]], axis=0),
        )
        query_grads = [
            mm(turned_keys[DK * half : DK * (half + 1), :count], grad_scores[half])
            for half in range(2)
        ]
        if causal:
            for half in range(2):
                tile_sum[half, length - count : length, :] += grad_scores[half].astype(f32)
        begun = ahead
        joined = jnp.concatenate(query_grads, axis=0).T.astype(bf16)
        if causal:
            out_ref[0, first : first + ROWS, :] = joined
        else:
            dq_ref[first : first + ROWS, :] = joined
    if causal:
        out_ref[1] = key_sum[...].astype(bf16)
        out_ref[2] = value_sum[...].astype(bf16)
        by_gap = jnp.concatenate(
            [diagonal_sums(tile_sum, half) for half in range(2)]
            + [jnp.zeros((6, length), f32)],
            axis=0,
        )
        match = lax.broadcasted_iota(jnp.int32, (SHARE, length), 0) == bucket_ref[...]
        table_ref[...] = lax.dot_general(
            by_gap, match.astype(f32), NT,
            precision=lax.Precision.HIGHEST, preferred_element_type=f32,
        )
    else:
        pair_ref[0] = key_sum[...].astype(bf16)
        pair_ref[1] = value_sum[...].astype(bf16)


def diagonal_sums(tile_sum, half):
    length = tile_sum.shape[1]
    wide = 2 * ROWS
    pieces = []
    carried = None
    for tile in range(length // ROWS):
        rows = tile_sum[half, ROWS * tile : ROWS * (tile + 1), :]
        rows = jnp.concatenate([rows, jnp.zeros_like(rows)], axis=1)
        while rows.shape[0] > 1:
            middle = rows.shape[0] // 2
            rows = rows[:middle] + pltpu.roll(rows[middle:], wide - middle, 1)
        low = rows[:, :ROWS]
        if carried is not None:
            low = low + carried
        carried = rows[:, ROWS:]
        pieces.append(low)
    return jnp.concatenate(pieces[::-1], axis=1)


def self_backward(heads, grad, logs, bias, kseg, qseg, bucket_table):
    length = heads.shape[1]
    pairs = H // 2
    return pl.pallas_call(
        functools.partial(backward_kernel, True),
        grid=(pairs,),
        in_specs=[
            squeezed(length, lambda p: (0, 0, p)),
            squeezed(length, lambda p: (1, 0, p)),
            squeezed(length, lambda p: (2, 0, p)),
            column(length),
            log_spec(length),
            bias_spec(length),
            whole((length, PAIR)),
            whole((length, PAIR)),
            whole((1, length)),
        ],
        out_specs=[
            pl.BlockSpec((3, length, PAIR), lambda p: (0, 0, p)),
            pl.BlockSpec((None, 8, SHARE), lambda p: (p, 0, 0)),
        ],
        out_shape=[
            jax.ShapeDtypeStruct((3, length, H * DK), bf16),
            jax.ShapeDtypeStruct((pairs, 8, SHARE), f32),
        ],
        scratch_shapes=[
            pltpu.VMEM((length, PAIR), f32),
            pltpu.VMEM((length, PAIR), f32),
            pltpu.VMEM((2, length, ROWS), f32),
        ],
        name="self_backward",
    )(heads, heads, heads, grad, logs, bias, kseg, qseg, bucket_table.reshape(1, length))


def cross_backward(query, pairs_kv, grad, logs):
    length = query.shape[0]
    states = pairs_kv.shape[1]
    pairs = H // 2
    return pl.pallas_call(
        functools.partial(backward_kernel, False),
        grid=(pairs,),
        in_specs=[
            column(length),
            squeezed(states, lambda p: (0, 0, p)),
            squeezed(states, lambda p: (1, 0, p)),
            column(length),
            log_spec(length),
        ],
        out_specs=[column(length), pl.BlockSpec((2, states, PAIR), lambda p: (0, 0, p))],
        out_shape=[
            jax.ShapeDtypeStruct((length, H * DK), bf16),
            jax.ShapeDtypeStruct((2, states, H * DK), bf16),
        ],
        scratch_shapes=[pltpu.VMEM((states, PAIR), f32), pltpu.VMEM((states, PAIR), f32)],
        name="cross_backward",
    )(query, pairs_kv, pairs_kv, grad, logs)


def call(kernel, grid, in_specs, out_specs, out_shape, scratch):
    return pl.pallas_call(
        kernel,
        grid=grid,
        in_specs=in_specs,
        out_specs=out_specs,
        out_shape=out_shape,
        scratch_shapes=scratch,
    )


def shape_of(shape, dtype):
    return jax.ShapeDtypeStruct(shape, dtype)


def rows_spec(rows, width):
    return pl.BlockSpec((rows, width), lambda i: (i, 0))


def fixed(shape):
    return pl.BlockSpec(shape, lambda *i: (0,) * len(shape))


def resident(shape):
    return pl.BlockSpec(
        shape, lambda *i: (0,) * len(shape), pipeline_mode=pl.Buffered(1)
    )


def scalars():
    return pl.BlockSpec(memory_space=pltpu.SMEM)


def part_of(me, step):
    return pl.ds(pl.multiple_of((me ^ step) * SHARE, SHARE), SHARE)


def norm_scale(values):
    return lax.rsqrt(jnp.mean(values * values, axis=-1, keepdims=True) + epsilon)


def norm_pull(values, gain, grad_normed):
    scale = norm_scale(values)
    weighted = grad_normed * gain
    pulled = scale * weighted - values * (
        scale * scale * scale * jnp.mean(weighted * values, axis=-1, keepdims=True)
    )
    return pulled, jnp.sum(grad_normed * values * scale, axis=0, keepdims=True)


def clear_first(*refs):
    @pl.when(pl.program_id(0) == 0)
    def _():
        for ref in refs:
            ref[...] = jnp.zeros_like(ref)


def pack_kernel(here_ref, attn_ref, out_ref, ffin_ref, ffout_ref, one, two, one_half, two_half):
    core = here_ref[1]
    inner = H * DK
    for at in range(2):
        one[inner * at : inner * (at + 1), :] = out_ref[at].astype(bf16)
    base = 2 * inner
    for matrix in range(3):
        for chunk in range(inner // SHARE):
            one[base : base + SHARE, :] = attn_ref[
                3 + matrix, :, SHARE * chunk : SHARE * (chunk + 1)
            ].astype(bf16)
            base += SHARE
    base = 0
    for matrix in range(2):
        for chunk in range(ffin_ref.shape[2] // SHARE):
            two[base : base + SHARE, :] = ffin_ref[
                matrix, :, SHARE * chunk : SHARE * (chunk + 1)
            ].astype(bf16)
            base += SHARE
    two[base:, :] = ffout_ref[...].astype(bf16)
    for full, half in ((one, one_half), (two, two_half)):
        rows = half.shape[0]
        half[...] = full[pl.ds(pl.multiple_of(core * rows, rows), rows), :]


def pack_weights(here, w_attn, w_attn_out, w_ff_in, w_ff_out):
    first = 5 * H * DK
    second = 3 * w_ff_in.shape[2]
    return pl.pallas_call(
        pack_kernel,
        in_specs=[scalars()] + [pl.BlockSpec(memory_space=pltpu.VMEM)] * 4,
        out_shape=[
            shape_of((first, SHARE), bf16),
            shape_of((second, SHARE), bf16),
            shape_of((first // 2, SHARE), bf16),
            shape_of((second // 2, SHARE), bf16),
        ],
        name="pack_weights",
    )(here, w_attn, w_attn_out, w_ff_in, w_ff_out)


def low_kernel(source_ref, out_ref):
    out_ref[...] = source_ref[...].astype(bf16)


def low_first(w_attn):
    spec = pl.BlockSpec((1,) + w_attn.shape[1:], lambda i: (i, 0, 0))
    return call(low_kernel, (3,), [spec], spec, shape_of((3,) + w_attn.shape[1:], bf16), [])(w_attn)


def qkv_kernel(here_ref, x_ref, gains_ref, *refs):
    shares, (heads_ref, normed_ref, full_ref) = refs[:4], refs[4:]
    inner = H * DK

    @pl.when(pl.program_id(0) == 0)
    def _():
        for step in range(4):
            for matrix in range(3):
                full_ref[part_of(here_ref[0], step), inner * matrix : inner * (matrix + 1)] = (
                    shares[step][matrix]
                )

    values = x_ref[...].astype(f32)
    normed = (values * norm_scale(values) * gains_ref[0:1, :]).astype(bf16)
    normed_ref[...] = normed
    for matrix in range(3):
        heads_ref[matrix] = mm(
            normed, full_ref[:, inner * matrix : inner * (matrix + 1)]
        ).astype(bf16)


def qkv_forward(here, stream, gains, shares):
    tokens, width = stream.shape
    inner = H * DK
    return call(
        qkv_kernel,
        (tokens // TILE,),
        [scalars(), rows_spec(TILE, width), fixed(gains.shape)]
        + [fixed(share.shape) for share in shares],
        [
            pl.BlockSpec((3, TILE, inner), lambda i: (0, i, 0)),
            rows_spec(TILE, width),
            fixed((width, 3 * inner)),
        ],
        [
            shape_of((3, tokens, inner), bf16),
            shape_of((tokens, width), bf16),
            shape_of((width, 3 * inner), bf16),
        ],
        [],
    )(here, stream, gains, *shares)


def join_halves(here_ref, buffer, mine, other):
    rows = mine.shape[0]
    core = here_ref[1]
    buffer[pl.ds(pl.multiple_of(core * rows, rows), rows), :] = mine[...]
    buffer[pl.ds(pl.multiple_of((1 - core) * rows, rows), rows), :] = other[...]


def middle_kernel(here_ref, att_ref, x_ref, valid_ref, states_ref, gains_ref, own, m1, m2, m3,
                  o1, o2, o3, hidden_ref, normed_ref, query_ref, pairs_ref, sums_ref, wo_ref,
                  co_ref, full_ref, buffer):
    inner = H * DK
    clear_first(sums_ref)

    @pl.when(pl.program_id(0) == 0)
    def _():
        for step, pair in enumerate(((own, None), (m1, o1), (m2, o2), (m3, o3))):
            source = own
            if step:
                join_halves(here_ref, buffer, *pair)
                source = buffer
            place = part_of(here_ref[0], step)
            wo_ref[:, place] = source[0:inner, :]
            co_ref[:, place] = source[inner : 2 * inner, :]
            for chunk in range(3 * inner // SHARE):
                base = 2 * inner + SHARE * chunk
                full_ref[place, SHARE * chunk : SHARE * (chunk + 1)] = source[
                    base : base + SHARE, :
                ]

    stream = x_ref[...].astype(f32)
    valid = 1.0 - valid_ref[:, 0:1].astype(f32)
    branch = mm(att_ref[...], wo_ref[...])
    hidden = stream + branch
    sums_ref[0:1, :] += jnp.sum(valid * (stream * stream), axis=0, keepdims=True)
    sums_ref[1:2, :] += jnp.sum(valid * (branch * branch), axis=0, keepdims=True)
    sums_ref[4:5, :] += jnp.sum(jnp.broadcast_to(valid, stream.shape), axis=0, keepdims=True)
    hidden_ref[...] = hidden
    normed = (hidden * norm_scale(hidden) * gains_ref[1:2, :]).astype(bf16)
    normed_ref[...] = normed
    query_ref[...] = mm(normed, full_ref[:, :inner]).astype(bf16)
    for at in range(2):
        pairs_ref[at] = mm(
            states_ref[...], full_ref[:, inner * (at + 1) : inner * (at + 2)]
        ).astype(bf16)


def middle_forward(here, attended, stream, valid, states, gains, own, mine, other):
    tokens, width = stream.shape
    inner = H * DK
    steps = tokens // TILE
    state_rows = states.shape[0] // steps
    return call(
        middle_kernel,
        (steps,),
        [
            scalars(),
            rows_spec(TILE, inner),
            rows_spec(TILE, width),
            rows_spec(TILE, PAIR),
            rows_spec(state_rows, width),
            fixed(gains.shape),
            resident(own.shape),
        ]
        + [resident(mine[0].shape)] * 6,
        [
            rows_spec(TILE, width),
            rows_spec(TILE, width),
            rows_spec(TILE, inner),
            pl.BlockSpec((2, state_rows, inner), lambda i: (0, i, 0)),
            fixed((8, width)),
            fixed((inner, width)),
            fixed((inner, width)),
            fixed((width, 3 * inner)),
        ],
        [
            shape_of((tokens, width), f32),
            shape_of((tokens, width), bf16),
            shape_of((tokens, inner), bf16),
            shape_of((2, states.shape[0], inner), bf16),
            shape_of((8, width), f32),
            shape_of((inner, width), bf16),
            shape_of((inner, width), bf16),
            shape_of((width, 3 * inner), bf16),
        ],
        [pltpu.VMEM(own.shape, bf16)],
    )(here, attended, stream, valid, states, gains, own, *mine, *other)


gelu_scale = 0.7978845608028654
gelu_cubic = 0.044715


def outer_kernel(here_ref, att_ref, hidden_ref, valid_ref, cot_ref, gains_ref, co_ref, own, m1,
                 m2, m3, o1, o2, o3, output_ref, grad_ref, att_grad_ref, sums_ref, gain_ref,
                 mine_ref, to_x, to_y, keep_y, keep_x, buffer, up_ref, down_ref, up_sum, down_sum,
                 out_sum):
    hidden_units = down_ref.shape[0]
    clear_first(sums_ref, gain_ref, up_sum, down_sum, out_sum)

    @pl.when(pl.program_id(0) == 0)
    def _():
        for step, pair in enumerate(((own, None), (m1, o1), (m2, o2), (m3, o3))):
            source = own
            if step:
                join_halves(here_ref, buffer, *pair)
                source = buffer
            place = part_of(here_ref[0], step)
            for chunk in range(2 * hidden_units // SHARE):
                up_ref[place, SHARE * chunk : SHARE * (chunk + 1)] = source[
                    SHARE * chunk : SHARE * (chunk + 1), :
                ]
            down_ref[:, place] = source[2 * hidden_units :, :]

    valid = 1.0 - valid_ref[:, 0:1].astype(f32)
    attended = att_ref[...]
    branch = mm(attended, co_ref[...])
    hidden = hidden_ref[...] + branch
    sums_ref[2:3, :] += jnp.sum(valid * (branch * branch), axis=0, keepdims=True)
    gain = gains_ref[2:3, :]
    normed = (hidden * norm_scale(hidden) * gain).astype(bf16)
    gate = mm(normed, up_ref[:, :hidden_units])
    upward = mm(normed, up_ref[:, hidden_units:])
    square = gate * gate
    bend = jnp.tanh(gelu_scale * (gate + gelu_cubic * (square * gate)))
    half = 0.5 * (1.0 + bend)
    curved = gate * half
    slope = half + 0.5 * gate * (1.0 - bend * bend) * (
        gelu_scale * (1.0 + 3.0 * gelu_cubic * square)
    )
    active = (curved * upward).astype(bf16)
    branch = mm(active, down_ref[...])
    sums_ref[3:4, :] += jnp.sum(valid * (branch * branch), axis=0, keepdims=True)
    output_ref[...] = (hidden + branch).astype(bf16)
    grad_out = cot_ref[...].astype(f32) * valid
    grad_low = grad_out.astype(bf16)
    down_sum[...] += mm(active, grad_low, TN)
    grad_active = mm(grad_low, down_ref[...], NT)
    grad_gate = (grad_active * upward * slope).astype(bf16)
    grad_upward = (grad_active * curved).astype(bf16)
    up_sum[:, :hidden_units] += mm(normed, grad_gate, TN)
    up_sum[:, hidden_units:] += mm(normed, grad_upward, TN)
    grad_normed = mm(grad_gate, up_ref[:, :hidden_units], NT) + mm(
        grad_upward, up_ref[:, hidden_units:], NT
    )
    pulled, gain_grad = norm_pull(hidden, gain, grad_normed)
    gain_ref[0:1, :] += gain_grad
    grad_hidden = grad_out + pulled
    grad_ref[...] = grad_hidden
    grad_low = grad_hidden.astype(bf16)
    out_sum[...] += mm(attended, grad_low, TN)
    att_grad_ref[...] = mm(grad_low, co_ref[...], NT).astype(bf16)

    @pl.when(pl.program_id(0) == pl.num_programs(0) - 1)
    def _():
        cut = keep_y.shape[0]

        def fill(place, low, high, low_base, high_base):
            def put(first, value):
                if first < cut:
                    if low is not None:
                        at = low_base + first
                        low[at : at + value.shape[0], :] = value.astype(low.dtype)
                elif high is not None:
                    at = high_base + first - cut
                    high[at : at + value.shape[0], :] = value.astype(high.dtype)

            for chunk in range(2 * hidden_units // SHARE):
                put(SHARE * chunk, up_sum[place, SHARE * chunk : SHARE * (chunk + 1)])
            put(2 * hidden_units, down_sum[:, place])
            put(3 * hidden_units, out_sum[:, place])

        me = here_ref[0]
        high_rows = keep_x.shape[0]
        fill(part_of(me, 0), mine_ref, mine_ref, 0, cut)
        fill(part_of(me, 1), to_x, keep_x, 0, 0)
        fill(part_of(me, 2), keep_y, to_y, 0, 0)
        fill(part_of(me, 3), to_x, to_y, cut, high_rows)


def outer_layer(here, attended, hidden, valid, cotangent, gains, co_full, own, mine, other):
    tokens, width = hidden.shape
    inner = H * DK
    units = own.shape[0] // 3
    send = (3 * units + inner, SHARE)
    cut = units * 3 // 2 + SHARE
    high = send[0] - cut
    sends = [(2 * cut, SHARE), (2 * high, SHARE), (cut, SHARE), (high, SHARE)]
    return call(
        outer_kernel,
        (tokens // ROWS,),
        [
            scalars(),
            rows_spec(ROWS, inner),
            rows_spec(ROWS, width),
            rows_spec(ROWS, PAIR),
            rows_spec(ROWS, width),
            fixed(gains.shape),
            resident(co_full.shape),
            resident(own.shape),
        ]
        + [resident(mine[0].shape)] * 6,
        [
            rows_spec(ROWS, width),
            rows_spec(ROWS, width),
            rows_spec(ROWS, inner),
            fixed((8, width)),
            fixed((8, width)),
        ]
        + [resident(shape) for shape in [send] + sends],
        [
            shape_of((tokens, width), bf16),
            shape_of((tokens, width), f32),
            shape_of((tokens, inner), bf16),
            shape_of((8, width), f32),
            shape_of((8, width), f32),
            shape_of(send, f32),
        ]
        + [shape_of(shape, bf16) for shape in sends],
        [
            pltpu.VMEM(own.shape, bf16),
            pltpu.VMEM((width, 2 * units), bf16),
            pltpu.VMEM((units, width), bf16),
            pltpu.VMEM((width, 2 * units), f32),
            pltpu.VMEM((units, width), f32),
            pltpu.VMEM((inner, width), f32),
        ],
    )(here, attended, hidden, valid, cotangent, gains, co_full, own, *mine, *other)


def inner_kernel(here_ref, query_grad_ref, hidden_ref, normed_ref, att_ref, grad_ref, pair_ref,
                 states_ref, gains_ref, wo_ref, full_ref, grad1_ref, att_grad_ref, states_grad_ref,
                 gain_ref, mine_ref, s1, s2, s3, out_sum, full_sum):
    inner = H * DK
    clear_first(gain_ref, out_sum, full_sum)
    query_grad = query_grad_ref[...]
    grad_normed = mm(query_grad, full_ref[:, :inner], NT)
    pulled, gain_grad = norm_pull(hidden_ref[...], gains_ref[1:2, :], grad_normed)
    gain_ref[0:1, :] += gain_grad
    grad_hidden = grad_ref[...] + pulled
    grad1_ref[...] = grad_hidden
    grad_low = grad_hidden.astype(bf16)
    out_sum[...] += mm(att_ref[...], grad_low, TN)
    att_grad_ref[...] = mm(grad_low, wo_ref[...], NT).astype(bf16)
    full_sum[:, :inner] += mm(normed_ref[...], query_grad, TN)
    total = None
    for at in range(2):
        columns = slice(inner * (at + 1), inner * (at + 2))
        full_sum[:, columns] += mm(states_ref[...], pair_ref[at], TN)
        piece = mm(pair_ref[at], full_ref[:, columns], NT)
        total = piece if total is None else total + piece
    states_grad_ref[...] = total

    @pl.when(pl.program_id(0) == pl.num_programs(0) - 1)
    def _():
        for step, target in enumerate((mine_ref, s1, s2, s3)):
            place = part_of(here_ref[0], step)
            kind = target.dtype
            target[:inner, :] = out_sum[:, place].astype(kind)
            for chunk in range(3 * inner // SHARE):
                base = inner + SHARE * chunk
                target[base : base + SHARE, :] = full_sum[
                    place, SHARE * chunk : SHARE * (chunk + 1)
                ].astype(kind)


def inner_backward(here, query_grad, hidden, normed, attended, grad, pair_grad, states, gains,
                   wo_full, full):
    tokens, width = hidden.shape
    inner = H * DK
    steps = tokens // TILE
    state_rows = states.shape[0] // steps
    send = (4 * inner, SHARE)
    return call(
        inner_kernel,
        (steps,),
        [
            scalars(),
            rows_spec(TILE, inner),
            rows_spec(TILE, width),
            rows_spec(TILE, width),
            rows_spec(TILE, inner),
            rows_spec(TILE, width),
            pl.BlockSpec((2, state_rows, inner), lambda i: (0, i, 0)),
            rows_spec(state_rows, width),
            fixed(gains.shape),
            resident(wo_full.shape),
            resident(full.shape),
        ],
        [
            rows_spec(TILE, width),
            rows_spec(TILE, inner),
            rows_spec(state_rows, width),
            fixed((8, width)),
        ]
        + [resident(send)] * 4,
        [
            shape_of((tokens, width), f32),
            shape_of((tokens, inner), bf16),
            shape_of(states.shape, f32),
            shape_of((8, width), f32),
            shape_of(send, f32),
        ]
        + [shape_of(send, bf16)] * 3,
        [pltpu.VMEM((inner, width), f32), pltpu.VMEM((width, 3 * inner), f32)],
    )(here, query_grad, hidden, normed, attended, grad, pair_grad, states, gains, wo_full, full)


def weights_kernel(here_ref, heads_ref, normed_ref, mine_ref, s1, s2, s3, full_sum):
    inner = H * DK
    clear_first(full_sum)
    normed = normed_ref[...]
    for matrix in range(3):
        full_sum[:, inner * matrix : inner * (matrix + 1)] += mm(normed, heads_ref[matrix], TN)

    @pl.when(pl.program_id(0) == pl.num_programs(0) - 1)
    def _():
        for step, target in enumerate((mine_ref, s1, s2, s3)):
            place = part_of(here_ref[0], step)
            for chunk in range(3 * inner // SHARE):
                target[SHARE * chunk : SHARE * (chunk + 1), :] = full_sum[
                    place, SHARE * chunk : SHARE * (chunk + 1)
                ].astype(target.dtype)


def qkv_weights(here, head_grads, normed):
    tokens, width = normed.shape
    inner = H * DK
    send = (3 * inner, SHARE)
    return call(
        weights_kernel,
        (tokens // TILE,),
        [
            scalars(),
            pl.BlockSpec((3, TILE, inner), lambda i: (0, i, 0)),
            rows_spec(TILE, width),
        ],
        [resident(send)] * 4,
        [shape_of(send, f32)] + [shape_of(send, bf16)] * 3,
        [pltpu.VMEM((width, 3 * inner), f32)],
    )(here, head_grads, normed)


def last_kernel(here_ref, heads_ref, x_ref, grad_ref, gains_ref, full_ref, table_ref, gain1_ref,
                gain2_ref, sums1_ref, sums2_ref, out_ref, mine_ref, s1, s2, s3, gain_sum):
    inner = H * DK
    clear_first(gain_sum)
    grad_normed = None
    for matrix in range(3):
        piece = mm(heads_ref[matrix], full_ref[:, inner * matrix : inner * (matrix + 1)], NT)
        grad_normed = piece if grad_normed is None else grad_normed + piece
    pulled, gain_grad = norm_pull(x_ref[...].astype(f32), gains_ref[0:1, :], grad_normed)
    gain_sum[0:1, :] += gain_grad
    out_ref[...] = grad_ref[...] + pulled

    @pl.when(pl.program_id(0) == pl.num_programs(0) - 1)
    def _():
        table = [table_ref[at, 0:2, :] for at in range(H // 2)]
        sums = sums1_ref[...] + sums2_ref[...]
        folded = sums[:, :SHARE]
        for chunk in range(1, sums.shape[1] // SHARE):
            folded = folded + sums[:, SHARE * chunk : SHARE * (chunk + 1)]
        upper = folded.astype(bf16).astype(f32)
        for step, target in enumerate((mine_ref, s1, s2, s3)):
            place = part_of(here_ref[0], step)
            target[...] = jnp.concatenate(
                [gain_sum[0:1, place], gain1_ref[0:1, place], gain2_ref[0:1, place],
                 jnp.zeros((5, SHARE), f32)]
                + table
                + [jnp.zeros((8 - H, SHARE), f32), upper, folded - upper],
                axis=0,
            ).astype(target.dtype)


def last_backward(here, head_grads, stream, grad, gains, full, table, gain1, gain2, sums1, sums2):
    tokens, width = stream.shape
    inner = H * DK
    send = (32, SHARE)
    return call(
        last_kernel,
        (tokens // TILE,),
        [
            scalars(),
            pl.BlockSpec((3, TILE, inner), lambda i: (0, i, 0)),
            rows_spec(TILE, width),
            rows_spec(TILE, width),
            fixed(gains.shape),
            resident(full.shape),
            fixed(table.shape),
            fixed(gain1.shape),
            fixed(gain2.shape),
            fixed(sums1.shape),
            fixed(sums2.shape),
        ],
        [rows_spec(TILE, width)] + [resident(send)] * 4,
        [shape_of((tokens, width), f32), shape_of(send, f32)] + [shape_of(send, bf16)] * 3,
        [pltpu.VMEM((8, width), f32)],
    )(here, head_grads, stream, grad, gains, full, table, gain1, gain2, sums1, sums2)


def split(value):
    upper = value.astype(bf16)
    return upper, (value - upper.astype(f32)).astype(bf16)


def project(small, big, dims):
    small_upper, small_lower = split(small)
    big_upper, big_lower = split(big)
    rows = small.shape[0]
    product = mm(jnp.concatenate([small_upper, small_lower], axis=0), big_upper, dims)
    return product[:rows] + product[rows:] + mm(small_upper, big_lower, dims)


def outer_product(left, right):
    left_upper, left_lower = split(left)
    right_upper, right_lower = split(right)
    return mm(
        jnp.concatenate([left_upper, left_upper, left_lower], axis=0),
        jnp.concatenate([right_upper, right_lower, right_upper], axis=0),
        TN,
    )


def gathered_sum(refs, first, rows):
    total = refs[0][first : first + rows, :]
    for ref in refs[1:]:
        total = total + ref[first : first + rows, :].astype(f32)
    return total


def joined_sum(refs, first, chunks):
    pick = relayed_sum if len(refs) == 5 else gathered_sum
    return jnp.concatenate(
        [pick(refs, first + SHARE * chunk, SHARE) for chunk in range(chunks)], axis=1
    )


def relayed_sum(refs, first, rows):
    own, from_x, next_y, from_y, next_x = refs
    cut = next_y.shape[0]
    pieces, at = ((from_x, next_y), first) if first < cut else ((from_y, next_x), first - cut)
    total = own[first : first + rows, :]
    for piece in pieces:
        total = total + piece[at : at + rows, :].astype(f32)
    return total


def tail_kernel(*refs):
    fs, cs = refs[0:5], refs[5:9]
    attn_err, out_err, ffin_err, ffout_err, start_ref = refs[9:14]
    (part_ref, out_grad, ffin_grad, ffout_grad, part_sum, out_sum, ffin_sum, ffout_sum,
     left_ref) = refs[14:]
    inner = H * DK
    units = ffout_err.shape[0]
    at = 0
    for matrix in range(3):
        share = joined_sum(cs, inner + inner * matrix, inner // SHARE)
        part_ref[matrix] = share
        merged = share + attn_err[3 + matrix]
        part_sum[matrix] = merged
        left_ref[:, at : at + inner] = project(start_ref[3 + matrix], merged, NN)
        at += inner
    for matrix in range(2):
        share = gathered_sum(cs, 0, inner) if matrix == 0 else relayed_sum(fs, 3 * units, inner)
        out_grad[matrix] = share
        merged = share + out_err[matrix]
        out_sum[matrix] = merged
        left_ref[:, at : at + inner] = project(start_ref[6 + matrix], merged, NT)
        at += inner
    for matrix in range(2):
        share = joined_sum(fs, units * matrix, units // SHARE)
        ffin_grad[matrix] = share
        merged = share + ffin_err[matrix]
        ffin_sum[matrix] = merged
        left_ref[:, at : at + units] = project(start_ref[8 + matrix], merged, NN)
        at += units
    share = relayed_sum(fs, 2 * units, units)
    ffout_grad[...] = share
    merged = share + ffout_err[...]
    ffout_sum[...] = merged
    left_ref[:, at : at + units] = project(start_ref[10], merged, NT)


def tail_first(fs, cs, errors, start):
    inner = H * DK
    units = errors[3].shape[0]
    shapes = [
        shape_of((3, SHARE, inner), f32),
        shape_of((2, inner, SHARE), f32),
        shape_of((2, SHARE, units), f32),
        shape_of((units, SHARE), f32),
    ]
    return pl.pallas_call(
        tail_kernel,
        out_shape=shapes * 2 + [shape_of((8, 5 * inner + 3 * units), f32)],
        name="tail_first",
    )(*fs, *cs, *errors, start)


def tail_qkv_kernel(*refs):
    qs = refs[0:4]
    attn_err, start_ref, part_ref, part_sum, grad_ref, sum_ref, left_ref = refs[4:]
    inner = H * DK
    for matrix in range(3):
        share = joined_sum(qs, inner * matrix, inner // SHARE)
        grad_ref[matrix] = share
        grad_ref[3 + matrix] = part_ref[matrix]
        merged = share + attn_err[matrix]
        sum_ref[matrix] = merged
        sum_ref[3 + matrix] = part_sum[matrix]
        left_ref[:, inner * matrix : inner * (matrix + 1)] = project(
            start_ref[matrix], merged, NN
        )


def tail_qkv(qs, attn_err, start, part, part_sum):
    return pl.pallas_call(
        tail_qkv_kernel,
        out_shape=[
            shape_of(attn_err.shape, f32),
            shape_of(attn_err.shape, f32),
            shape_of((8, 3 * H * DK), f32),
        ],
        name="tail_qkv",
    )(*qs, attn_err, start, part, part_sum)


def orthonormal(current):
    row = lax.broadcasted_iota(jnp.int32, (current.shape[0], 1), 0)
    for column in range(current.shape[0]):
        line = current[column : column + 1]
        line = line * lax.rsqrt(jnp.sum(line * line, axis=1, keepdims=True) + epsilon)
        dots = jnp.sum(current * line, axis=1, keepdims=True)
        later = current - dots * line
        current = jnp.where(row > column, later, jnp.where(row == column, line, current))
    return current


def matrices(inner, units):
    listed = []
    base = 0
    for group, count, width in ((0, 6, inner), (1, 2, inner), (2, 2, units), (3, 1, units)):
        for at in range(count):
            listed.append((group, at, base, width))
            base += width
    return listed


def spot_of(group, at):
    return slice(None) if group == 3 else at


def owned_row(here_ref, rows, per):
    return pltpu.roll(rows, lax.rem(SHARE - per * here_ref[0], SHARE), 1)[:, :per]


def owned_bias(here_ref, tile, per):
    turned_tile = pltpu.roll(tile, lax.rem(SHARE - per * here_ref[0], SHARE), 1).T
    return turned_tile[:per, :H]


def right_kernel(replicas, listed, groups, per, here_ref, total_ref, *refs):
    count = len(groups)
    merged = dict(zip(groups, refs[:count]))
    if per:
        ts = refs[count : count + 4]
        left_ref, right_ref, gains_ref, bias_ref = refs[count + 4 :]
        small = gathered_sum(ts, 0, 32)
        base = 8 * len(listed)
        right_ref[base : base + 16, :] = small[:16]
        right_ref[base + 16 :, :] = small[16:24] + small[24:]
        for row in range(3):
            gains_ref[row] = small[row : row + 1]
        for head in range(H):
            bias_ref[head] = owned_row(here_ref, small[8 + head : 9 + head], per)
    else:
        left_ref, right_ref = refs[count:]
    lefts = [
        orthonormal(
            total_ref[:, base - listed[0][2] : base - listed[0][2] + width] * (1.0 / replicas)
        )
        for group, at, base, width in listed
    ]
    for index, (group, at, base, width) in enumerate(listed):
        left_ref[:, base - listed[0][2] : base - listed[0][2] + width] = lefts[index]
        right_ref[8 * index : 8 * (index + 1), :] = project(
            lefts[index], merged[group][spot_of(group, at)], NN if group in (1, 3) else NT
        )


def in_vmem(values):
    return [pl.BlockSpec(memory_space=pltpu.VMEM)] * len(values)


def tail_right(replicas, listed, here, total, merged, ts=(), per=0):
    groups = tuple(sorted(set(item[0] for item in listed)))
    lanes = sum(item[3] for item in listed)
    inputs = [total] + [merged[group] for group in groups] + list(ts)
    shapes = [
        shape_of((8, lanes), f32),
        shape_of((8 * len(listed) + (24 if per else 0), SHARE), f32),
    ]
    if per:
        shapes += [shape_of((3, 1, SHARE), f32), shape_of((H, 1, per), f32)]
    return pl.pallas_call(
        functools.partial(right_kernel, replicas, listed, groups, per),
        in_specs=[scalars()] + in_vmem(inputs),
        out_shape=shapes,
        name="tail_right",
    )(here, *inputs)


def final_kernel(replicas, listed, groups, more, per, here_ref, *refs):
    rights, lefts, refs = refs[0:more], refs[more : 2 * more], refs[2 * more :]
    count = len(groups)
    merged, moments, new_errors, new_moments, updates = (
        {} for _ in range(5)
    )
    for at, table in enumerate((merged, moments)):
        table.update(zip(groups, refs[count * at : count * (at + 1)]))
    refs = refs[2 * count :]
    if per:
        gain_moment, bias_moment, late_factors = refs[0:3]
        refs = refs[3:]
    for at, table in enumerate((new_errors, new_moments, updates)):
        table.update(zip(groups, refs[count * at : count * (at + 1)]))
    factor_ref = refs[3 * count]
    for place, (source, row, base, group, at, width) in enumerate(listed):
        mean = rights[source][8 * row : 8 * (row + 1), :] * (1.0 / replicas)
        factor_ref[place] = mean
        left = lefts[source][:, base : base + width]
        change = outer_product(left, mean) if group in (1, 3) else outer_product(mean, left)
        spot = spot_of(group, at)
        new_errors[group][spot] = merged[group][spot] - change
        moment = decay * moments[group][spot] + change
        new_moments[group][spot] = moment
        updates[group][spot] = -rates[group] * moment
    if per:
        factor_ref[len(listed) :] = late_factors[...]
        new_gain, new_bias, gain_update, bias_update, rms_ref = refs[3 * count + 1 :]
        base = rights[0].shape[0] - 24
        moment = decay * gain_moment[...] + rights[0][base : base + 3, :] * (1.0 / replicas)
        new_gain[...] = moment
        gain_update[...] = -rates[4] * moment
        mean = owned_bias(here_ref, rights[0][base + 8 : base + 16, :], per) * (1.0 / replicas)
        moment = decay * bias_moment[...] + mean
        new_bias[...] = moment
        bias_update[...] = -rates[5] * moment
        totals = jnp.sum(rights[0][base + 16 :, :].T, axis=0, keepdims=True)
        rms_ref[...] = jnp.sqrt(totals[:, 0:4] / totals[:, 4:5])


def tail_final(replicas, listed, here, rights, lefts, merged, moments, extra=(), per=0):
    groups = tuple(sorted(set(item[3] for item in listed)))
    picked = [table[group] for table in (merged, moments) for group in groups]
    shapes = [shape_of(moments[group].shape, f32) for group in groups]
    inputs = [*rights, *lefts, *picked, *extra]
    small = [shape_of(value.shape, f32) for value in extra[:2]] * 2
    factors = len(listed)
    if per:
        small.append(shape_of((1, 4), f32))
        factors += extra[2].shape[0]
    return pl.pallas_call(
        functools.partial(final_kernel, replicas, listed, groups, len(rights), per),
        in_specs=[scalars()] + in_vmem(inputs),
        out_shape=shapes * 3 + [shape_of((factors, 8, SHARE), f32)] + small,
        name="tail_final",
    )(here, *inputs)


def swap(value, axis, bit):
    size = lax.axis_size(axis)
    return lax.ppermute(value, axis, [(at, at ^ bit) for at in range(size)])


def sum_over(value, axis, bit=1):
    while bit < lax.axis_size(axis):
        value = value + swap(value, axis, bit)
        bit *= 2
    return value


def joined_half(kept, received):
    total = kept.astype(f32) + received[kept.shape[0] :].astype(f32)
    return total.astype(bf16)


def after(value, *others):
    return lax.optimization_barrier((value,) + others)[0]


def layer(
    block_input,
    cotangent,
    encoder_states,
    segment_ids,
    bucket_table,
    w_attn,
    w_attn_out,
    w_ff_in,
    w_ff_out,
    norm_gains,
    rel_bias,
    mom_attn,
    mom_attn_out,
    mom_ff_in,
    mom_ff_out,
    mom_gains,
    mom_bias,
    err_attn,
    err_attn_out,
    err_ff_in,
    err_ff_out,
    q_start,
):
    _, width = block_input.shape[1:]
    replicas = lax.axis_size("rep")
    owners = lax.axis_size("grp")
    buckets = rel_bias.shape[0] * owners
    group = lax.axis_index("grp")
    here = jnp.stack([group, lax.axis_index("rep") % 2]).astype(jnp.int32)
    stream = block_input[0]
    states = encoder_states[0]
    segment = segment_ids[0]

    small = jnp.concatenate(
        [norm_gains, jnp.pad(rel_bias, ((0, 0), (0, SHARE - H))), jnp.zeros((5, SHARE), f32)],
        axis=0,
    ).astype(bf16)
    smalls = [small] + [swap(small, "grp", step) for step in range(1, owners)]
    stacked = jnp.stack(smalls)
    ordered = jnp.stack(
        [lax.dynamic_index_in_dim(stacked, group ^ owner, 0, False) for owner in range(owners)]
    )
    gains = ordered[:, 0:3].transpose(1, 0, 2).reshape(3, width).astype(f32)
    table_low = ordered[:, 3:11, :H].reshape(buckets, H)
    first = low_first(w_attn)
    first_shares = [first] + [
        swap(after(first, *smalls[1:]), "grp", step) for step in range(1, owners)
    ]
    one, two, one_half, two_half = pack_weights(here, w_attn, w_attn_out, w_ff_in, w_ff_out)
    bias = bias_tiles(bucket_table, table_low)
    one_hot = segment[:, None] == jnp.arange(PAIR)[None, :]
    kseg = one_hot.astype(bf16)
    known = jnp.arange(PAIR)[None, :] < 8
    qseg = jnp.where(known & ~one_hot, masked_score, 0.0).astype(bf16)
    one_half, bias, *first_shares = lax.optimization_barrier((one_half, bias, *first_shares))
    one_mine = [swap(one_half, "grp", step) for step in range(1, owners)]

    heads, normed0, qkv_full = qkv_forward(here, stream, gains, first_shares)
    heads, two_half = lax.optimization_barrier((heads, two_half))
    two_mine = [swap(two_half, "grp", step) for step in range(1, owners)]
    attended, self_logs = self_forward(heads, bias, kseg, qseg)
    attended, *one_mine = lax.optimization_barrier((attended, *one_mine))
    one_other = [swap(part, "rep", 1) for part in one_mine]
    hidden1, normed1, cross_query, cross_pairs, sums1, wo_full, co_full, cross_full = middle_forward(
        here, attended, stream, kseg, states, gains, one, one_mine, one_other
    )
    cross_query, *two_mine = lax.optimization_barrier((cross_query, *two_mine))
    two_other = [swap(part, "rep", 1) for part in two_mine]
    cross_attended, cross_logs = cross_forward(cross_query, cross_pairs)
    (block_output, grad_h2, grad_cross_att, sums2, gain2, f_own, to_x, to_y, keep_y, keep_x) = outer_layer(
        here, cross_attended, hidden1, kseg, cotangent[0], gains, co_full, two, two_mine, two_other
    )
    from_x, from_y = swap(to_x, "grp", 1), swap(to_y, "grp", 2)
    grad_cross_query, grad_cross_pairs = cross_backward(
        cross_query, cross_pairs, grad_cross_att, cross_logs
    )
    (grad_h1, grad_attended, encoder_grad, gain1, c_own, *c_sends) = inner_backward(
        here, grad_cross_query, hidden1, normed1, attended, grad_h2, grad_cross_pairs, states, gains,
        wo_full, cross_full,
    )
    grad_attended, from_x, from_y = lax.optimization_barrier((grad_attended, from_x, from_y))
    next_y = swap(joined_half(keep_y, from_x), "grp", 2)
    next_x = swap(joined_half(keep_x, from_y), "grp", 1)
    c_parts = [swap(part, "grp", step) for step, part in zip(range(1, owners), c_sends)]
    head_grads, table_parts = self_backward(
        heads, grad_attended, self_logs, bias, kseg, qseg, bucket_table
    )
    q_own, *q_sends = qkv_weights(here, head_grads, normed0)
    errors = (err_attn[0], err_attn_out[0], err_ff_in[0], err_ff_out[0])
    moments = (mom_attn, mom_attn_out, mom_ff_in, mom_ff_out)
    start = jnp.swapaxes(q_start, 1, 2)
    head_grads, c_own, *q_sends = lax.optimization_barrier((head_grads, c_own, *q_sends))
    q_parts = [swap(part, "grp", step) for step, part in zip(range(1, owners), q_sends)]
    *firsts, left_two = tail_first(
        [f_own, from_x, next_y, from_y, next_x], [c_own] + c_parts, errors, start
    )
    part, out_grad, ffin_grad, ffout_grad, part_sum, out_sum, ffin_sum, ffout_sum = firsts
    left_two = left_two + swap(left_two, "rep", 1)
    left_two, grad_h1 = lax.optimization_barrier((left_two, grad_h1))
    (input_grad, t_own, *t_sends) = last_backward(
        here, head_grads, stream, grad_h1, gains, qkv_full, table_parts, gain1, gain2, sums1, sums2
    )
    t_parts = [swap(part, "grp", step) for step, part in zip(range(1, owners), t_sends)]
    left_two = left_two + swap(left_two, "rep", 2)
    left_two = sum_over(left_two, "rep", 4)
    attn_grad, attn_sum, left_one = tail_qkv(
        [q_own] + q_parts, errors[0], start, part, part_sum
    )
    left_one = left_one + swap(left_one, "rep", 1)
    left_one, left_two = lax.optimization_barrier((left_one, left_two))
    listed = matrices(H * DK, w_ff_out.shape[0])
    base = 3 * H * DK
    per = buckets // owners
    late_list = [(group, at - 3 if group == 0 else at, lane, lanes)
                 for group, at, lane, lanes in listed[3:]]
    left_late, right_late = tail_right(
        replicas, late_list, here, left_two, (part_sum, out_sum, ffin_sum, ffout_sum)
    )
    left_one = sum_over(left_one, "rep", 2)
    sums = (attn_sum, out_sum, ffin_sum, ffout_sum)
    right_late = sum_over(right_late, "rep")
    left_early, right_early, share_gains, share_bias = tail_right(
        replicas, listed[:3], here, left_one, sums, [t_own] + t_parts, per
    )
    right_early = right_early + swap(right_early, "rep", 1)
    right_early, right_late = lax.optimization_barrier((right_early, right_late))
    finals_late = tail_final(
        replicas,
        [(0, 3 + place, item[2] - base, item[0], item[1], item[3])
         for place, item in enumerate(listed[6:])],
        here, [right_late], [left_late], sums, moments,
    )
    right_early = sum_over(right_early, "rep", 2)
    finals = tail_final(
        replicas,
        [(0, place, item[2], item[0], item[1], item[3]) for place, item in enumerate(listed[:3])]
        + [(1, place, item[2] - base, item[0], item[1], item[3])
           for place, item in enumerate(listed[3:6])],
        here, [right_early, right_late], [left_early, left_late], sums, moments,
        (mom_gains, mom_bias, finals_late[9]), per,
    )
    gain_moment, bias_moment, gain_update, bias_update, branch_rms = finals[4:]
    branch_rms = branch_rms[0]
    factors = jnp.swapaxes(finals[3], 1, 2)
    return (
        block_output[None],
        input_grad[None],
        encoder_grad[None],
        branch_rms,
        attn_grad[None],
        out_grad[None],
        ffin_grad[None],
        ffout_grad[None],
        share_gains.transpose(1, 0, 2),
        share_bias.transpose(1, 2, 0),
        finals[0][None],
        finals_late[0][None],
        finals_late[1][None],
        finals_late[2][None],
        finals[1],
        finals_late[3],
        finals_late[4],
        finals_late[5],
        gain_moment,
        bias_moment,
        finals[2],
        finals_late[6],
        finals_late[7],
        finals_late[8],
        gain_update,
        bias_update,
        factors,
    )


def solution(mesh):
    in_specs = (
        P(("grp", "rep"), None, None),
        P(("grp", "rep"), None, None),
        P(("grp", "rep"), None, None),
        P(("grp", "rep"), None),
        P(),
        P(None, "grp", None),
        P(None, None, "grp"),
        P(None, "grp", None),
        P(None, "grp"),
        P(None, "grp"),
        P("grp", None),
        P(None, "grp", None),
        P(None, None, "grp"),
        P(None, "grp", None),
        P(None, "grp"),
        P(None, "grp"),
        P("grp", None),
        P("rep", None, "grp", None),
        P("rep", None, None, "grp"),
        P("rep", None, "grp", None),
        P("rep", None, "grp"),
        P(None, "grp", None),
    )
    out_specs = (
        P(("grp", "rep"), None, None),
        P(("grp", "rep"), None, None),
        P(("grp", "rep"), None, None),
        P(),
        P("rep", None, "grp", None),
        P("rep", None, None, "grp"),
        P("rep", None, "grp", None),
        P("rep", None, "grp"),
        P("rep", None, "grp"),
        P("rep", "grp", None),
        P("rep", None, "grp", None),
        P("rep", None, None, "grp"),
        P("rep", None, "grp", None),
        P("rep", None, "grp"),
        P(None, "grp", None),
        P(None, None, "grp"),
        P(None, "grp", None),
        P(None, "grp"),
        P(None, "grp"),
        P("grp", None),
        P(None, "grp", None),
        P(None, None, "grp"),
        P(None, "grp", None),
        P(None, "grp"),
        P(None, "grp"),
        P("grp", None),
        P(None, "grp", None),
    )
    return jax.shard_map(layer, mesh=mesh, in_specs=in_specs, out_specs=out_specs, check_vma=False)
```

```python
import functools

import jax
import jax.numpy as jnp
from jax import lax
from jax.experimental import pallas as pl
from jax.experimental.pallas import tpu as pltpu
from jax.sharding import PartitionSpec as P


H = 6
DK = 64
PAIR = 2 * DK
ROWS = 256
SHARE = 128
TILE = 512

epsilon = 1e-06
decay = 0.5
rates = (0.002, 0.5, 0.015, 0.015, 0.005, 0.05)
masked_score = -1e30
NT = (((1,), (1,)), ((), ()))
NN = (((1,), (0,)), ((), ()))
TN = (((0,), (0,)), ((), ()))
f32 = jnp.float32
bf16 = jnp.bfloat16


def mm(left, right, dims=NN):
    return lax.dot_general(left, right, dims, preferred_element_type=f32)


def bias_kernel(length, owned, here_ref, bucket_ref, own, s1, s2, s3, out_ref, gains_ref, table_ref):
    for step, source in enumerate((own, s1, s2, s3)):
        owner = here_ref[0] ^ step
        small = source[...].astype(f32)
        gains_ref[:, pl.ds(pl.multiple_of(owner * SHARE, SHARE), SHARE)] = small[0:3]
        table_ref[pl.ds(pl.multiple_of(owner * owned, owned), owned), :] = small[3 : 3 + owned]
    buckets = table_ref.shape[0]
    bucket = bucket_ref[...]
    match = lax.broadcasted_iota(jnp.int32, (buckets, length), 0) == bucket
    by_gap = mm(table_ref[...].astype(bf16), match.astype(bf16), TN)[:H]
    tiles = length // ROWS
    wide = 2 * ROWS
    padded = jnp.concatenate(
        [jnp.full((H, ROWS), masked_score, f32), by_gap], axis=1
    )
    for head in range(H):
        for tile in range(tiles):
            first = length - ROWS * (tile + 1)
            line = padded[head : head + 1, first : first + wide]
            rows = jnp.concatenate(
                [line] + [pltpu.roll(line, step, 1) for step in range(1, 8)], axis=0
            )
            while rows.shape[0] < ROWS:
                rows = jnp.concatenate([rows, pltpu.roll(rows, rows.shape[0], 1)], axis=0)
            out_ref[head, ROWS * tile : ROWS * (tile + 1), :] = rows[:, ROWS:]


def bias_tiles(here, bucket_table, smalls, owned):
    length = bucket_table.shape[0]
    owners = len(smalls)
    return pl.pallas_call(
        functools.partial(bias_kernel, length, owned),
        in_specs=[pl.BlockSpec(memory_space=pltpu.SMEM)]
        + [pl.BlockSpec(memory_space=pltpu.VMEM)] * (1 + owners),
        out_shape=[
            jax.ShapeDtypeStruct((H, length, ROWS), f32),
            jax.ShapeDtypeStruct((3, owners * SHARE), f32),
        ],
        scratch_shapes=[pltpu.VMEM((owners * owned, SHARE), f32)],
        name="bias_tiles",
    )(here, bucket_table.reshape(1, length), *smalls)


def lane_masks(rows):
    lane = lax.broadcasted_iota(jnp.int32, (rows, PAIR), 1)
    return (lane < DK, lane >= DK)


def turned(value):
    return value.astype(f32).T.astype(bf16)


def scores_of(q_ref, keys, bias_ref, qseg_ref, first, count, half, mask):
    query = q_ref[first : first + ROWS, :]
    query = jnp.where(mask, query, jnp.zeros_like(query))
    full = query
    if qseg_ref is not None:
        full = jnp.concatenate([query, qseg_ref[first : first + ROWS, :]], axis=1)
    scores = mm(keys[:count], full, NT)
    if bias_ref is not None:
        length = bias_ref.shape[1]
        scores = scores + bias_ref[half, length - count : length, :]
    return query, scores


def forward_kernel(causal, *refs):
    if causal:
        q_ref, k_ref, v_ref, bias_ref, kseg_ref, qseg_ref, out_ref, log_ref = refs
        keys = jnp.concatenate([k_ref[...], kseg_ref[...]], axis=1)
    else:
        q_ref, k_ref, v_ref, out_ref, log_ref = refs
        bias_ref = qseg_ref = None
        keys = k_ref[...]
    length = q_ref.shape[0]
    values = turned(v_ref[...])
    masks = lane_masks(ROWS)
    log_ref[...] = jnp.zeros_like(log_ref)

    def start(first):
        count = first + ROWS if causal else keys.shape[0]
        return [
            scores_of(q_ref, keys, bias_ref, qseg_ref, first, count, half, masks[half])[1]
            for half in range(2)
        ]

    scores = start(0)
    for first in range(0, length, ROWS):
        tops = [jnp.max(score, axis=0, keepdims=True) for score in scores]
        ahead = start(first + ROWS) if first + ROWS < length else None
        powers = [jnp.exp(score - top) for score, top in zip(scores, tops)]
        totals = [jnp.sum(power, axis=0, keepdims=True) for power in powers]
        probs = [(power * (1.0 / total)).astype(bf16) for power, total in zip(powers, totals)]
        mixed = [
            mm(values[DK * half : DK * (half + 1), : probs[half].shape[0]], probs[half])
            for half in range(2)
        ]
        for half in range(2):
            log_ref[half : half + 1, first : first + ROWS] = tops[half] + jnp.log(totals[half])
        out_ref[first : first + ROWS, :] = jnp.concatenate(mixed, axis=0).T.astype(bf16)
        scores = ahead


def squeezed(rows, index):
    return pl.BlockSpec((None, rows, PAIR), index)


def column(rows):
    return pl.BlockSpec((rows, PAIR), lambda p: (0, p))


def whole(shape):
    return pl.BlockSpec(shape, lambda p: (0,) * len(shape))


def log_spec(length):
    return pl.BlockSpec((None, 8, length), lambda p: (p, 0, 0))


def bias_spec(length):
    return pl.BlockSpec((2, length, ROWS), lambda p: (p, 0, 0))


def self_forward(heads, bias, kseg, qseg):
    length = heads.shape[1]
    pairs = H // 2
    return pl.pallas_call(
        functools.partial(forward_kernel, True),
        grid=(pairs,),
        in_specs=[
            squeezed(length, lambda p: (0, 0, p)),
            squeezed(length, lambda p: (1, 0, p)),
            squeezed(length, lambda p: (2, 0, p)),
            bias_spec(length),
            whole((length, PAIR)),
            whole((length, PAIR)),
        ],
        out_specs=[column(length), log_spec(length)],
        out_shape=[
            jax.ShapeDtypeStruct((length, H * DK), bf16),
            jax.ShapeDtypeStruct((pairs, 8, length), f32),
        ],
        name="self_forward",
    )(heads, heads, heads, bias, kseg, qseg)


def cross_forward(query, pairs_kv):
    length = query.shape[0]
    states = pairs_kv.shape[1]
    pairs = H // 2
    return pl.pallas_call(
        functools.partial(forward_kernel, False),
        grid=(pairs,),
        in_specs=[
            column(length),
            squeezed(states, lambda p: (0, 0, p)),
            squeezed(states, lambda p: (1, 0, p)),
        ],
        out_specs=[column(length), log_spec(length)],
        out_shape=[
            jax.ShapeDtypeStruct((length, H * DK), bf16),
            jax.ShapeDtypeStruct((pairs, 8, length), f32),
        ],
        name="cross_forward",
    )(query, pairs_kv, pairs_kv)


def backward_kernel(causal, *refs):
    if causal:
        (q_ref, k_ref, v_ref, grad_ref, log_ref, bias_ref, kseg_ref, qseg_ref, bucket_ref,
         out_ref, table_ref, key_sum, value_sum, tile_sum) = refs
        keys = jnp.concatenate([k_ref[...], kseg_ref[...]], axis=1)
        tile_sum[...] = jnp.zeros_like(tile_sum)
    else:
        q_ref, k_ref, v_ref, grad_ref, log_ref, dq_ref, pair_ref, key_sum, value_sum = refs
        bias_ref = qseg_ref = None
        keys = k_ref[...]
    length = q_ref.shape[0]
    states = keys.shape[0]
    turned_keys = turned(k_ref[...])
    masks = lane_masks(ROWS)
    key_sum[...] = jnp.zeros_like(key_sum)
    value_sum[...] = jnp.zeros_like(value_sum)

    def start(first):
        count = first + ROWS if causal else states
        begun = []
        for half in range(2):
            query, scores = scores_of(
                q_ref, keys, bias_ref, qseg_ref, first, count, half, masks[half]
            )
            grad = grad_ref[first : first + ROWS, :]
            grad = jnp.where(masks[half], grad, jnp.zeros_like(grad))
            begun.append((query, scores, grad, mm(v_ref[:count, :], grad, NT)))
        return begun

    begun = start(0)
    for first in range(0, length, ROWS):
        count = first + ROWS if causal else states
        probs = [
            jnp.exp(begun[half][1] - log_ref[half : half + 1, first : first + ROWS])
            for half in range(2)
        ]
        ahead = start(first + ROWS) if first + ROWS < length else None
        dots = [
            jnp.sum(begun[half][3] * probs[half], axis=0, keepdims=True) for half in range(2)
        ]
        grad_scores = [
            (probs[half] * (begun[half][3] - dots[half])).astype(bf16) for half in range(2)
        ]
        value_sum[:count, :] += mm(
            jnp.concatenate([prob.astype(bf16) for prob in probs], axis=1),
            jnp.concatenate([begun[0][2], begun[1][2]], axis=0),
        )
        key_sum[:count, :] += mm(
            jnp.concatenate(grad_scores, axis=1),
            jnp.concatenate([begun[0][0], begun[1][0]], axis=0),
        )
        query_grads = [
            mm(turned_keys[DK * half : DK * (half + 1), :count], grad_scores[half])
            for half in range(2)
        ]
        if causal:
            for half in range(2):
                tile_sum[half, length - count : length, :] += grad_scores[half].astype(f32)
        begun = ahead
        joined = jnp.concatenate(query_grads, axis=0).T.astype(bf16)
        if causal:
            out_ref[0, first : first + ROWS, :] = joined
        else:
            dq_ref[first : first + ROWS, :] = joined
    if causal:
        out_ref[1] = key_sum[...].astype(bf16)
        out_ref[2] = value_sum[...].astype(bf16)
        by_gap = jnp.concatenate(
            [diagonal_sums(tile_sum, half) for half in range(2)]
            + [jnp.zeros((6, length), f32)],
            axis=0,
        )
        match = lax.broadcasted_iota(jnp.int32, (SHARE, length), 0) == bucket_ref[...]
        table_ref[...] = lax.dot_general(
            by_gap, match.astype(f32), NT,
            precision=lax.Precision.HIGHEST, preferred_element_type=f32,
        )
    else:
        pair_ref[0] = key_sum[...].astype(bf16)
        pair_ref[1] = value_sum[...].astype(bf16)


def diagonal_sums(tile_sum, half):
    length = tile_sum.shape[1]
    wide = 2 * ROWS
    pieces = []
    carried = None
    for tile in range(length // ROWS):
        rows = tile_sum[half, ROWS * tile : ROWS * (tile + 1), :]
        rows = jnp.concatenate([rows, jnp.zeros_like(rows)], axis=1)
        while rows.shape[0] > 1:
            middle = rows.shape[0] // 2
            rows = rows[:middle] + pltpu.roll(rows[middle:], wide - middle, 1)
        low = rows[:, :ROWS]
        if carried is not None:
            low = low + carried
        carried = rows[:, ROWS:]
        pieces.append(low)
    return jnp.concatenate(pieces[::-1], axis=1)


def self_backward(heads, grad, logs, bias, kseg, qseg, bucket_table):
    length = heads.shape[1]
    pairs = H // 2
    return pl.pallas_call(
        functools.partial(backward_kernel, True),
        grid=(pairs,),
        in_specs=[
            squeezed(length, lambda p: (0, 0, p)),
            squeezed(length, lambda p: (1, 0, p)),
            squeezed(length, lambda p: (2, 0, p)),
            column(length),
            log_spec(length),
            bias_spec(length),
            whole((length, PAIR)),
            whole((length, PAIR)),
            whole((1, length)),
        ],
        out_specs=[
            pl.BlockSpec((3, length, PAIR), lambda p: (0, 0, p)),
            pl.BlockSpec((None, 8, SHARE), lambda p: (p, 0, 0)),
        ],
        out_shape=[
            jax.ShapeDtypeStruct((3, length, H * DK), bf16),
            jax.ShapeDtypeStruct((pairs, 8, SHARE), f32),
        ],
        scratch_shapes=[
            pltpu.VMEM((length, PAIR), f32),
            pltpu.VMEM((length, PAIR), f32),
            pltpu.VMEM((2, length, ROWS), f32),
        ],
        name="self_backward",
    )(heads, heads, heads, grad, logs, bias, kseg, qseg, bucket_table.reshape(1, length))


def cross_backward(query, pairs_kv, grad, logs):
    length = query.shape[0]
    states = pairs_kv.shape[1]
    pairs = H // 2
    return pl.pallas_call(
        functools.partial(backward_kernel, False),
        grid=(pairs,),
        in_specs=[
            column(length),
            squeezed(states, lambda p: (0, 0, p)),
            squeezed(states, lambda p: (1, 0, p)),
            column(length),
            log_spec(length),
        ],
        out_specs=[column(length), pl.BlockSpec((2, states, PAIR), lambda p: (0, 0, p))],
        out_shape=[
            jax.ShapeDtypeStruct((length, H * DK), bf16),
            jax.ShapeDtypeStruct((2, states, H * DK), bf16),
        ],
        scratch_shapes=[pltpu.VMEM((states, PAIR), f32), pltpu.VMEM((states, PAIR), f32)],
        name="cross_backward",
    )(query, pairs_kv, pairs_kv, grad, logs)


def call(kernel, grid, in_specs, out_specs, out_shape, scratch):
    return pl.pallas_call(
        kernel,
        grid=grid,
        in_specs=in_specs,
        out_specs=out_specs,
        out_shape=out_shape,
        scratch_shapes=scratch,
    )


def shape_of(shape, dtype):
    return jax.ShapeDtypeStruct(shape, dtype)


def rows_spec(rows, width):
    return pl.BlockSpec((rows, width), lambda i: (i, 0))


def fixed(shape):
    return pl.BlockSpec(shape, lambda *i: (0,) * len(shape))


def resident(shape):
    return pl.BlockSpec(
        shape, lambda *i: (0,) * len(shape), pipeline_mode=pl.Buffered(1)
    )


def scalars():
    return pl.BlockSpec(memory_space=pltpu.SMEM)


def part_of(me, step):
    return pl.ds(pl.multiple_of((me ^ step) * SHARE, SHARE), SHARE)


def norm_scale(values):
    return lax.rsqrt(jnp.mean(values * values, axis=-1, keepdims=True) + epsilon)


def norm_pull(values, gain, grad_normed):
    scale = norm_scale(values)
    weighted = grad_normed * gain
    pulled = scale * weighted - values * (
        scale * scale * scale * jnp.mean(weighted * values, axis=-1, keepdims=True)
    )
    return pulled, jnp.sum(grad_normed * values * scale, axis=0, keepdims=True)


def clear_first(*refs):
    @pl.when(pl.program_id(0) == 0)
    def _():
        for ref in refs:
            ref[...] = jnp.zeros_like(ref)


def half_of(here_ref, full, half):
    rows = half.shape[0]
    half[...] = full[pl.ds(pl.multiple_of(here_ref[1] * rows, rows), rows), :]


def pack_first_kernel(here_ref, attn_ref, out_ref, gains_ref, table_ref, full, half, small_ref):
    inner = H * DK
    owned = table_ref.shape[0]
    table = jnp.concatenate([table_ref[...], jnp.zeros((owned, SHARE - H), f32)], axis=1)
    blank = jnp.zeros((small_ref.shape[0] - 3 - owned, SHARE), f32)
    small_ref[...] = jnp.concatenate([gains_ref[...], table, blank], axis=0).astype(bf16)
    base = 0
    for matrix in range(6):
        for chunk in range(inner // SHARE):
            full[base : base + SHARE, :] = attn_ref[
                matrix, :, SHARE * chunk : SHARE * (chunk + 1)
            ].astype(bf16)
            base += SHARE
    for at in range(2):
        full[base : base + inner, :] = out_ref[at].astype(bf16)
        base += inner
    half_of(here_ref, full, half)


def pack_second_kernel(here_ref, ffin_ref, ffout_ref, full, half):
    base = 0
    for matrix in range(2):
        for chunk in range(ffin_ref.shape[2] // SHARE):
            full[base : base + SHARE, :] = ffin_ref[
                matrix, :, SHARE * chunk : SHARE * (chunk + 1)
            ].astype(bf16)
            base += SHARE
    full[base:, :] = ffout_ref[...].astype(bf16)
    half_of(here_ref, full, half)


def pack(kernel, here, inputs, rows, extra):
    return pl.pallas_call(
        kernel,
        in_specs=[scalars()] + in_vmem(inputs),
        out_shape=[shape_of((rows, SHARE), bf16), shape_of((rows // 2, SHARE), bf16)] + extra,
    )(here, *inputs)


def qkv_kernel(here_ref, x_ref, gains_ref, own, m1, m2, m3, o1, o2, o3, heads_ref, normed_ref,
               full_ref, cross_ref, wo_ref, co_ref, buffer):
    inner = H * DK
    chunks = 3 * inner // SHARE

    @pl.when(pl.program_id(0) == 0)
    def _():
        for step, pair in enumerate(((own, None), (m1, o1), (m2, o2), (m3, o3))):
            source = own
            if step:
                join_halves(here_ref, buffer, *pair)
                source = buffer
            place = part_of(here_ref[0], step)
            for at, target in enumerate((full_ref, cross_ref)):
                for chunk in range(chunks):
                    base = SHARE * (chunks * at + chunk)
                    target[place, SHARE * chunk : SHARE * (chunk + 1)] = source[
                        base : base + SHARE, :
                    ]
            base = 6 * inner
            wo_ref[:, place] = source[base : base + inner, :]
            co_ref[:, place] = source[base + inner : base + 2 * inner, :]

    values = x_ref[...].astype(f32)
    normed = (values * norm_scale(values) * gains_ref[0:1, :]).astype(bf16)
    normed_ref[...] = normed
    for matrix in range(3):
        heads_ref[matrix] = mm(
            normed, full_ref[:, inner * matrix : inner * (matrix + 1)]
        ).astype(bf16)


def qkv_forward(here, stream, gains, own, mine, other):
    tokens, width = stream.shape
    inner = H * DK
    return call(
        qkv_kernel,
        (tokens // TILE,),
        [scalars(), rows_spec(TILE, width), fixed(gains.shape), resident(own.shape)]
        + [resident(mine[0].shape)] * 6,
        [
            pl.BlockSpec((3, TILE, inner), lambda i: (0, i, 0)),
            rows_spec(TILE, width),
            resident((width, 3 * inner)),
            resident((width, 3 * inner)),
            resident((inner, width)),
            resident((inner, width)),
        ],
        [
            shape_of((3, tokens, inner), bf16),
            shape_of((tokens, width), bf16),
            shape_of((width, 3 * inner), bf16),
            shape_of((width, 3 * inner), bf16),
            shape_of((inner, width), bf16),
            shape_of((inner, width), bf16),
        ],
        [pltpu.VMEM(own.shape, bf16)],
    )(here, stream, gains, own, *mine, *other)


def join_halves(here_ref, buffer, mine, other):
    rows = mine.shape[0]
    core = here_ref[1]
    buffer[pl.ds(pl.multiple_of(core * rows, rows), rows), :] = mine[...]
    buffer[pl.ds(pl.multiple_of((1 - core) * rows, rows), rows), :] = other[...]


def middle_kernel(att_ref, x_ref, valid_ref, states_ref, gains_ref, wo_ref, full_ref, hidden_ref,
                  normed_ref, query_ref, pairs_ref, sums_ref):
    inner = H * DK
    clear_first(sums_ref)
    stream = x_ref[...].astype(f32)
    valid = 1.0 - valid_ref[:, 0:1].astype(f32)
    branch = mm(att_ref[...], wo_ref[...])
    hidden = stream + branch
    sums_ref[0:1, :] += jnp.sum(valid * (stream * stream), axis=0, keepdims=True)
    sums_ref[1:2, :] += jnp.sum(valid * (branch * branch), axis=0, keepdims=True)
    sums_ref[4:5, :] += jnp.sum(jnp.broadcast_to(valid, stream.shape), axis=0, keepdims=True)
    hidden_ref[...] = hidden
    normed = (hidden * norm_scale(hidden) * gains_ref[1:2, :]).astype(bf16)
    normed_ref[...] = normed
    query_ref[...] = mm(normed, full_ref[:, :inner]).astype(bf16)
    for at in range(2):
        pairs_ref[at] = mm(
            states_ref[...], full_ref[:, inner * (at + 1) : inner * (at + 2)]
        ).astype(bf16)


def middle_forward(attended, stream, valid, states, gains, wo_full, cross_full):
    tokens, width = stream.shape
    inner = H * DK
    steps = tokens // TILE
    state_rows = states.shape[0] // steps
    return call(
        middle_kernel,
        (steps,),
        [
            rows_spec(TILE, inner),
            rows_spec(TILE, width),
            rows_spec(TILE, PAIR),
            rows_spec(state_rows, width),
            fixed(gains.shape),
            resident(wo_full.shape),
            resident(cross_full.shape),
        ],
        [
            rows_spec(TILE, width),
            rows_spec(TILE, width),
            rows_spec(TILE, inner),
            pl.BlockSpec((2, state_rows, inner), lambda i: (0, i, 0)),
            fixed((8, width)),
        ],
        [
            shape_of((tokens, width), f32),
            shape_of((tokens, width), bf16),
            shape_of((tokens, inner), bf16),
            shape_of((2, states.shape[0], inner), bf16),
            shape_of((8, width), f32),
        ],
        [],
    )(attended, stream, valid, states, gains, wo_full, cross_full)


gelu_scale = 0.7978845608028654
gelu_cubic = 0.044715


def outer_kernel(here_ref, att_ref, hidden_ref, valid_ref, cot_ref, gains_ref, co_ref, own, m1,
                 m2, m3, o1, o2, o3, output_ref, grad_ref, att_grad_ref, sums_ref, gain_ref,
                 mine_ref, to_x, to_y, keep_y, keep_x, buffer, up_ref, down_ref, up_sum, down_sum,
                 out_sum):
    hidden_units = down_ref.shape[0]
    clear_first(sums_ref, gain_ref, up_sum, down_sum, out_sum)

    @pl.when(pl.program_id(0) == 0)
    def _():
        for step, pair in enumerate(((own, None), (m1, o1), (m2, o2), (m3, o3))):
            source = own
            if step:
                join_halves(here_ref, buffer, *pair)
                source = buffer
            place = part_of(here_ref[0], step)
            for chunk in range(2 * hidden_units // SHARE):
                up_ref[place, SHARE * chunk : SHARE * (chunk + 1)] = source[
                    SHARE * chunk : SHARE * (chunk + 1), :
                ]
            down_ref[:, place] = source[2 * hidden_units :, :]

    valid = 1.0 - valid_ref[:, 0:1].astype(f32)
    attended = att_ref[...]
    branch = mm(attended, co_ref[...])
    hidden = hidden_ref[...] + branch
    sums_ref[2:3, :] += jnp.sum(valid * (branch * branch), axis=0, keepdims=True)
    gain = gains_ref[2:3, :]
    normed = (hidden * norm_scale(hidden) * gain).astype(bf16)
    gate = mm(normed, up_ref[:, :hidden_units])
    upward = mm(normed, up_ref[:, hidden_units:])
    square = gate * gate
    bend = jnp.tanh(gelu_scale * (gate + gelu_cubic * (square * gate)))
    half = 0.5 * (1.0 + bend)
    curved = gate * half
    slope = half + 0.5 * gate * (1.0 - bend * bend) * (
        gelu_scale * (1.0 + 3.0 * gelu_cubic * square)
    )
    active = (curved * upward).astype(bf16)
    branch = mm(active, down_ref[...])
    sums_ref[3:4, :] += jnp.sum(valid * (branch * branch), axis=0, keepdims=True)
    output_ref[...] = (hidden + branch).astype(bf16)
    grad_out = cot_ref[...].astype(f32) * valid
    grad_low = grad_out.astype(bf16)
    down_sum[...] += mm(active, grad_low, TN)
    grad_active = mm(grad_low, down_ref[...], NT)
    grad_gate = (grad_active * upward * slope).astype(bf16)
    grad_upward = (grad_active * curved).astype(bf16)
    up_sum[:, :hidden_units] += mm(normed, grad_gate, TN)
    up_sum[:, hidden_units:] += mm(normed, grad_upward, TN)
    grad_normed = mm(grad_gate, up_ref[:, :hidden_units], NT) + mm(
        grad_upward, up_ref[:, hidden_units:], NT
    )
    pulled, gain_grad = norm_pull(hidden, gain, grad_normed)
    gain_ref[0:1, :] += gain_grad
    grad_hidden = grad_out + pulled
    grad_ref[...] = grad_hidden
    grad_low = grad_hidden.astype(bf16)
    out_sum[...] += mm(attended, grad_low, TN)
    att_grad_ref[...] = mm(grad_low, co_ref[...], NT).astype(bf16)

    @pl.when(pl.program_id(0) == pl.num_programs(0) - 1)
    def _():
        cut = keep_y.shape[0]

        def fill(place, low, high, low_base, high_base):
            def put(first, value):
                if first < cut:
                    if low is not None:
                        at = low_base + first
                        low[at : at + value.shape[0], :] = value.astype(low.dtype)
                elif high is not None:
                    at = high_base + first - cut
                    high[at : at + value.shape[0], :] = value.astype(high.dtype)

            for chunk in range(2 * hidden_units // SHARE):
                put(SHARE * chunk, up_sum[place, SHARE * chunk : SHARE * (chunk + 1)])
            put(2 * hidden_units, down_sum[:, place])
            put(3 * hidden_units, out_sum[:, place])

        me = here_ref[0]
        high_rows = keep_x.shape[0]
        fill(part_of(me, 0), mine_ref, mine_ref, 0, cut)
        fill(part_of(me, 1), to_x, keep_x, 0, 0)
        fill(part_of(me, 2), keep_y, to_y, 0, 0)
        fill(part_of(me, 3), to_x, to_y, cut, high_rows)


def outer_layer(here, attended, hidden, valid, cotangent, gains, co_full, own, mine, other):
    tokens, width = hidden.shape
    inner = H * DK
    units = own.shape[0] // 3
    send = (3 * units + inner, SHARE)
    cut = units * 3 // 2 + SHARE
    high = send[0] - cut
    sends = [(2 * cut, SHARE), (2 * high, SHARE), (cut, SHARE), (high, SHARE)]
    return call(
        outer_kernel,
        (tokens // ROWS,),
        [
            scalars(),
            rows_spec(ROWS, inner),
            rows_spec(ROWS, width),
            rows_spec(ROWS, PAIR),
            rows_spec(ROWS, width),
            fixed(gains.shape),
            resident(co_full.shape),
            resident(own.shape),
        ]
        + [resident(mine[0].shape)] * 6,
        [
            rows_spec(ROWS, width),
            rows_spec(ROWS, width),
            rows_spec(ROWS, inner),
            fixed((8, width)),
            fixed((8, width)),
        ]
        + [resident(shape) for shape in [send] + sends],
        [
            shape_of((tokens, width), bf16),
            shape_of((tokens, width), f32),
            shape_of((tokens, inner), bf16),
            shape_of((8, width), f32),
            shape_of((8, width), f32),
            shape_of(send, f32),
        ]
        + [shape_of(shape, bf16) for shape in sends],
        [
            pltpu.VMEM(own.shape, bf16),
            pltpu.VMEM((width, 2 * units), bf16),
            pltpu.VMEM((units, width), bf16),
            pltpu.VMEM((width, 2 * units), f32),
            pltpu.VMEM((units, width), f32),
            pltpu.VMEM((inner, width), f32),
        ],
    )(here, attended, hidden, valid, cotangent, gains, co_full, own, *mine, *other)


def inner_kernel(here_ref, query_grad_ref, hidden_ref, normed_ref, att_ref, grad_ref, pair_ref,
                 states_ref, gains_ref, wo_ref, full_ref, grad1_ref, att_grad_ref, states_grad_ref,
                 gain_ref, mine_ref, s1, s2, s3, out_sum, full_sum):
    inner = H * DK
    clear_first(gain_ref, out_sum, full_sum)
    query_grad = query_grad_ref[...]
    grad_normed = mm(query_grad, full_ref[:, :inner], NT)
    pulled, gain_grad = norm_pull(hidden_ref[...], gains_ref[1:2, :], grad_normed)
    gain_ref[0:1, :] += gain_grad
    grad_hidden = grad_ref[...] + pulled
    grad1_ref[...] = grad_hidden
    grad_low = grad_hidden.astype(bf16)
    out_sum[...] += mm(att_ref[...], grad_low, TN)
    att_grad_ref[...] = mm(grad_low, wo_ref[...], NT).astype(bf16)
    full_sum[:, :inner] += mm(normed_ref[...], query_grad, TN)
    total = None
    for at in range(2):
        columns = slice(inner * (at + 1), inner * (at + 2))
        full_sum[:, columns] += mm(states_ref[...], pair_ref[at], TN)
        piece = mm(pair_ref[at], full_ref[:, columns], NT)
        total = piece if total is None else total + piece
    states_grad_ref[...] = total

    @pl.when(pl.program_id(0) == pl.num_programs(0) - 1)
    def _():
        for step, target in enumerate((mine_ref, s1, s2, s3)):
            place = part_of(here_ref[0], step)
            kind = target.dtype
            target[:inner, :] = out_sum[:, place].astype(kind)
            for chunk in range(3 * inner // SHARE):
                base = inner + SHARE * chunk
                target[base : base + SHARE, :] = full_sum[
                    place, SHARE * chunk : SHARE * (chunk + 1)
                ].astype(kind)


def inner_backward(here, query_grad, hidden, normed, attended, grad, pair_grad, states, gains,
                   wo_full, full):
    tokens, width = hidden.shape
    inner = H * DK
    steps = tokens // TILE
    state_rows = states.shape[0] // steps
    send = (4 * inner, SHARE)
    return call(
        inner_kernel,
        (steps,),
        [
            scalars(),
            rows_spec(TILE, inner),
            rows_spec(TILE, width),
            rows_spec(TILE, width),
            rows_spec(TILE, inner),
            rows_spec(TILE, width),
            pl.BlockSpec((2, state_rows, inner), lambda i: (0, i, 0)),
            rows_spec(state_rows, width),
            fixed(gains.shape),
            resident(wo_full.shape),
            resident(full.shape),
        ],
        [
            rows_spec(TILE, width),
            rows_spec(TILE, inner),
            rows_spec(state_rows, width),
            fixed((8, width)),
        ]
        + [resident(send)] * 4,
        [
            shape_of((tokens, width), f32),
            shape_of((tokens, inner), bf16),
            shape_of(states.shape, f32),
            shape_of((8, width), f32),
            shape_of(send, f32),
        ]
        + [shape_of(send, bf16)] * 3,
        [pltpu.VMEM((inner, width), f32), pltpu.VMEM((width, 3 * inner), f32)],
    )(here, query_grad, hidden, normed, attended, grad, pair_grad, states, gains, wo_full, full)


def last_kernel(here_ref, heads_ref, normed_ref, x_ref, grad_ref, gains_ref, full_ref, table_ref,
                gain1_ref, gain2_ref, sums1_ref, sums2_ref, out_ref, mine_ref, s1, s2, s3,
                full_sum, gain_sum):
    inner = H * DK
    clear_first(full_sum, gain_sum)
    normed = normed_ref[...]
    grad_normed = None
    for matrix in range(3):
        columns = slice(inner * matrix, inner * (matrix + 1))
        piece = mm(heads_ref[matrix], full_ref[:, columns], NT)
        grad_normed = piece if grad_normed is None else grad_normed + piece
        full_sum[:, columns] += mm(normed, heads_ref[matrix], TN)
    pulled, gain_grad = norm_pull(x_ref[...].astype(f32), gains_ref[0:1, :], grad_normed)
    gain_sum[0:1, :] += gain_grad
    out_ref[...] = grad_ref[...] + pulled

    @pl.when(pl.program_id(0) == pl.num_programs(0) - 1)
    def _():
        table = [table_ref[at, 0:2, :] for at in range(H // 2)]
        sums = sums1_ref[...] + sums2_ref[...]
        folded = sums[:, :SHARE]
        for chunk in range(1, sums.shape[1] // SHARE):
            folded = folded + sums[:, SHARE * chunk : SHARE * (chunk + 1)]
        upper = folded.astype(bf16).astype(f32)
        for step, target in enumerate((mine_ref, s1, s2, s3)):
            place = part_of(here_ref[0], step)
            for chunk in range(3 * inner // SHARE):
                target[SHARE * chunk : SHARE * (chunk + 1), :] = full_sum[
                    place, SHARE * chunk : SHARE * (chunk + 1)
                ].astype(target.dtype)
            target[3 * inner :, :] = jnp.concatenate(
                [gain_sum[0:1, place], gain1_ref[0:1, place], gain2_ref[0:1, place],
                 jnp.zeros((5, SHARE), f32)]
                + table
                + [jnp.zeros((8 - H, SHARE), f32), upper, folded - upper],
                axis=0,
            ).astype(target.dtype)


def last_backward(here, head_grads, normed, stream, grad, gains, full, table, gain1, gain2, sums1,
                  sums2):
    tokens, width = stream.shape
    inner = H * DK
    send = (3 * inner + 32, SHARE)
    return call(
        last_kernel,
        (tokens // TILE,),
        [
            scalars(),
            pl.BlockSpec((3, TILE, inner), lambda i: (0, i, 0)),
            rows_spec(TILE, width),
            rows_spec(TILE, width),
            rows_spec(TILE, width),
            fixed(gains.shape),
            resident(full.shape),
            fixed(table.shape),
            fixed(gain1.shape),
            fixed(gain2.shape),
            fixed(sums1.shape),
            fixed(sums2.shape),
        ],
        [rows_spec(TILE, width)] + [resident(send)] * 4,
        [shape_of((tokens, width), f32), shape_of(send, f32)] + [shape_of(send, bf16)] * 3,
        [pltpu.VMEM((width, 3 * inner), f32), pltpu.VMEM((8, width), f32)],
    )(here, head_grads, normed, stream, grad, gains, full, table, gain1, gain2, sums1, sums2)


def split(value):
    upper = value.astype(bf16)
    return upper, (value - upper.astype(f32)).astype(bf16)


def project(small, big, dims):
    small_upper, small_lower = split(small)
    big_upper, big_lower = split(big)
    rows = small.shape[0]
    product = mm(jnp.concatenate([small_upper, small_lower], axis=0), big_upper, dims)
    return product[:rows] + product[rows:] + mm(small_upper, big_lower, dims)


def outer_product(left, right):
    left_upper, left_lower = split(left)
    right_upper, right_lower = split(right)
    return mm(
        jnp.concatenate([left_upper, left_upper, left_lower], axis=0),
        jnp.concatenate([right_upper, right_lower, right_upper], axis=0),
        TN,
    )


def gathered_sum(refs, first, rows):
    total = refs[0][first : first + rows, :]
    for ref in refs[1:]:
        total = total + ref[first : first + rows, :].astype(f32)
    return total


def joined_sum(refs, first, chunks):
    pick = relayed_sum if len(refs) == 5 else gathered_sum
    return jnp.concatenate(
        [pick(refs, first + SHARE * chunk, SHARE) for chunk in range(chunks)], axis=1
    )


def relayed_sum(refs, first, rows):
    own, from_x, next_y, from_y, next_x = refs
    cut = next_y.shape[0]
    pieces, at = ((from_x, next_y), first) if first < cut else ((from_y, next_x), first - cut)
    total = own[first : first + rows, :]
    for piece in pieces:
        total = total + piece[at : at + rows, :].astype(f32)
    return total


def tail_kernel(*refs):
    fs, cs = refs[0:5], refs[5:9]
    attn_err, out_err, ffin_err, ffout_err, start_ref = refs[9:14]
    (part_ref, out_grad, ffin_grad, ffout_grad, part_sum, out_sum, ffin_sum, ffout_sum,
     left_ref) = refs[14:]
    inner = H * DK
    units = ffout_err.shape[0]
    at = 0
    for matrix in range(3):
        share = joined_sum(cs, inner + inner * matrix, inner // SHARE)
        part_ref[matrix] = share
        merged = share + attn_err[3 + matrix]
        part_sum[matrix] = merged
        left_ref[:, at : at + inner] = project(start_ref[3 + matrix], merged, NN)
        at += inner
    for matrix in range(2):
        share = gathered_sum(cs, 0, inner) if matrix == 0 else relayed_sum(fs, 3 * units, inner)
        out_grad[matrix] = share
        merged = share + out_err[matrix]
        out_sum[matrix] = merged
        left_ref[:, at : at + inner] = project(start_ref[6 + matrix], merged, NT)
        at += inner
    for matrix in range(2):
        share = joined_sum(fs, units * matrix, units // SHARE)
        ffin_grad[matrix] = share
        merged = share + ffin_err[matrix]
        ffin_sum[matrix] = merged
        left_ref[:, at : at + units] = project(start_ref[8 + matrix], merged, NN)
        at += units
    share = relayed_sum(fs, 2 * units, units)
    ffout_grad[...] = share
    merged = share + ffout_err[...]
    ffout_sum[...] = merged
    left_ref[:, at : at + units] = project(start_ref[10], merged, NT)


def tail_first(fs, cs, errors, start):
    inner = H * DK
    units = errors[3].shape[0]
    shapes = [
        shape_of((3, SHARE, inner), f32),
        shape_of((2, inner, SHARE), f32),
        shape_of((2, SHARE, units), f32),
        shape_of((units, SHARE), f32),
    ]
    return pl.pallas_call(
        tail_kernel,
        out_shape=shapes * 2 + [shape_of((8, 5 * inner + 3 * units), f32)],
        name="tail_first",
    )(*fs, *cs, *errors, start)


def tail_qkv_kernel(*refs):
    qs = refs[0:4]
    attn_err, start_ref, part_ref, part_sum, grad_ref, sum_ref, left_ref = refs[4:]
    inner = H * DK
    for matrix in range(3):
        share = joined_sum(qs, inner * matrix, inner // SHARE)
        grad_ref[matrix] = share
        grad_ref[3 + matrix] = part_ref[matrix]
        merged = share + attn_err[matrix]
        sum_ref[matrix] = merged
        sum_ref[3 + matrix] = part_sum[matrix]
        left_ref[:, inner * matrix : inner * (matrix + 1)] = project(
            start_ref[matrix], merged, NN
        )


def tail_qkv(qs, attn_err, start, part, part_sum):
    return pl.pallas_call(
        tail_qkv_kernel,
        out_shape=[
            shape_of(attn_err.shape, f32),
            shape_of(attn_err.shape, f32),
            shape_of((8, 3 * H * DK), f32),
        ],
        name="tail_qkv",
    )(*qs, attn_err, start, part, part_sum)


def orthonormal(current):
    row = lax.broadcasted_iota(jnp.int32, (current.shape[0], 1), 0)
    for column in range(current.shape[0]):
        line = current[column : column + 1]
        line = line * lax.rsqrt(jnp.sum(line * line, axis=1, keepdims=True) + epsilon)
        dots = jnp.sum(current * line, axis=1, keepdims=True)
        later = current - dots * line
        current = jnp.where(row > column, later, jnp.where(row == column, line, current))
    return current


def matrices(inner, units):
    listed = []
    base = 0
    for group, count, width in ((0, 6, inner), (1, 2, inner), (2, 2, units), (3, 1, units)):
        for at in range(count):
            listed.append((group, at, base, width))
            base += width
    return listed


def spot_of(group, at):
    return slice(None) if group == 3 else at


def owned_row(here_ref, rows, per):
    return pltpu.roll(rows, lax.rem(SHARE - per * here_ref[0], SHARE), 1)[:, :per]


def owned_bias(here_ref, tile, per):
    turned_tile = pltpu.roll(tile, lax.rem(SHARE - per * here_ref[0], SHARE), 1).T
    return turned_tile[:per, :H]


def right_kernel(replicas, listed, groups, per, here_ref, total_ref, *refs):
    count = len(groups)
    merged = dict(zip(groups, refs[:count]))
    if per:
        ts = refs[count : count + 4]
        late_ref, left_ref, right_ref, gains_ref, bias_ref = refs[count + 4 :]
        small = gathered_sum(ts, ts[0].shape[0] - 32, 32)
        base = 8 * len(listed)
        right_ref[base : base + 16, :] = small[:16]
        right_ref[base + 16 : base + 24, :] = small[16:24] + small[24:]
        right_ref[base + 24 :, :] = late_ref[...]
        for row in range(3):
            gains_ref[row] = small[row : row + 1]
        for head in range(H):
            bias_ref[head] = owned_row(here_ref, small[8 + head : 9 + head], per)
    else:
        left_ref, right_ref = refs[count:]
    lefts = [
        orthonormal(
            total_ref[:, base - listed[0][2] : base - listed[0][2] + width] * (1.0 / replicas)
        )
        for group, at, base, width in listed
    ]
    for index, (group, at, base, width) in enumerate(listed):
        left_ref[:, base - listed[0][2] : base - listed[0][2] + width] = lefts[index]
        right_ref[8 * index : 8 * (index + 1), :] = project(
            lefts[index], merged[group][spot_of(group, at)], NN if group in (1, 3) else NT
        )


def in_vmem(values):
    return [pl.BlockSpec(memory_space=pltpu.VMEM)] * len(values)


def tail_right(replicas, listed, here, total, merged, ts=(), per=0, late=()):
    groups = tuple(sorted(set(item[0] for item in listed)))
    lanes = sum(item[3] for item in listed)
    inputs = [total] + [merged[group] for group in groups] + list(ts) + list(late)
    shapes = [
        shape_of((8, lanes), f32),
        shape_of((8 * len(listed) + (24 + late[0].shape[0] if per else 0), SHARE), f32),
    ]
    if per:
        shapes += [shape_of((3, 1, SHARE), f32), shape_of((H, 1, per), f32)]
    return pl.pallas_call(
        functools.partial(right_kernel, replicas, listed, groups, per),
        in_specs=[scalars()] + in_vmem(inputs),
        out_shape=shapes,
        name="tail_right" if per else "tail_right_late",
    )(here, *inputs)


def final_kernel(replicas, listed, groups, per, here_ref, *refs):
    rights, lefts, refs = refs[0:1], refs[1:3], refs[3:]
    count = len(groups)
    merged, moments, new_errors, new_moments, updates = (
        {} for _ in range(5)
    )
    for at, table in enumerate((merged, moments)):
        table.update(zip(groups, refs[count * at : count * (at + 1)]))
    refs = refs[2 * count :]
    if per:
        gain_moment, bias_moment = refs[0:2]
        refs = refs[2:]
    for at, table in enumerate((new_errors, new_moments, updates)):
        table.update(zip(groups, refs[count * at : count * (at + 1)]))
    factor_ref = refs[3 * count]
    for place, (source, row, base, group, at, width) in enumerate(listed):
        mean = rights[0][8 * row : 8 * (row + 1), :] * (1.0 / replicas)
        factor_ref[place] = mean
        left = lefts[source][:, base : base + width]
        change = outer_product(left, mean) if group in (1, 3) else outer_product(mean, left)
        spot = spot_of(group, at)
        new_errors[group][spot] = merged[group][spot] - change
        moment = decay * moments[group][spot] + change
        new_moments[group][spot] = moment
        updates[group][spot] = -rates[group] * moment
    if per:
        new_gain, new_bias, gain_update, bias_update, rms_ref = refs[3 * count + 1 :]
        base = 24
        moment = decay * gain_moment[...] + rights[0][base : base + 3, :] * (1.0 / replicas)
        new_gain[...] = moment
        gain_update[...] = -rates[4] * moment
        mean = owned_bias(here_ref, rights[0][base + 8 : base + 16, :], per) * (1.0 / replicas)
        moment = decay * bias_moment[...] + mean
        new_bias[...] = moment
        bias_update[...] = -rates[5] * moment
        totals = jnp.sum(rights[0][base + 16 : base + 24, :].T, axis=0, keepdims=True)
        rms_ref[...] = jnp.sqrt(totals[:, 0:4] / totals[:, 4:5])


def tail_final(replicas, listed, here, rights, lefts, merged, moments, extra=(), per=0):
    groups = tuple(sorted(set(item[3] for item in listed)))
    picked = [table[group] for table in (merged, moments) for group in groups]
    shapes = [shape_of(moments[group].shape, f32) for group in groups]
    inputs = [*rights, *lefts, *picked, *extra]
    small = [shape_of(value.shape, f32) for value in extra] * 2
    if per:
        small.append(shape_of((1, 4), f32))
    return pl.pallas_call(
        functools.partial(final_kernel, replicas, listed, groups, per),
        in_specs=[scalars()] + in_vmem(inputs),
        out_shape=shapes * 3 + [shape_of((len(listed), 8, SHARE), f32)] + small,
        name="tail_final",
    )(here, *inputs)


def swap(value, axis, bit):
    size = lax.axis_size(axis)
    return lax.ppermute(value, axis, [(at, at ^ bit) for at in range(size)])


def sum_over(value, axis, bit=1):
    while bit < lax.axis_size(axis):
        value = value + swap(value, axis, bit)
        bit *= 2
    return value


def sum_four(value, axis):
    return (value + swap(value, axis, 1)) + (swap(value, axis, 2) + swap(value, axis, 3))


def joined_half(kept, received):
    total = kept.astype(f32) + received[kept.shape[0] :].astype(f32)
    return total.astype(bf16)


def after(value, *others):
    return lax.optimization_barrier((value,) + others)[0]


def layer(
    block_input,
    cotangent,
    encoder_states,
    segment_ids,
    bucket_table,
    w_attn,
    w_attn_out,
    w_ff_in,
    w_ff_out,
    norm_gains,
    rel_bias,
    mom_attn,
    mom_attn_out,
    mom_ff_in,
    mom_ff_out,
    mom_gains,
    mom_bias,
    err_attn,
    err_attn_out,
    err_ff_in,
    err_ff_out,
    q_start,
):
    replicas = lax.axis_size("rep")
    owners = lax.axis_size("grp")
    buckets = rel_bias.shape[0] * owners
    group = lax.axis_index("grp")
    here = jnp.stack([group, lax.axis_index("rep") % 2]).astype(jnp.int32)
    stream = block_input[0]
    states = encoder_states[0]
    segment = segment_ids[0]

    one, one_half, small = pack(
        pack_first_kernel, here, [w_attn, w_attn_out, norm_gains, rel_bias], 8 * H * DK,
        [shape_of((16, SHARE), bf16)],
    )
    smalls = [small] + [swap(small, "grp", step) for step in range(1, owners)]
    one_half = after(one_half, *smalls[1:])
    one_mine = [swap(one_half, "grp", step) for step in range(1, owners)]
    two, two_half = pack(pack_second_kernel, here, [w_ff_in, w_ff_out], 3 * w_ff_out.shape[0], [])
    segment, one = lax.optimization_barrier((segment, one))
    bias, gains = bias_tiles(here, bucket_table, smalls, rel_bias.shape[0])
    one_hot = segment[:, None] == jnp.arange(PAIR)[None, :]
    kseg = one_hot.astype(bf16)
    known = jnp.arange(PAIR)[None, :] < 8
    qseg = jnp.where(known & ~one_hot, masked_score, 0.0).astype(bf16)
    kseg, qseg, bias, gains, *one_mine = lax.optimization_barrier(
        (kseg, qseg, bias, gains, *one_mine)
    )
    one_other = [swap(part, "rep", 1) for part in one_mine]
    two_half = after(two_half, *one_other)
    two_mine = [swap(two_half, "grp", step) for step in range(1, owners)]
    heads, normed0, qkv_full, cross_full, wo_full, co_full = qkv_forward(
        here, stream, gains, one, one_mine, one_other
    )
    attended, self_logs = self_forward(heads, bias, kseg, qseg)
    hidden1, normed1, cross_query, cross_pairs, sums1 = middle_forward(
        attended, stream, kseg, states, gains, wo_full, cross_full
    )
    cross_query, *two_mine = lax.optimization_barrier((cross_query, *two_mine))
    two_other = [swap(part, "rep", 1) for part in two_mine]
    cross_attended, cross_logs = cross_forward(cross_query, cross_pairs)
    (block_output, grad_h2, grad_cross_att, sums2, gain2, f_own, to_x, to_y, keep_y, keep_x) = outer_layer(
        here, cross_attended, hidden1, kseg, cotangent[0], gains, co_full, two, two_mine, two_other
    )
    from_x, from_y = swap(to_x, "grp", 1), swap(to_y, "grp", 2)
    grad_cross_query, grad_cross_pairs = cross_backward(
        cross_query, cross_pairs, grad_cross_att, cross_logs
    )
    (grad_h1, grad_attended, encoder_grad, gain1, c_own, *c_sends) = inner_backward(
        here, grad_cross_query, hidden1, normed1, attended, grad_h2, grad_cross_pairs, states, gains,
        wo_full, cross_full,
    )
    grad_attended, from_x, from_y = lax.optimization_barrier((grad_attended, from_x, from_y))
    next_y = swap(joined_half(keep_y, from_x), "grp", 2)
    next_x = swap(joined_half(keep_x, from_y), "grp", 1)
    c_parts = [swap(part, "grp", step) for step, part in zip(range(1, owners), c_sends)]
    head_grads, table_parts = self_backward(
        heads, grad_attended, self_logs, bias, kseg, qseg, bucket_table
    )
    (input_grad, q_own, *q_sends) = last_backward(
        here, head_grads, normed0, stream, grad_h1, gains, qkv_full, table_parts, gain1, gain2,
        sums1, sums2,
    )
    errors = (err_attn[0], err_attn_out[0], err_ff_in[0], err_ff_out[0])
    moments = (mom_attn, mom_attn_out, mom_ff_in, mom_ff_out)
    start = jnp.swapaxes(q_start, 1, 2)
    c_own, *q_sends = lax.optimization_barrier((c_own, *q_sends))
    q_parts = [swap(part, "grp", step) for step, part in zip(range(1, owners), q_sends)]
    *firsts, left_two = tail_first(
        [f_own, from_x, next_y, from_y, next_x], [c_own] + c_parts, errors, start
    )
    part, out_grad, ffin_grad, ffout_grad, part_sum, out_sum, ffin_sum, ffout_sum = firsts
    left_two = left_two + swap(left_two, "rep", 1)
    left_two = left_two + swap(left_two, "rep", 2)
    left_two = sum_over(left_two, "rep", 4)
    attn_grad, attn_sum, left_one = tail_qkv(
        [q_own] + q_parts, errors[0], start, part, part_sum
    )
    left_one = sum_four(left_one, "rep")
    listed = matrices(H * DK, w_ff_out.shape[0])
    base = 3 * H * DK
    per = buckets // owners
    late_list = [(group, at - 3 if group == 0 else at, lane, lanes)
                 for group, at, lane, lanes in listed[3:]]
    left_late, right_late = tail_right(
        replicas, late_list, here, left_two, (part_sum, out_sum, ffin_sum, ffout_sum)
    )
    left_one = left_one + swap(left_one, "rep", 4)
    left_one = sum_over(left_one, "rep", 8)
    sums = (attn_sum, out_sum, ffin_sum, ffout_sum)
    left_early, right, share_gains, share_bias = tail_right(
        replicas, listed[:3], here, left_one, sums, [q_own] + q_parts, per, [right_late]
    )
    right = sum_over(sum_four(right, "rep"), "rep", 4)
    finals = tail_final(
        replicas,
        [(0, place, item[2], item[0], item[1], item[3]) for place, item in enumerate(listed[:3])]
        + [(1, 6 + place, item[2] - base, item[0], item[1], item[3])
           for place, item in enumerate(listed[3:], 0)],
        here, [right], [left_early, left_late], sums, moments, (mom_gains, mom_bias), per,
    )
    gain_moment, bias_moment, gain_update, bias_update, branch_rms = finals[13:]
    branch_rms = branch_rms[0]
    factors = jnp.swapaxes(finals[12], 1, 2)
    return (
        block_output[None],
        input_grad[None],
        encoder_grad[None],
        branch_rms,
        attn_grad[None],
        out_grad[None],
        ffin_grad[None],
        ffout_grad[None],
        share_gains.transpose(1, 0, 2),
        share_bias.transpose(1, 2, 0),
        finals[0][None],
        finals[1][None],
        finals[2][None],
        finals[3][None],
        finals[4],
        finals[5],
        finals[6],
        finals[7],
        gain_moment,
        bias_moment,
        finals[8],
        finals[9],
        finals[10],
        finals[11],
        gain_update,
        bias_update,
        factors,
    )


def solution(mesh):
    in_specs = (
        P(("grp", "rep"), None, None),
        P(("grp", "rep"), None, None),
        P(("grp", "rep"), None, None),
        P(("grp", "rep"), None),
        P(),
        P(None, "grp", None),
        P(None, None, "grp"),
        P(None, "grp", None),
        P(None, "grp"),
        P(None, "grp"),
        P("grp", None),
        P(None, "grp", None),
        P(None, None, "grp"),
        P(None, "grp", None),
        P(None, "grp"),
        P(None, "grp"),
        P("grp", None),
        P("rep", None, "grp", None),
        P("rep", None, None, "grp"),
        P("rep", None, "grp", None),
        P("rep", None, "grp"),
        P(None, "grp", None),
    )
    out_specs = (
        P(("grp", "rep"), None, None),
        P(("grp", "rep"), None, None),
        P(("grp", "rep"), None, None),
        P(),
        P("rep", None, "grp", None),
        P("rep", None, None, "grp"),
        P("rep", None, "grp", None),
        P("rep", None, "grp"),
        P("rep", None, "grp"),
        P("rep", "grp", None),
        P("rep", None, "grp", None),
        P("rep", None, None, "grp"),
        P("rep", None, "grp", None),
        P("rep", None, "grp"),
        P(None, "grp", None),
        P(None, None, "grp"),
        P(None, "grp", None),
        P(None, "grp"),
        P(None, "grp"),
        P("grp", None),
        P(None, "grp", None),
        P(None, None, "grp"),
        P(None, "grp", None),
        P(None, "grp"),
        P(None, "grp"),
        P("grp", None),
        P(None, "grp", None),
    )
    return jax.shard_map(layer, mesh=mesh, in_specs=in_specs, out_specs=out_specs, check_vma=False)
```
